32 devices in a mesh: dp: 2 (over core), ctx: 4 (over z), fsdp: 4 (over y, x).
Axes of the slice: x: 2, y: 2, z: 4, core: 2. Of those that a mesh axis runs over, the one named last changes fastest.
Arguments:
- tokens: bfloat16 [8, 2, 1024, 2048], P(('dp', 'fsdp'), None, 'ctx'), may hold values from -6 to 6
- cotangent: bfloat16 [8, 2, 1024, 2048], P(('dp', 'fsdp'), None, 'ctx'), may hold values from -6 to 6
- lengths: int32 [8, 2], P(('dp', 'fsdp')), may hold values from 513 to 1024, as said below
- deal: int32 [8, 2, 8], P(('dp', 'fsdp')), may hold values from 0 to 7, each once within a row
- ln_gain: bfloat16 [2048], P('fsdp'), may hold values from 0.5 to 1.5
- ln_bias: bfloat16 [2048], P('fsdp'), may hold values from -1 to 1
- w_qkv: bfloat16 [2048, 6144], P('fsdp'), may hold values from -0.125 to 0.125
- b_qkv: bfloat16 [6144], P('fsdp'), may hold values from -1 to 1
- w_out: bfloat16 [2048, 2048], P('fsdp'), may hold values from -3 to 3
- b_out: bfloat16 [2048], P('fsdp'), may hold values from -2.5 to 2.5
- w_up: bfloat16 [2048, 8192], P('fsdp'), may hold values from -0.125 to 0.125
- b_up: bfloat16 [8192], P('fsdp'), may hold values from -1 to 1
- w_down: bfloat16 [8192, 2048], P('fsdp'), may hold values from -0.0625 to 0.0625
- b_down: bfloat16 [2048], P('fsdp'), may hold values from -2.5 to 2.5
Outputs:
- outputs: bfloat16 [8, 2, 1024, 2048], P(('dp', 'fsdp'), None, 'ctx')
- input_grad: bfloat16 [8, 2, 1024, 2048], P(('dp', 'fsdp'), None, 'ctx')
- grad_ln_gain: float32 [2048], P('fsdp')
- grad_ln_bias: float32 [2048], P('fsdp')
- grad_w_qkv: float32 [2048, 6144], P('fsdp')
- grad_b_qkv: float32 [6144], P('fsdp')
- grad_w_out: float32 [2048, 2048], P('fsdp')
- grad_b_out: float32 [2048], P('fsdp')
- grad_w_up: float32 [2048, 8192], P('fsdp')
- grad_b_up: float32 [8192], P('fsdp')
- grad_w_down: float32 [8192, 2048], P('fsdp')
- grad_b_down: float32 [2048], P('fsdp')
The draws below stay inside these ranges and needn't reach their ends.
Inputs may be any that keep to these rules, and one draw needn't show every extreme that they name: lengths[g, m] tokens fill the first positions of a sequence, the rest is padding; in every draw one sequence is exactly 1024 long and one exactly 513. Each row of deal is a permutation of the 8 blocks of a sequence.
All inputs are finite; a program needn't handle non-finite values.
Results may differ from the reference program's by a relative error of at most 0.02.
Values may be sent and summed in bfloat16 or wider, within the bound.
No kernel may reach another device: no remote copies, remote signals or barrier semaphores. Data moves between devices by JAX's collectives and lax.ppermute only.
A program may use at most 832 MiB of HBM per device.

```python
import jax
import jax.numpy as jnp
from jax import lax

D = 2048
HEADS = 32
HEAD_DIM = 64
ROT = 32
FF = 8192
MICRO = 2
BLK = 128
L = 1024
NBLK = 8
GROUPS = 8


def draw_lengths(key, part):
    count = GROUPS * MICRO
    drawn = jax.random.randint(key, (count,), L // 2 + 1, L + 1)
    order = jax.random.permutation(jax.random.fold_in(key, 11), count)
    drawn = jnp.where(order == 0, L, drawn)
    drawn = jnp.where(order == 1, L // 2 + 1, drawn)
    return drawn.reshape(GROUPS, MICRO).astype(jnp.int32)


def shard_levels(own_key, extent, cuts, least, top_value):
    level = 1.0
    for dim, shards_of in cuts:
        steps = jax.random.uniform(jax.random.fold_in(jax.random.fold_in(own_key, 6), dim), (shards_of,), jnp.float32, least / len(cuts), top_value / len(cuts))
        level = level * jnp.repeat(jnp.exp(steps), extent[dim] // shards_of).reshape((-1,) + (1,) * (len(extent) - 1 - dim))
    return level


def normal_values(stream_key, extent, deviation, most, cuts=(), held_as=jnp.bfloat16):
    array = jax.random.normal(stream_key, extent, jnp.float32) * deviation
    if len(cuts) > 0:
        array = shard_levels(stream_key, extent, cuts, -0.22, 0.18) * array
    return jnp.clip(array, min=-most, max=most).astype(held_as)


def setup_inputs(seed: int = 0) -> dict:
    seeds = jax.random.split(jax.random.key(seed), 15)
    tokens = normal_values(seeds[0], (GROUPS, MICRO, L, D), 1.0, 6.0, ((0, 8), (2, 4)))
    cotangent = normal_values(seeds[1], (GROUPS, MICRO, L, D), 1.0, 6.0, ((0, 8), (2, 4)))
    lengths = draw_lengths(jax.random.fold_in(seeds[14], 71), 0)
    deal = jax.vmap(lambda own: jax.random.permutation(own, NBLK))(jax.random.split(seeds[3], GROUPS * MICRO)).reshape((GROUPS, MICRO, NBLK)).astype(jnp.int32)
    ln_gain = jnp.clip(1.0 + 0.1 * jax.random.normal(seeds[4], (D,), jnp.float32), 0.5, 1.5).astype(jnp.bfloat16)
    ln_bias = normal_values(seeds[5], (D,), 0.2, 1.0, ((0, 4),))
    w_qkv = normal_values(seeds[6], (D, 3 * D), D ** -0.5, 0.125, ((0, 4),))
    b_qkv = normal_values(seeds[7], (3 * D,), 0.2, 1.0, ((0, 4),))
    w_out = normal_values(seeds[8], (D, D), (max(1, D // 512)) ** -0.5, 3.0, ((0, 4),))
    b_out = normal_values(seeds[9], (D,), 0.5, 2.5, ((0, 4),))
    w_up = normal_values(seeds[10], (D, FF), D ** -0.5, 0.125, ((0, 4),))
    b_up = normal_values(seeds[11], (FF,), 0.2, 1.0, ((0, 4),))
    w_down = normal_values(seeds[12], (FF, D), FF ** -0.5, 0.0625, ((0, 4),))
    b_down = normal_values(seeds[13], (D,), 0.5, 2.5, ((0, 4),))
    return dict(tokens=tokens, cotangent=cotangent, lengths=lengths, deal=deal, ln_gain=ln_gain, ln_bias=ln_bias, w_qkv=w_qkv, b_qkv=b_qkv, w_out=w_out, b_out=b_out, w_up=w_up, b_up=b_up, w_down=w_down, b_down=b_down)


EPS = 1e-05
BASE = 10000.0

@jax.custom_vjp
def low(v):
    return lax.optimization_barrier(v.astype(jnp.bfloat16)).astype(jnp.float32)

@jax.custom_vjp
def low_back(v):
    return v

def low_keep(v):
    return (low(v), None)

def low_pass(kept, grad):
    return (grad,)

def back_keep(v):
    return (v, None)

def back_low(kept, grad):
    return (low(grad),)
low.defvjp(low_keep, low_pass)
low_back.defvjp(back_keep, back_low)

def matmul(left, right):
    return jnp.dot(left, right, precision=lax.Precision.HIGHEST)

def rotate(values, positions):
    half = ROT // 2
    freqs = BASE ** (-(jnp.arange(half, dtype=jnp.float32) * 2.0) / ROT)
    angles = positions.astype(jnp.float32)[:, None] * freqs[None, :]
    cosine = jnp.cos(angles)[:, None, :]
    sine = jnp.sin(angles)[:, None, :]
    first = values[..., :half]
    second = values[..., half:ROT]
    return jnp.concatenate([first * cosine - second * sine, second * cosine + first * sine, values[..., ROT:]], axis=-1)

def layer(params, inputs, positions, length):
    gain, shift, w_qkv, b_qkv, w_out, b_out, w_up, b_up, w_down, b_down = params
    seq_len = inputs.shape[0]
    centered = inputs - lax.optimization_barrier(jnp.mean(inputs, axis=-1, keepdims=True))
    variance = lax.optimization_barrier(jnp.mean(centered * centered, axis=-1, keepdims=True))
    normed = centered * lax.rsqrt(variance + EPS)
    hidden = low(normed * gain + shift)
    joined = low_back(matmul(hidden, w_qkv) + b_qkv)
    query = low(rotate(joined[:, :D].reshape(seq_len, HEADS, HEAD_DIM), positions))
    keyed = low(rotate(joined[:, D:2 * D].reshape(seq_len, HEADS, HEAD_DIM), positions))
    valued = low(joined[:, 2 * D:].reshape(seq_len, HEADS, HEAD_DIM))
    scores = low_back(jnp.einsum('qhd,khd->hqk', query, keyed, precision=lax.Precision.HIGHEST) * HEAD_DIM ** (-0.5))
    allowed = (positions[None, :] <= positions[:, None]) & (positions[None, :] < length)
    probs = low(jax.nn.softmax(jnp.where(allowed[None], scores, -1e+30), axis=-1))
    mixed = jnp.einsum('hqk,khd->qhd', probs, valued, precision=lax.Precision.HIGHEST).reshape(seq_len, D)
    attended = low(low_back(mixed))
    branch = matmul(attended, w_out) + b_out
    upward = low_back(matmul(hidden, w_up) + b_up)
    activated = low(jax.nn.gelu(upward, approximate=True))
    feed = matmul(activated, w_down) + b_down
    valid = (positions < length).astype(jnp.float32)[:, None]
    return valid * (inputs + branch + feed)

def reference(tokens, cotangent, lengths, deal, ln_gain, ln_bias, w_qkv, b_qkv, w_out, b_out, w_up, b_up, w_down, b_down):
    params = tuple((piece.astype(jnp.float32) for piece in (ln_gain, ln_bias, w_qkv, b_qkv, w_out, b_out, w_up, b_up, w_down, b_down)))
    offsets = jnp.arange(BLK, dtype=jnp.int32)
    positions = (deal.astype(jnp.int32)[..., None] * BLK + offsets).reshape(GROUPS * MICRO, L).astype(jnp.int32)
    flat_lengths = lengths.astype(jnp.int32).reshape(GROUPS * MICRO)

    def forward(weights, inputs):

        def one_seq(carry, item):
            return (carry, jax.checkpoint(layer)(weights, item[0], item[1], item[2]))
        _, results = lax.scan(one_seq, jnp.zeros((), jnp.float32), (inputs.reshape(GROUPS * MICRO, L, D), positions, flat_lengths))
        return results.reshape(GROUPS, MICRO, L, D)
    results, pull = jax.vjp(forward, params, tokens.astype(jnp.float32))
    weight_grads, token_grads = pull(cotangent.astype(jnp.float32))
    return (results.astype(jnp.bfloat16), token_grads.astype(jnp.bfloat16), weight_grads[0], weight_grads[1], weight_grads[2], weight_grads[3], weight_grads[4], weight_grads[5], weight_grads[6], weight_grads[7], weight_grads[8], weight_grads[9])
```

```python
import jax
import jax.numpy as jnp
from jax import lax
from jax.experimental import pallas as pl
from jax.experimental.pallas import tpu as pltpu
from jax.sharding import PartitionSpec as P

HEAD_DIM = 64
ROT = 32


EPS = 1e-05
BASE = 10000.0


def contract_rows(left, right):
    return lax.dot_general(
        left, right, (((0,), (0,)), ((), ())), preferred_element_type=jnp.float32
    )


def contract_cols(left, right):
    return lax.dot_general(
        left, right, (((1,), (1,)), ((), ())), preferred_element_type=jnp.float32
    )


def angles_of(positions):
    half = ROT // 2
    freqs = BASE ** (-(jnp.arange(half, dtype=jnp.float32) * 2.0) / ROT)
    angles = positions.astype(jnp.float32)[:, None] * freqs[None, :]
    return (jnp.cos(angles)[:, None, :], jnp.sin(angles)[:, None, :])


def rotate(values, cosine, sine):
    half = ROT // 2
    first = values[..., :half]
    second = values[..., half:ROT]
    return jnp.concatenate(
        [first * cosine - second * sine, second * cosine + first * sine, values[..., ROT:]], axis=-1
    )


def rotate_back(values, cosine, sine):
    half = ROT // 2
    first = values[..., :half]
    second = values[..., half:ROT]
    return jnp.concatenate(
        [first * cosine + second * sine, second * cosine - first * sine, values[..., ROT:]], axis=-1
    )


def layer_step(weights, inputs, upstream, length, deal_row):
    gain, shift, w_qkv, b_qkv, w_out, b_out, w_up, b_up, w_down, b_down = weights
    row_count, width = inputs.shape
    block_rows = row_count // 2
    head_count = width // HEAD_DIM
    scale = HEAD_DIM ** (-0.5)
    place = lax.axis_index("ctx")
    offsets = jnp.arange(block_rows, dtype=jnp.int32)
    own_blocks = lax.dynamic_slice_in_dim(deal_row, 2 * place, 2)
    local_pos = (own_blocks[:, None] * block_rows + offsets[None, :]).reshape(row_count)
    every_pos = (deal_row[:, None] * block_rows + offsets[None, :]).reshape(-1)
    valid = (local_pos < length).astype(jnp.float32)[:, None]
    allowed = (every_pos[None, :] <= local_pos[:, None]) & (every_pos[None, :] < length)
    cosine, sine = angles_of(local_pos)
    inputs_f = inputs.astype(jnp.float32)
    gain_f = gain.astype(jnp.float32)
    centered = inputs_f - jnp.mean(inputs_f, axis=-1, keepdims=True)
    variance = jnp.mean(centered * centered, axis=-1, keepdims=True)
    inv_std = lax.rsqrt(variance + EPS)
    normed = centered * inv_std
    hidden = (normed * gain_f + shift.astype(jnp.float32)).astype(jnp.bfloat16)
    joined = jnp.dot(hidden, w_qkv, preferred_element_type=jnp.float32) + b_qkv.astype(jnp.float32)
    query = (
        rotate(joined[:, :width].reshape(row_count, head_count, HEAD_DIM), cosine, sine)
        .reshape(row_count, width)
        .astype(jnp.bfloat16)
    )
    keyed = (
        rotate(joined[:, width : 2 * width].reshape(row_count, head_count, HEAD_DIM), cosine, sine)
        .reshape(row_count, width)
        .astype(jnp.bfloat16)
    )
    valued = joined[:, 2 * width :].astype(jnp.bfloat16)
    keys_all, values_all = (
        lax.all_gather(keyed, "ctx", axis=0, tiled=True),
        lax.all_gather(valued, "ctx", axis=0, tiled=True),
    )
    total_keys = keys_all.shape[0]
    group = min(8, head_count)
    span = group * HEAD_DIM

    def heads_of(array, start, count):
        return array[:, start : start + span].reshape(count, group, HEAD_DIM)

    def block_scores(start):
        raw = (
            jnp.einsum(
                "qhd,khd->hqk",
                heads_of(query, start, row_count),
                heads_of(keys_all, start, total_keys),
                preferred_element_type=jnp.float32,
            )
            * scale
        )
        return jnp.where(allowed[None], raw, -1e30)

    attended_parts = []
    lse_parts = []
    for start in range(0, width, span):
        masked = block_scores(start)
        highest = jnp.max(masked, axis=-1, keepdims=True)
        expo = jnp.exp(masked - highest)
        total = jnp.sum(expo, axis=-1, keepdims=True)
        weights_low = (expo / total).astype(jnp.bfloat16)
        mixed = jnp.einsum(
            "hqk,khd->qhd",
            weights_low,
            heads_of(values_all, start, total_keys),
            preferred_element_type=jnp.float32,
        )
        attended_parts.append(mixed.reshape(row_count, span))
        lse_parts.append(highest + jnp.log(total))
    attended = jnp.concatenate(attended_parts, axis=1).astype(jnp.bfloat16)
    branch = jnp.dot(attended, w_out, preferred_element_type=jnp.float32) + b_out.astype(
        jnp.float32
    )
    upward = jnp.dot(hidden, w_up, preferred_element_type=jnp.float32) + b_up.astype(jnp.float32)
    activated = jax.nn.gelu(upward, approximate=True).astype(jnp.bfloat16)
    feed = jnp.dot(activated, w_down, preferred_element_type=jnp.float32) + b_down.astype(
        jnp.float32
    )
    result = (valid * (inputs_f + branch + feed)).astype(jnp.bfloat16)
    grad_out = upstream.astype(jnp.float32) * valid
    grad_low = grad_out.astype(jnp.bfloat16)
    row_total = jnp.sum(grad_out, axis=0)
    d_down = contract_rows(activated, grad_low)
    d_wout = contract_rows(attended, grad_low)
    d_act = contract_cols(grad_low, w_down)
    _, gelu_pull = jax.vjp(lambda value: jax.nn.gelu(value, approximate=True), upward)
    d_upward = gelu_pull(d_act)[0].astype(jnp.bfloat16)
    d_wup = contract_rows(hidden, d_upward)
    d_bup = jnp.sum(d_upward.astype(jnp.float32), axis=0)
    d_attended = contract_cols(grad_low, w_out).astype(jnp.bfloat16)
    dq_parts = []
    dk_parts = []
    dv_parts = []
    delta_parts = []
    for index, start in enumerate(range(0, width, span)):
        masked = block_scores(start)
        probs = jnp.where(allowed[None], jnp.exp(masked - lse_parts[index]), 0.0)
        d_heads = heads_of(d_attended, start, row_count)
        d_probs = jnp.einsum(
            "qhd,khd->hqk",
            d_heads,
            heads_of(values_all, start, total_keys),
            preferred_element_type=jnp.float32,
        )
        delta = jnp.sum(probs * d_probs, axis=-1, keepdims=True)
        d_scores = (probs * (d_probs - delta)).astype(jnp.bfloat16)
        d_query = (
            jnp.einsum(
                "hqk,khd->qhd",
                d_scores,
                heads_of(keys_all, start, total_keys),
                preferred_element_type=jnp.float32,
            )
            * scale
        )
        dq_parts.append(d_query.reshape(row_count, span))
        delta_parts.append(delta[:, :, 0].T)
        d_keyed = (
            jnp.einsum(
                "hqk,qhd->khd",
                d_scores,
                heads_of(query, start, row_count),
                preferred_element_type=jnp.float32,
            )
            * scale
        )
        d_valued = jnp.einsum(
            "hqk,qhd->khd", probs.astype(jnp.bfloat16), d_heads, preferred_element_type=jnp.float32
        )
        dk_parts.append(d_keyed.reshape(total_keys, span))
        dv_parts.append(d_valued.reshape(total_keys, span))
    keys_grad_all = jnp.concatenate(dk_parts, axis=1)
    values_grad_all = jnp.concatenate(dv_parts, axis=1)
    keys_grad, values_grad = (
        lax.psum_scatter(
            keys_grad_all.astype(jnp.bfloat16), "ctx", scatter_dimension=0, tiled=True
        ).astype(jnp.float32),
        lax.psum_scatter(
            values_grad_all.astype(jnp.bfloat16), "ctx", scatter_dimension=0, tiled=True
        ).astype(jnp.float32),
    )
    query_grad = rotate_back(
        jnp.concatenate(dq_parts, axis=1).reshape(row_count, head_count, HEAD_DIM), cosine, sine
    ).reshape(row_count, width)
    keyed_grad = rotate_back(
        keys_grad.reshape(row_count, head_count, HEAD_DIM), cosine, sine
    ).reshape(row_count, width)
    d_joined = jnp.concatenate([query_grad, keyed_grad, values_grad], axis=1).astype(jnp.bfloat16)
    d_wqkv = contract_rows(hidden, d_joined)
    d_bqkv = jnp.sum(d_joined.astype(jnp.float32), axis=0)
    d_hidden = contract_cols(d_joined, w_qkv) + contract_cols(d_upward, w_up)
    d_gain = jnp.sum(d_hidden * normed, axis=0)
    d_shift = jnp.sum(d_hidden, axis=0)
    d_norm = d_hidden * gain_f
    d_inputs = inv_std * (
        d_norm
        - jnp.mean(d_norm, axis=-1, keepdims=True)
        - normed * jnp.mean(d_norm * normed, axis=-1, keepdims=True)
    )
    back = (grad_out + d_inputs).astype(jnp.bfloat16)
    return (
        result,
        back,
        (d_gain, d_shift, d_wqkv, d_bqkv, d_wout, row_total, d_wup, d_bup, d_down, row_total),
    )


def gathered_body(
    tokens,
    cotangent,
    lengths,
    deal,
    ln_gain,
    ln_bias,
    w_qkv,
    b_qkv,
    w_out,
    b_out,
    w_up,
    b_up,
    w_down,
    b_down,
):
    shards = (ln_gain, ln_bias, w_qkv, b_qkv, w_out, b_out, w_up, b_up, w_down, b_down)
    shard_count = lax.axis_size("fsdp")
    summed = tuple(
        (
            jnp.zeros((piece.shape[0] * shard_count,) + piece.shape[1:], jnp.float32)
            for piece in shards
        )
    )
    results = []
    backs = []
    for micro_index in range(tokens.shape[1]):
        gathered = (
            lax.all_gather(ln_gain, "fsdp", axis=0, tiled=True),
            lax.all_gather(ln_bias, "fsdp", axis=0, tiled=True),
            lax.all_gather(w_qkv, "fsdp", axis=0, tiled=True),
            lax.all_gather(b_qkv, "fsdp", axis=0, tiled=True),
            lax.all_gather(w_out, "fsdp", axis=0, tiled=True),
            lax.all_gather(b_out, "fsdp", axis=0, tiled=True),
            lax.all_gather(w_up, "fsdp", axis=0, tiled=True),
            lax.all_gather(b_up, "fsdp", axis=0, tiled=True),
            lax.all_gather(w_down, "fsdp", axis=0, tiled=True),
            lax.all_gather(b_down, "fsdp", axis=0, tiled=True),
        )
        result, back, local = layer_step(
            gathered,
            tokens[0, micro_index],
            cotangent[0, micro_index],
            lengths[0, micro_index],
            deal[0, micro_index],
        )
        results.append(result)
        backs.append(back)
        summed = tuple((older + newer for older, newer in zip(summed, local)))
    summed = (
        lax.psum_scatter(
            summed[0].astype(jnp.bfloat16), "fsdp", scatter_dimension=0, tiled=True
        ).astype(jnp.float32),
        lax.psum_scatter(
            summed[1].astype(jnp.bfloat16), "fsdp", scatter_dimension=0, tiled=True
        ).astype(jnp.float32),
        lax.psum_scatter(
            summed[2].astype(jnp.bfloat16), "fsdp", scatter_dimension=0, tiled=True
        ).astype(jnp.float32),
        lax.psum_scatter(
            summed[3].astype(jnp.bfloat16), "fsdp", scatter_dimension=0, tiled=True
        ).astype(jnp.float32),
        lax.psum_scatter(
            summed[4].astype(jnp.bfloat16), "fsdp", scatter_dimension=0, tiled=True
        ).astype(jnp.float32),
        lax.psum_scatter(
            summed[5].astype(jnp.bfloat16), "fsdp", scatter_dimension=0, tiled=True
        ).astype(jnp.float32),
        lax.psum_scatter(
            summed[6].astype(jnp.bfloat16), "fsdp", scatter_dimension=0, tiled=True
        ).astype(jnp.float32),
        lax.psum_scatter(
            summed[7].astype(jnp.bfloat16), "fsdp", scatter_dimension=0, tiled=True
        ).astype(jnp.float32),
        lax.psum_scatter(
            summed[8].astype(jnp.bfloat16), "fsdp", scatter_dimension=0, tiled=True
        ).astype(jnp.float32),
        lax.psum_scatter(
            summed[9].astype(jnp.bfloat16), "fsdp", scatter_dimension=0, tiled=True
        ).astype(jnp.float32),
    )
    totals = (
        lax.psum(summed[0].astype(jnp.bfloat16), ("dp", "ctx")).astype(jnp.float32),
        lax.psum(summed[1].astype(jnp.bfloat16), ("dp", "ctx")).astype(jnp.float32),
        lax.psum(summed[2].astype(jnp.bfloat16), ("dp", "ctx")).astype(jnp.float32),
        lax.psum(summed[3].astype(jnp.bfloat16), ("dp", "ctx")).astype(jnp.float32),
        lax.psum(summed[4].astype(jnp.bfloat16), ("dp", "ctx")).astype(jnp.float32),
        lax.psum(summed[5].astype(jnp.bfloat16), ("dp", "ctx")).astype(jnp.float32),
        lax.psum(summed[6].astype(jnp.bfloat16), ("dp", "ctx")).astype(jnp.float32),
        lax.psum(summed[7].astype(jnp.bfloat16), ("dp", "ctx")).astype(jnp.float32),
        lax.psum(summed[8].astype(jnp.bfloat16), ("dp", "ctx")).astype(jnp.float32),
        lax.psum(summed[9].astype(jnp.bfloat16), ("dp", "ctx")).astype(jnp.float32),
    )
    stacked_out = jnp.stack(results)[None]
    stacked_back = jnp.stack(backs)[None]
    return (
        stacked_out,
        stacked_back,
        totals[0],
        totals[1],
        totals[2],
        totals[3],
        totals[4],
        totals[5],
        totals[6],
        totals[7],
        totals[8],
        totals[9],
    )


SWAP = [(0, 1), (1, 0)]


def swap_dp(value):
    return lax.ppermute(value, "dp", SWAP)


def by_core(core, mine, other, axis):
    first = jnp.where(core == 0, mine, other)
    second = jnp.where(core == 0, other, mine)
    return jnp.stack([first, second], axis=axis)


def pick(array, index, axis):
    return lax.dynamic_index_in_dim(array, index, axis, keepdims=False)


def to_plane(rows, core, blk):
    micro, count, width = rows.shape
    split = rows.reshape(micro, 2, blk, width)
    received = swap_dp(pick(split, 1 - core, 1))
    lined = by_core(core, pick(split, core, 1), received, 0).reshape(2 * micro, blk, width)
    dealt = lax.all_to_all(lined, "ctx", 0, 0, tiled=True)
    own = lax.all_gather(dealt.reshape(-1, width), "fsdp", axis=0, tiled=True)
    return own, swap_dp(own)


def to_home(part_own, part_oth, core, micro, blk):
    width = part_own.shape[1]
    total = (part_own + swap_dp(part_oth).astype(jnp.float32)).astype(jnp.bfloat16)
    mine = lax.psum_scatter(total, "fsdp", scatter_dimension=0, tiled=True)
    lined = lax.all_to_all(mine.reshape(-1, blk, width), "ctx", 0, 0, tiled=True)
    lined = lined.reshape(2, micro, blk, width)
    kept = pick(lined, core, 0)
    received = swap_dp(pick(lined, 1 - core, 0))
    return by_core(core, kept, received, 1).reshape(micro, 2 * blk, width)


def columns_of(weight, parts, core, shards):
    rows, total = weight.shape
    width = total // (parts * shards * 2)
    mine = pick(weight.reshape(rows, parts, shards, 2, width), core, 3)
    sent = mine.transpose(2, 0, 1, 3).reshape(shards * rows, parts * width)
    return lax.all_to_all(sent, "fsdp", 0, 0, tiled=True)


def line_sum(value, place):
    inward = lax.ppermute(value, "ctx", [(0, 1), (3, 2)])
    half = value + inward
    across = lax.ppermute(half, "ctx", [(1, 2), (2, 1)])
    whole = half + across
    outward = lax.ppermute(whole, "ctx", [(1, 0), (2, 3)])
    inner = (place == 1) | (place == 2)
    return jnp.where(inner, whole, outward)


def sum_ctx(value, place):
    if lax.axis_size("ctx") == 4:
        return line_sum(value, place)
    return lax.psum(value, "ctx")


GELU_C = 0.7978845608028654
GELU_A = 0.044715


def gelu_pair(value):
    square = value * value
    tanh = jnp.tanh(GELU_C * value * (1.0 + GELU_A * square))
    half = 0.5 * (1.0 + tanh)
    slope = half + 0.5 * value * (1.0 - tanh * tanh) * (GELU_C * (1.0 + 3.0 * GELU_A * square))
    return value * half, slope


def rope_tables(seq_len):
    lane = jnp.arange(2 * HEAD_DIM, dtype=jnp.int32) % HEAD_DIM
    half = ROT // 2
    turned = lane < ROT
    index = jnp.where(turned, lane % half, 0).astype(jnp.float32)
    freqs = BASE ** (-(index * 2.0) / ROT)
    angles = jnp.arange(seq_len, dtype=jnp.float32)[:, None] * freqs[None, :]
    sine = jnp.sin(angles)
    cosine = jnp.where(turned[None], jnp.cos(angles), 1.0)
    up = jnp.where((lane < half)[None], -sine, 0.0)
    down = jnp.where(((lane >= half) & turned)[None], sine, 0.0)
    return cosine, up, down


def attention_call(deal_own, deal_oth, lengths, joined_own, joined_oth, datt_own, datt_oth, blk):
    seqs, half_rows, wide = joined_own.shape
    heads_wide = wide // 3
    pairs = heads_wide // 128
    seq_len = 2 * half_rows
    per_side = half_rows // blk
    step = 256
    tables = rope_tables(seq_len)
    scale = HEAD_DIM ** (-0.5)
    half = ROT // 2
    contract_last = (((1,), (1,)), ((), ()))
    contract_first = (((0,), (0,)), ((), ()))

    def kernel(own_at, oth_at, len_at, cos_ref, up_ref, down_ref, q0, k0, v0, d0, q1, k1, v1, d1,
               att0, dq0, dk0, dv0, att1, dq1, dk1, dv1,
               qs, ks, vs, ds, att_s, dq_s, dk_s, dv_s):
        seq = pl.program_id(0)
        length = len_at[seq]

        def turn(x, at):
            return (x * cos_ref[at, :] + pltpu.roll(x, 128 - half, 1) * up_ref[at, :]
                    + pltpu.roll(x, half, 1) * down_ref[at, :])

        def unturn(x, at):
            return (x * cos_ref[at, :] - pltpu.roll(x, 128 - half, 1) * up_ref[at, :]
                    - pltpu.roll(x, half, 1) * down_ref[at, :])

        sides = ((own_at, q0, k0, v0, d0, att0, dq0, dk0, dv0), (oth_at, q1, k1, v1, d1, att1, dq1, dk1, dv1))
        for where_at, q_ref, k_ref, v_ref, d_ref, *_ in sides:
            for j in range(per_side):
                at = pl.ds(pl.multiple_of(where_at[seq, j] * blk, blk), blk)
                here = slice(j * blk, (j + 1) * blk)
                qs[at, :] = (turn(q_ref[0, here, :].astype(jnp.float32), at)).astype(jnp.bfloat16) * jnp.bfloat16(scale)
                ks[at, :] = turn(k_ref[0, here, :].astype(jnp.float32), at).astype(jnp.bfloat16)
                vs[at, :] = v_ref[0, here, :]
                ds[at, :] = d_ref[0, here, :]
        att_s[...] = jnp.zeros_like(att_s)
        dq_s[...] = jnp.zeros_like(dq_s)
        dk_s[...] = jnp.zeros_like(dk_s)
        dv_s[...] = jnp.zeros_like(dv_s)
        lane = lax.broadcasted_iota(jnp.int32, (1, 128), 1)

        def one_head(h, carry):
            chosen = (lane // HEAD_DIM) == h
            keep_f = jnp.where(chosen, 1.0, 0.0)
            keep = keep_f.astype(jnp.bfloat16)
            for i in range(seq_len // step):
                rows = slice(i * step, (i + 1) * step)
                n = (i + 1) * step
                q = qs[rows, :] * keep
                d = ds[rows, :] * keep
                k = ks[:n, :]
                v = vs[:n, :]
                s = lax.dot_general(q, k, contract_last, preferred_element_type=jnp.float32)
                q_pos = i * step + lax.broadcasted_iota(jnp.int32, (step, 1), 0)
                limit = jnp.minimum(q_pos, length - 1)
                k_pos = lax.broadcasted_iota(jnp.int32, (step, n), 1)
                s = jnp.where(k_pos <= limit, s, -1e30)
                e = jnp.exp(s - jnp.max(s, axis=-1, keepdims=True))
                p = e * (1.0 / jnp.sum(e, axis=-1, keepdims=True))
                p_low = p.astype(jnp.bfloat16)
                dp = lax.dot_general(d, v, contract_last, preferred_element_type=jnp.float32)
                delta = jnp.sum(p * dp, axis=-1, keepdims=True)
                dsc = (p * (dp - delta)).astype(jnp.bfloat16)
                att_s[rows, :] += keep_f * jnp.dot(p_low, v, preferred_element_type=jnp.float32)
                dq_s[rows, :] += keep_f * jnp.dot(dsc, k, preferred_element_type=jnp.float32)
                dk_s[:n, :] += lax.dot_general(dsc, q, contract_first, preferred_element_type=jnp.float32)
                dv_s[:n, :] += lax.dot_general(p_low, d, contract_first, preferred_element_type=jnp.float32)
            return carry

        lax.fori_loop(0, 128 // HEAD_DIM, one_head, 0)
        for where_at, _, _, _, _, att_ref, dq_ref, dk_ref, dv_ref in sides:
            for j in range(per_side):
                at = pl.ds(pl.multiple_of(where_at[seq, j] * blk, blk), blk)
                here = slice(j * blk, (j + 1) * blk)
                att_ref[0, here, :] = att_s[at, :].astype(jnp.bfloat16)
                dq_ref[0, here, :] = unturn(dq_s[at, :] * scale, at).astype(jnp.bfloat16)
                dk_ref[0, here, :] = unturn(dk_s[at, :], at).astype(jnp.bfloat16)
                dv_ref[0, here, :] = dv_s[at, :].astype(jnp.bfloat16)

    def lanes(offset):
        return pl.BlockSpec((1, half_rows, 128), lambda s, p, *_: (s, 0, offset + p))

    table = pl.BlockSpec((seq_len, 128), lambda s, p, *_: (0, 0))
    side_in = [lanes(0), lanes(pairs), lanes(2 * pairs), lanes(0)]
    side_out = [lanes(0)] * 4
    narrow = jax.ShapeDtypeStruct((seqs, half_rows, heads_wide), jnp.bfloat16)
    work = seqs * pairs * 2 * seq_len * seq_len * 64
    result = pl.pallas_call(
        kernel,
        grid_spec=pltpu.PrefetchScalarGridSpec(
            num_scalar_prefetch=3,
            grid=(seqs, pairs),
            in_specs=[table] * 3 + side_in + side_in,
            out_specs=side_out + side_out,
            scratch_shapes=[pltpu.VMEM((seq_len, 128), jnp.bfloat16)] * 4
            + [pltpu.VMEM((seq_len, 128), jnp.float32)] * 4,
        ),
        out_shape=[narrow] * 8,
        compiler_params=pltpu.CompilerParams(
            dimension_semantics=("arbitrary", "arbitrary"), vmem_limit_bytes=56 * 1024 * 1024
        ),
        cost_estimate=pl.CostEstimate(
            flops=12 * work, transcendentals=work // 64, bytes_accessed=2 * 8 * seqs * seq_len * heads_wide
        ),
    )(deal_own, deal_oth, lengths, *tables, joined_own, joined_own, joined_own, datt_own,
      joined_oth, joined_oth, joined_oth, datt_oth)
    return result[:4], result[4:]


def plane_body(
    tokens, cotangent, lengths, deal, ln_gain, ln_bias, w_qkv, b_qkv, w_out, b_out, w_up, b_up, w_down, b_down
):
    shards = lax.axis_size("fsdp")
    core = lax.axis_index("dp")
    place = lax.axis_index("ctx")
    shard = lax.axis_index("fsdp")
    _, micro, rows, width = tokens.shape
    blocks = deal.shape[2]
    lined = lax.axis_size("ctx")
    blk = rows * lined // blocks
    hidden_units = w_down.shape[0] // 2
    head_cols = w_out.shape[0] // 2
    low = jnp.bfloat16
    wide = jnp.float32

    small = jnp.concatenate([ln_gain, ln_bias, b_qkv, b_out, b_up, b_down])
    small = lax.all_gather(small, "fsdp", axis=0, tiled=False).astype(wide)
    bounds = [0]
    for piece in (ln_gain, ln_bias, b_qkv, b_out, b_up, b_down):
        bounds.append(bounds[-1] + piece.shape[0])
    gain, shift, bias_qkv, bias_out, bias_up, bias_down = (
        small[:, a:b].reshape(-1) for a, b in zip(bounds[:-1], bounds[1:])
    )
    meta = jnp.concatenate([deal[0].reshape(-1), lengths[0]])
    meta = lax.all_gather(meta, ("dp", "fsdp"), axis=0, tiled=False).reshape(2, shards, -1)
    meta = pick(meta, place // micro, 0)
    plane_deal = pick(meta[:, : micro * blocks].reshape(shards, micro, blocks), place % micro, 1)
    plane_len = pick(meta[:, micro * blocks :], place % micro, 1)
    plane_deal = plane_deal.reshape(shards, lined, 2)
    deal_own = pick(plane_deal, core, 2)
    deal_oth = pick(plane_deal, 1 - core, 2)

    own_blocks = lax.dynamic_slice_in_dim(deal[0], 2 * place, 2, axis=1)
    local_pos = (own_blocks[:, :, None] * blk + jnp.arange(blk, dtype=jnp.int32)).reshape(micro, rows)
    valid = (local_pos < lengths[0][:, None])[:, :, None]
    inputs = tokens[0].astype(wide)
    centered = inputs - jnp.mean(inputs, axis=-1, keepdims=True)
    inv_std = lax.rsqrt(jnp.mean(centered * centered, axis=-1, keepdims=True) + EPS)
    hidden_home = (centered * inv_std * gain + shift).astype(low)
    gout_home = jnp.where(valid, cotangent[0], jnp.zeros((), low))

    up_w = columns_of(w_up, 1, core, shards)
    hidden = to_plane(hidden_home, core, blk)
    qkv_w = columns_of(w_qkv, 3, core, shards)
    gout = to_plane(gout_home, core, blk)
    down_w = lax.dynamic_slice_in_dim(w_down, core * hidden_units, hidden_units, 0)
    out_w = lax.dynamic_slice_in_dim(w_out, core * head_cols, head_cols, 0)
    up_b = lax.dynamic_slice_in_dim(bias_up, (2 * shard + core) * hidden_units, hidden_units)
    qkv_b = pick(bias_qkv.reshape(3, 2 * shards, head_cols), 2 * shard + core, 1).reshape(-1)

    acts, dups, joins, datts = [], [], [], []
    for h, g in zip(hidden, gout):
        upward = jnp.dot(h, up_w, preferred_element_type=wide) + up_b
        act, slope = gelu_pair(upward)
        acts.append(act.astype(low))
        joins.append((jnp.dot(h, qkv_w, preferred_element_type=wide) + qkv_b).astype(low))
        dups.append((contract_cols(g, down_w) * slope.astype(low).astype(wide)).astype(low))
        datts.append(contract_cols(g, out_w).astype(low))

    def both(first, second):
        return (contract_rows(first[0], second[0]) + contract_rows(first[1], second[1])).astype(low)

    g_down = both(acts, gout)
    g_up = both(hidden, dups)
    g_up = lax.all_to_all(g_up, "fsdp", 0, 0, tiled=True)
    t_down = sum_ctx(g_down, place)
    t_up = sum_ctx(g_up, place)

    per_seq = (shards, lined * blk, -1)
    side_own, side_oth = attention_call(
        deal_own, deal_oth, plane_len,
        joins[0].reshape(per_seq), joins[1].reshape(per_seq),
        datts[0].reshape(per_seq), datts[1].reshape(per_seq), blk,
    )
    flat = lambda piece: piece.reshape(shards * lined * blk, -1)
    atts = [flat(side_own[0]), flat(side_oth[0])]
    dfused = [jnp.concatenate([flat(piece) for piece in side[1:]], axis=1) for side in (side_own, side_oth)]

    g_out = both(atts, gout)
    g_qkv = both(hidden, dfused)
    g_qkv = lax.all_to_all(g_qkv, "fsdp", 0, 0, tiled=True)
    t_out = sum_ctx(g_out, place)
    t_qkv = sum_ctx(g_qkv, place)

    def forward_part(side):
        return jnp.dot(acts[side], down_w, preferred_element_type=wide) + jnp.dot(
            atts[side], out_w, preferred_element_type=wide
        )

    def backward_part(side):
        return contract_cols(dups[side], up_w) + contract_cols(dfused[side], qkv_w)

    mixed = to_home(forward_part(0), forward_part(1).astype(low), core, micro, blk)
    d_hidden = to_home(backward_part(0), backward_part(1).astype(low), core, micro, blk).astype(wide)

    result = jnp.where(valid, inputs + mixed.astype(wide) + bias_out + bias_down, 0.0).astype(low)
    normed = centered * inv_std
    d_norm = d_hidden * gain
    d_inputs = inv_std * (
        d_norm
        - jnp.mean(d_norm, axis=-1, keepdims=True)
        - normed * jnp.mean(d_norm * normed, axis=-1, keepdims=True)
    )
    back = (gout_home.astype(wide) + d_inputs).astype(low)

    def column_sum(pair):
        return sum(jnp.sum(piece.astype(wide), axis=0) for piece in pair)

    spot = 2 * shard + core
    s_up = lax.dynamic_update_slice_in_dim(
        jnp.zeros((2 * shards * hidden_units,), wide), column_sum(dups), spot * hidden_units, 0
    )
    s_qkv = lax.dynamic_update_slice(
        jnp.zeros((3, 2 * shards, head_cols), wide),
        column_sum(dfused).reshape(3, 1, head_cols), (0, spot, 0),
    ).reshape(-1)
    s_gout = jnp.sum(gout_home.astype(wide), axis=(0, 1))
    s_gain = jnp.sum(d_hidden * normed, axis=(0, 1))
    s_shift = jnp.sum(d_hidden, axis=(0, 1))
    sums = lax.psum(jnp.concatenate([s_gain, s_shift, s_gout, s_up, s_qkv]), ("dp", "ctx", "fsdp"))
    at = 0
    pieces = []
    for size in (width, width, width, s_up.shape[0], s_qkv.shape[0]):
        part = sums[at : at + size]
        pieces.append(lax.dynamic_slice_in_dim(part, shard * (size // shards), size // shards))
        at += size
    d_gain, d_shift, d_row, d_bup, d_bqkv = pieces

    def rows_out(mine):
        pair = by_core(core, mine, swap_dp(mine), 0)
        return pair.reshape(-1, mine.shape[1]).astype(wide)

    def cols_out(mine, parts):
        local = mine.shape[0] // shards
        pair = by_core(core, mine, swap_dp(mine), 0)
        pair = pair.reshape(2, shards, local, parts, -1).transpose(2, 3, 1, 0, 4)
        return pair.reshape(local, -1).astype(wide)

    return (
        result[None], back[None], d_gain, d_shift, cols_out(t_qkv, 3), d_bqkv,
        rows_out(t_out), d_row, cols_out(t_up, 1), d_bup, rows_out(t_down), d_row,
    )


def plane_fits(mesh, shapes):
    tokens, _, _, deal = shapes[:4]
    sizes = dict(mesh.shape)
    dp, ctx, fsdp = sizes["dp"], sizes["ctx"], sizes["fsdp"]
    micro, seq_len, width = tokens.shape[1:]
    blocks = deal.shape[2]
    heads = width // HEAD_DIM
    return (
        dp == 2
        and dp * micro == ctx
        and tokens.shape[0] == dp * fsdp
        and blocks == dp * ctx
        and heads % (2 * dp * fsdp) == 0
        and seq_len % 256 == 0
        and (seq_len // blocks) % 128 == 0
    )


def solution(mesh):
    in_specs = (
        P(("dp", "fsdp"), None, "ctx", None),
        P(("dp", "fsdp"), None, "ctx", None),
        P(("dp", "fsdp"), None),
        P(("dp", "fsdp"), None, None),
        P("fsdp"),
        P("fsdp"),
        P("fsdp", None),
        P("fsdp"),
        P("fsdp", None),
        P("fsdp"),
        P("fsdp", None),
        P("fsdp"),
        P("fsdp", None),
        P("fsdp"),
    )
    out_specs = (
        P(("dp", "fsdp"), None, "ctx", None),
        P(("dp", "fsdp"), None, "ctx", None),
        P("fsdp"),
        P("fsdp"),
        P("fsdp", None),
        P("fsdp"),
        P("fsdp", None),
        P("fsdp"),
        P("fsdp", None),
        P("fsdp"),
        P("fsdp", None),
        P("fsdp"),
    )

    def program(*arrays):
        body = plane_body if plane_fits(mesh, arrays) else gathered_body
        return jax.shard_map(body, mesh=mesh, in_specs=in_specs, out_specs=out_specs, check_vma=False)(*arrays)

    return program
```

```python
import jax
import jax.numpy as jnp
from jax import lax
from jax.experimental import pallas as pl
from jax.experimental.pallas import tpu as pltpu
from jax.sharding import PartitionSpec as P

HEAD_DIM = 64
ROT = 32


EPS = 1e-05
BASE = 10000.0


def contract_rows(left, right):
    return lax.dot_general(
        left, right, (((0,), (0,)), ((), ())), preferred_element_type=jnp.float32
    )


def contract_cols(left, right):
    return lax.dot_general(
        left, right, (((1,), (1,)), ((), ())), preferred_element_type=jnp.float32
    )


def angles_of(positions):
    half = ROT // 2
    freqs = BASE ** (-(jnp.arange(half, dtype=jnp.float32) * 2.0) / ROT)
    angles = positions.astype(jnp.float32)[:, None] * freqs[None, :]
    return (jnp.cos(angles)[:, None, :], jnp.sin(angles)[:, None, :])


def rotate(values, cosine, sine):
    half = ROT // 2
    first = values[..., :half]
    second = values[..., half:ROT]
    return jnp.concatenate(
        [first * cosine - second * sine, second * cosine + first * sine, values[..., ROT:]], axis=-1
    )


def rotate_back(values, cosine, sine):
    half = ROT // 2
    first = values[..., :half]
    second = values[..., half:ROT]
    return jnp.concatenate(
        [first * cosine + second * sine, second * cosine - first * sine, values[..., ROT:]], axis=-1
    )


def layer_step(weights, inputs, upstream, length, deal_row):
    gain, shift, w_qkv, b_qkv, w_out, b_out, w_up, b_up, w_down, b_down = weights
    row_count, width = inputs.shape
    block_rows = row_count // 2
    head_count = width // HEAD_DIM
    scale = HEAD_DIM ** (-0.5)
    place = lax.axis_index("ctx")
    offsets = jnp.arange(block_rows, dtype=jnp.int32)
    own_blocks = lax.dynamic_slice_in_dim(deal_row, 2 * place, 2)
    local_pos = (own_blocks[:, None] * block_rows + offsets[None, :]).reshape(row_count)
    every_pos = (deal_row[:, None] * block_rows + offsets[None, :]).reshape(-1)
    valid = (local_pos < length).astype(jnp.float32)[:, None]
    allowed = (every_pos[None, :] <= local_pos[:, None]) & (every_pos[None, :] < length)
    cosine, sine = angles_of(local_pos)
    inputs_f = inputs.astype(jnp.float32)
    gain_f = gain.astype(jnp.float32)
    centered = inputs_f - jnp.mean(inputs_f, axis=-1, keepdims=True)
    variance = jnp.mean(centered * centered, axis=-1, keepdims=True)
    inv_std = lax.rsqrt(variance + EPS)
    normed = centered * inv_std
    hidden = (normed * gain_f + shift.astype(jnp.float32)).astype(jnp.bfloat16)
    joined = jnp.dot(hidden, w_qkv, preferred_element_type=jnp.float32) + b_qkv.astype(jnp.float32)
    query = (
        rotate(joined[:, :width].reshape(row_count, head_count, HEAD_DIM), cosine, sine)
        .reshape(row_count, width)
        .astype(jnp.bfloat16)
    )
    keyed = (
        rotate(joined[:, width : 2 * width].reshape(row_count, head_count, HEAD_DIM), cosine, sine)
        .reshape(row_count, width)
        .astype(jnp.bfloat16)
    )
    valued = joined[:, 2 * width :].astype(jnp.bfloat16)
    keys_all, values_all = (
        lax.all_gather(keyed, "ctx", axis=0, tiled=True),
        lax.all_gather(valued, "ctx", axis=0, tiled=True),
    )
    total_keys = keys_all.shape[0]
    group = min(8, head_count)
    span = group * HEAD_DIM

    def heads_of(array, start, count):
        return array[:, start : start + span].reshape(count, group, HEAD_DIM)

    def block_scores(start):
        raw = (
            jnp.einsum(
                "qhd,khd->hqk",
                heads_of(query, start, row_count),
                heads_of(keys_all, start, total_keys),
                preferred_element_type=jnp.float32,
            )
            * scale
        )
        return jnp.where(allowed[None], raw, -1e30)

    attended_parts = []
    lse_parts = []
    for start in range(0, width, span):
        masked = block_scores(start)
        highest = jnp.max(masked, axis=-1, keepdims=True)
        expo = jnp.exp(masked - highest)
        total = jnp.sum(expo, axis=-1, keepdims=True)
        weights_low = (expo / total).astype(jnp.bfloat16)
        mixed = jnp.einsum(
            "hqk,khd->qhd",
            weights_low,
            heads_of(values_all, start, total_keys),
            preferred_element_type=jnp.float32,
        )
        attended_parts.append(mixed.reshape(row_count, span))
        lse_parts.append(highest + jnp.log(total))
    attended = jnp.concatenate(attended_parts, axis=1).astype(jnp.bfloat16)
    branch = jnp.dot(attended, w_out, preferred_element_type=jnp.float32) + b_out.astype(
        jnp.float32
    )
    upward = jnp.dot(hidden, w_up, preferred_element_type=jnp.float32) + b_up.astype(jnp.float32)
    activated = jax.nn.gelu(upward, approximate=True).astype(jnp.bfloat16)
    feed = jnp.dot(activated, w_down, preferred_element_type=jnp.float32) + b_down.astype(
        jnp.float32
    )
    result = (valid * (inputs_f + branch + feed)).astype(jnp.bfloat16)
    grad_out = upstream.astype(jnp.float32) * valid
    grad_low = grad_out.astype(jnp.bfloat16)
    row_total = jnp.sum(grad_out, axis=0)
    d_down = contract_rows(activated, grad_low)
    d_wout = contract_rows(attended, grad_low)
    d_act = contract_cols(grad_low, w_down)
    _, gelu_pull = jax.vjp(lambda value: jax.nn.gelu(value, approximate=True), upward)
    d_upward = gelu_pull(d_act)[0].astype(jnp.bfloat16)
    d_wup = contract_rows(hidden, d_upward)
    d_bup = jnp.sum(d_upward.astype(jnp.float32), axis=0)
    d_attended = contract_cols(grad_low, w_out).astype(jnp.bfloat16)
    dq_parts = []
    dk_parts = []
    dv_parts = []
    delta_parts = []
    for index, start in enumerate(range(0, width, span)):
        masked = block_scores(start)
        probs = jnp.where(allowed[None], jnp.exp(masked - lse_parts[index]), 0.0)
        d_heads = heads_of(d_attended, start, row_count)
        d_probs = jnp.einsum(
            "qhd,khd->hqk",
            d_heads,
            heads_of(values_all, start, total_keys),
            preferred_element_type=jnp.float32,
        )
        delta = jnp.sum(probs * d_probs, axis=-1, keepdims=True)
        d_scores = (probs * (d_probs - delta)).astype(jnp.bfloat16)
        d_query = (
            jnp.einsum(
                "hqk,khd->qhd",
                d_scores,
                heads_of(keys_all, start, total_keys),
                preferred_element_type=jnp.float32,
            )
            * scale
        )
        dq_parts.append(d_query.reshape(row_count, span))
        delta_parts.append(delta[:, :, 0].T)
        d_keyed = (
            jnp.einsum(
                "hqk,qhd->khd",
                d_scores,
                heads_of(query, start, row_count),
                preferred_element_type=jnp.float32,
            )
            * scale
        )
        d_valued = jnp.einsum(
            "hqk,qhd->khd", probs.astype(jnp.bfloat16), d_heads, preferred_element_type=jnp.float32
        )
        dk_parts.append(d_keyed.reshape(total_keys, span))
        dv_parts.append(d_valued.reshape(total_keys, span))
    keys_grad_all = jnp.concatenate(dk_parts, axis=1)
    values_grad_all = jnp.concatenate(dv_parts, axis=1)
    keys_grad, values_grad = (
        lax.psum_scatter(
            keys_grad_all.astype(jnp.bfloat16), "ctx", scatter_dimension=0, tiled=True
        ).astype(jnp.float32),
        lax.psum_scatter(
            values_grad_all.astype(jnp.bfloat16), "ctx", scatter_dimension=0, tiled=True
        ).astype(jnp.float32),
    )
    query_grad = rotate_back(
        jnp.concatenate(dq_parts, axis=1).reshape(row_count, head_count, HEAD_DIM), cosine, sine
    ).reshape(row_count, width)
    keyed_grad = rotate_back(
        keys_grad.reshape(row_count, head_count, HEAD_DIM), cosine, sine
    ).reshape(row_count, width)
    d_joined = jnp.concatenate([query_grad, keyed_grad, values_grad], axis=1).astype(jnp.bfloat16)
    d_wqkv = contract_rows(hidden, d_joined)
    d_bqkv = jnp.sum(d_joined.astype(jnp.float32), axis=0)
    d_hidden = contract_cols(d_joined, w_qkv) + contract_cols(d_upward, w_up)
    d_gain = jnp.sum(d_hidden * normed, axis=0)
    d_shift = jnp.sum(d_hidden, axis=0)
    d_norm = d_hidden * gain_f
    d_inputs = inv_std * (
        d_norm
        - jnp.mean(d_norm, axis=-1, keepdims=True)
        - normed * jnp.mean(d_norm * normed, axis=-1, keepdims=True)
    )
    back = (grad_out + d_inputs).astype(jnp.bfloat16)
    return (
        result,
        back,
        (d_gain, d_shift, d_wqkv, d_bqkv, d_wout, row_total, d_wup, d_bup, d_down, row_total),
    )


def gathered_body(
    tokens,
    cotangent,
    lengths,
    deal,
    ln_gain,
    ln_bias,
    w_qkv,
    b_qkv,
    w_out,
    b_out,
    w_up,
    b_up,
    w_down,
    b_down,
):
    shards = (ln_gain, ln_bias, w_qkv, b_qkv, w_out, b_out, w_up, b_up, w_down, b_down)
    shard_count = lax.axis_size("fsdp")
    summed = tuple(
        (
            jnp.zeros((piece.shape[0] * shard_count,) + piece.shape[1:], jnp.float32)
            for piece in shards
        )
    )
    results = []
    backs = []
    for micro_index in range(tokens.shape[1]):
        gathered = (
            lax.all_gather(ln_gain, "fsdp", axis=0, tiled=True),
            lax.all_gather(ln_bias, "fsdp", axis=0, tiled=True),
            lax.all_gather(w_qkv, "fsdp", axis=0, tiled=True),
            lax.all_gather(b_qkv, "fsdp", axis=0, tiled=True),
            lax.all_gather(w_out, "fsdp", axis=0, tiled=True),
            lax.all_gather(b_out, "fsdp", axis=0, tiled=True),
            lax.all_gather(w_up, "fsdp", axis=0, tiled=True),
            lax.all_gather(b_up, "fsdp", axis=0, tiled=True),
            lax.all_gather(w_down, "fsdp", axis=0, tiled=True),
            lax.all_gather(b_down, "fsdp", axis=0, tiled=True),
        )
        result, back, local = layer_step(
            gathered,
            tokens[0, micro_index],
            cotangent[0, micro_index],
            lengths[0, micro_index],
            deal[0, micro_index],
        )
        results.append(result)
        backs.append(back)
        summed = tuple((older + newer for older, newer in zip(summed, local)))
    summed = (
        lax.psum_scatter(
            summed[0].astype(jnp.bfloat16), "fsdp", scatter_dimension=0, tiled=True
        ).astype(jnp.float32),
        lax.psum_scatter(
            summed[1].astype(jnp.bfloat16), "fsdp", scatter_dimension=0, tiled=True
        ).astype(jnp.float32),
        lax.psum_scatter(
            summed[2].astype(jnp.bfloat16), "fsdp", scatter_dimension=0, tiled=True
        ).astype(jnp.float32),
        lax.psum_scatter(
            summed[3].astype(jnp.bfloat16), "fsdp", scatter_dimension=0, tiled=True
        ).astype(jnp.float32),
        lax.psum_scatter(
            summed[4].astype(jnp.bfloat16), "fsdp", scatter_dimension=0, tiled=True
        ).astype(jnp.float32),
        lax.psum_scatter(
            summed[5].astype(jnp.bfloat16), "fsdp", scatter_dimension=0, tiled=True
        ).astype(jnp.float32),
        lax.psum_scatter(
            summed[6].astype(jnp.bfloat16), "fsdp", scatter_dimension=0, tiled=True
        ).astype(jnp.float32),
        lax.psum_scatter(
            summed[7].astype(jnp.bfloat16), "fsdp", scatter_dimension=0, tiled=True
        ).astype(jnp.float32),
        lax.psum_scatter(
            summed[8].astype(jnp.bfloat16), "fsdp", scatter_dimension=0, tiled=True
        ).astype(jnp.float32),
        lax.psum_scatter(
            summed[9].astype(jnp.bfloat16), "fsdp", scatter_dimension=0, tiled=True
        ).astype(jnp.float32),
    )
    totals = (
        lax.psum(summed[0].astype(jnp.bfloat16), ("dp", "ctx")).astype(jnp.float32),
        lax.psum(summed[1].astype(jnp.bfloat16), ("dp", "ctx")).astype(jnp.float32),
        lax.psum(summed[2].astype(jnp.bfloat16), ("dp", "ctx")).astype(jnp.float32),
        lax.psum(summed[3].astype(jnp.bfloat16), ("dp", "ctx")).astype(jnp.float32),
        lax.psum(summed[4].astype(jnp.bfloat16), ("dp", "ctx")).astype(jnp.float32),
        lax.psum(summed[5].astype(jnp.bfloat16), ("dp", "ctx")).astype(jnp.float32),
        lax.psum(summed[6].astype(jnp.bfloat16), ("dp", "ctx")).astype(jnp.float32),
        lax.psum(summed[7].astype(jnp.bfloat16), ("dp", "ctx")).astype(jnp.float32),
        lax.psum(summed[8].astype(jnp.bfloat16), ("dp", "ctx")).astype(jnp.float32),
        lax.psum(summed[9].astype(jnp.bfloat16), ("dp", "ctx")).astype(jnp.float32),
    )
    stacked_out = jnp.stack(results)[None]
    stacked_back = jnp.stack(backs)[None]
    return (
        stacked_out,
        stacked_back,
        totals[0],
        totals[1],
        totals[2],
        totals[3],
        totals[4],
        totals[5],
        totals[6],
        totals[7],
        totals[8],
        totals[9],
    )


SWAP = [(0, 1), (1, 0)]
LOW = jnp.bfloat16
SLOW = 1.8
WIDE = jnp.float32


def hint(flops, transcendentals, bytes_accessed):
    return pl.CostEstimate(
        flops=int(flops * SLOW), transcendentals=transcendentals, bytes_accessed=bytes_accessed
    )


def after(value, *others):
    return lax.optimization_barrier((value,) + others)[0]


def swap_dp(value):
    return lax.ppermute(value, "dp", SWAP)


def swap_shard(value, bits):
    return lax.ppermute(value, "fsdp", [(i, i ^ bits) for i in range(4)])


def shift_ctx(value, steps):
    return lax.ppermute(value, "ctx", [(i, (i + steps) % 4) for i in range(4)])


def pick(array, index, axis):
    return lax.dynamic_index_in_dim(array, index, axis, keepdims=False)


def by_core(core, mine, other, axis):
    first = jnp.where(core == 0, mine, other)
    second = jnp.where(core == 0, other, mine)
    return jnp.stack([first, second], axis=axis)


def for_other(rows, core, blk):
    micro, _, width = rows.shape
    return swap_dp(pick(rows.reshape(micro, 2, blk, width), 1 - core, 1))


def slots_of(rows, received, core, place, blk):
    micro, _, width = rows.shape
    split = rows.reshape(micro, 2, blk, width)
    lined = by_core(core, pick(split, core, 1), received, 0).reshape(4, blk, width)
    first = pick(lined, place, 0)
    rest = [shift_ctx(pick(lined, (place + steps) % 4, 0), steps) for steps in (1, 2, 3)]
    return first, rest


def spread_first(rows):
    return [(bits, 0, swap_shard(rows, bits)) for bits in (1, 2, 3)] + [(0, 0, rows)]


def spread_rest(rows, start):
    half = rows.shape[0] // 2
    top, end = rows[:half], rows[half:]
    x_top, y_end = swap_shard(top, 1), swap_shard(end, 2)
    x_end, y_top = swap_shard(end, 1), swap_shard(top, 2)
    d_top, d_end = swap_shard(x_top, 2), swap_shard(y_end, 1)
    pairs = ((0, top, end), (1, x_top, x_end), (2, y_top, y_end), (3, d_top, d_end))
    return [(bits, start, one) for bits, one, _ in pairs] + [(bits, start + half, two) for bits, _, two in pairs]


def placed(pieces, shard, size, *gates):
    whole = after(jnp.zeros((4 * size, pieces[0][2].shape[1]), LOW), *gates)
    for bits, start, piece in pieces:
        whole = lax.dynamic_update_slice(whole, piece, ((shard ^ bits) * size + start, 0))
    return whole


def plus(first, *others):
    total = first.astype(WIDE)
    for other in others:
        total = total + other.astype(WIDE)
    return total.astype(LOW)


def collect(total, shard):
    size = total.shape[0] // 4
    half = size // 2

    def part(bits, which):
        return lax.dynamic_slice_in_dim(total, (shard ^ bits) * size + which * half, half, 0)

    via_x, via_y = swap_shard(part(3, 0), 1), swap_shard(part(3, 1), 2)
    x_top, y_end = swap_shard(part(1, 0), 1), swap_shard(part(2, 1), 2)
    y_top = swap_shard(plus(part(2, 0), via_x), 2)
    x_end = swap_shard(plus(part(1, 1), via_y), 1)
    return jnp.concatenate([plus(part(0, 0), x_top, y_top), plus(part(0, 1), x_end, y_end)]), (via_x, via_y)


def to_home(mine, core, place, blk):
    width = mine.shape[1]
    lined = jnp.concatenate([lax.dynamic_slice_in_dim(mine, (place - j) % 4 * blk, blk, 0) for j in range(4)])
    lined = lax.all_to_all(lined.reshape(4, blk, width), "ctx", 0, 0, tiled=True).reshape(2, 2, blk, width)
    kept = pick(lined, core, 0)
    received = swap_dp(pick(lined, 1 - core, 0))
    return by_core(core, kept, received, 1).reshape(2, 2 * blk, width)


def columns_cut(weight, parts, core, shard):
    width = weight.shape[1] // (parts * 8)
    pieces = []
    for bits in range(4):
        spot = 2 * (shard ^ bits) + core
        pieces.append(jnp.concatenate(
            [lax.dynamic_slice_in_dim(weight, (t * 8 + spot) * width, width, 1) for t in range(parts)], axis=1
        ))
    return pieces


def columns_sent(pieces):
    return [(bits, 0, piece if bits == 0 else swap_shard(piece, bits)) for bits, piece in enumerate(pieces)]


def inward(value):
    return lax.ppermute(value, "ctx", [(0, 1), (3, 2)])


def across(value):
    return lax.ppermute(value, "ctx", [(1, 2), (2, 1)])


def outward(value):
    return lax.ppermute(value, "ctx", [(1, 0), (2, 3)])


def line_sum(value, place):
    half = value + inward(value)
    whole = half + across(half)
    return line_end(whole, outward(whole), place)


def line_end(whole, received, place):
    return jnp.where((place == 1) | (place == 2), whole, received)


def every_sum(value, place):
    value = value + swap_dp(value)
    value = value + swap_shard(value, 1)
    value = value + swap_shard(value, 2)
    return line_sum(value, place)


def lay_out(core, shard, own, oth, out_shape, grid, block, in_at, out_at):
    def kernel(where, own_ref, oth_ref, out_ref):
        side = pl.program_id(len(grid))

        @pl.when(side == 0)
        def _():
            out_ref[...] = own_ref[...].astype(WIDE)

        @pl.when(side == 1)
        def _():
            out_ref[...] = oth_ref[...].astype(WIDE)

    source = pl.BlockSpec(block, lambda *args: in_at(*args[: len(grid)]))
    target = pl.BlockSpec(block, lambda *args: out_at(*args[:-1], args[-1][0], args[-1][1]))
    count = out_shape[0] * out_shape[1]
    return pl.pallas_call(
        kernel,
        grid_spec=pltpu.PrefetchScalarGridSpec(
            num_scalar_prefetch=1, grid=grid + (2,), in_specs=[source, source], out_specs=target
        ),
        out_shape=jax.ShapeDtypeStruct(out_shape, WIDE),
        compiler_params=pltpu.CompilerParams(dimension_semantics=("arbitrary",) * (len(grid) + 1)),
        cost_estimate=hint(flops=0, transcendentals=0, bytes_accessed=6 * count),
    )(jnp.stack([core, shard]).astype(jnp.int32), own, oth)


def rows_out(core, shard, own, oth):
    rows, width = own.shape
    tile = min(256, rows)
    steps = rows // tile
    return lay_out(
        core, shard, own, oth, (2 * rows, width), (steps,), (tile, width),
        lambda i: (i, 0), lambda i, s, c, f: ((c ^ s) * steps + i, 0),
    )


def cols_out(core, shard, own, oth, parts):
    lines, columns, rows, width = own.shape
    width = width // parts

    def kernel(where, own_ref, oth_ref, out_ref):
        side = pl.program_id(2)

        @pl.when(side == 0)
        def _():
            out_ref[...] = own_ref[...].reshape(lines * rows, width).astype(WIDE)

        @pl.when(side == 1)
        def _():
            out_ref[...] = oth_ref[...].reshape(lines * rows, width).astype(WIDE)

    source = pl.BlockSpec((lines, 1, rows, width), lambda b, t, s, where: (0, b, 0, t))
    target = pl.BlockSpec((lines * rows, width), lambda b, t, s, where: (0, t * 8 + 2 * b + (where[0] ^ s)))
    return pl.pallas_call(
        kernel,
        grid_spec=pltpu.PrefetchScalarGridSpec(
            num_scalar_prefetch=1, grid=(columns, parts, 2), in_specs=[source, source], out_specs=target
        ),
        out_shape=jax.ShapeDtypeStruct((lines * rows, 2 * columns * parts * width), WIDE),
        compiler_params=pltpu.CompilerParams(dimension_semantics=("arbitrary",) * 3),
        cost_estimate=pl.CostEstimate(flops=0, transcendentals=0, bytes_accessed=12 * own.size),
    )(jnp.stack([core, shard]).astype(jnp.int32), own, oth)


GELU_C = 0.7978845608028654
GELU_A = 0.044715


def gelu_pair(value):
    square = value * value
    tanh = jnp.tanh(GELU_C * value * (1.0 + GELU_A * square))
    half = 0.5 * (1.0 + tanh)
    slope = half + 0.5 * value * (1.0 - tanh * tanh) * (GELU_C * (1.0 + 3.0 * GELU_A * square))
    return value * half, slope


ROWS_OF = (((0,), (0,)), ((), ()))
COLS_OF = (((1,), (1,)), ((), ()))
ROOM = 56 * 1024 * 1024


def row_call(body, tiled, whole, widths, flops, tile=512):
    count = tiled[0].shape[0]

    def rows_spec(width):
        return pl.BlockSpec((tile, width), lambda i: (i, 0))

    moved = sum(a.size * a.dtype.itemsize for a in (*tiled, *whole)) + 2 * count * sum(widths)
    return pl.pallas_call(
        body,
        grid=(count // tile,),
        in_specs=[rows_spec(a.shape[1]) for a in tiled]
        + [pl.BlockSpec(a.shape, lambda i: (0, 0), pipeline_mode=pl.Buffered(1)) for a in whole],
        out_specs=[rows_spec(width) for width in widths],
        out_shape=[jax.ShapeDtypeStruct((count, width), LOW) for width in widths],
        compiler_params=pltpu.CompilerParams(dimension_semantics=("arbitrary",), vmem_limit_bytes=ROOM),
        cost_estimate=hint(flops=flops, transcendentals=0, bytes_accessed=moved),
    )(*tiled, *whole)


def strips(width):
    step = min(256, width)
    return [slice(at, at + step) for at in range(0, width, step)]


def up_call(rows, weight, bias):
    def body(rows_ref, weight_ref, bias_ref, act_ref, slope_ref):
        for at in strips(weight.shape[1]):
            total = jnp.dot(rows_ref[...], weight_ref[:, at], preferred_element_type=WIDE) + bias_ref[:, at]
            act, slope = gelu_pair(total)
            act_ref[:, at] = act.astype(LOW)
            slope_ref[:, at] = slope.astype(LOW)

    width = weight.shape[1]
    return row_call(body, [rows], [weight, bias[None]], [width, width], 2 * rows.shape[0] * weight.size)


def join_call(rows, weight, bias):
    def body(rows_ref, weight_ref, bias_ref, out_ref):
        for at in strips(weight.shape[1]):
            total = jnp.dot(rows_ref[...], weight_ref[:, at], preferred_element_type=WIDE)
            out_ref[:, at] = (total + bias_ref[:, at]).astype(LOW)

    return row_call(body, [rows], [weight, bias[None]], [weight.shape[1]], 2 * rows.shape[0] * weight.size)[0]


def down_back_call(rows, slopes, down_w, out_w):
    def body(rows_ref, slope_ref, down_ref, out_w_ref, dup_ref, datt_ref):
        for at in strips(down_w.shape[0]):
            total = lax.dot_general(rows_ref[...], down_ref[at, :], COLS_OF, preferred_element_type=WIDE)
            dup_ref[:, at] = (total * slope_ref[:, at].astype(WIDE)).astype(LOW)
        total = lax.dot_general(rows_ref[...], out_w_ref[...], COLS_OF, preferred_element_type=WIDE)
        datt_ref[...] = total.astype(LOW)

    flops = 2 * rows.shape[0] * (down_w.size + out_w.size)
    return row_call(body, [rows, slopes], [down_w, out_w], [down_w.shape[0], out_w.shape[0]], flops)


def forward_call(act, att, down_w, out_w, added=None):
    def body(*refs):
        act_ref, att_ref = refs[:2]
        down_ref, out_w_ref, out_ref = refs[-3:]
        for at in strips(down_w.shape[1]):
            total = jnp.dot(act_ref[...], down_ref[:, at], preferred_element_type=WIDE)
            total = total + jnp.dot(att_ref[...], out_w_ref[:, at], preferred_element_type=WIDE)
            if added is not None:
                total = total + refs[2][:, at].astype(WIDE)
            out_ref[:, at] = total.astype(LOW)

    tiled = [act, att] + ([] if added is None else [added])
    flops = 2 * act.shape[0] * (down_w.size + out_w.size)
    return row_call(body, tiled, [down_w, out_w], [down_w.shape[1]], flops)[0]


def backward_call(dup, turned, up_w, qkv_w, added=None):
    wide = turned[0].shape[1]

    def body(*refs):
        dup_ref, turned_refs = refs[0], refs[1:4]
        up_ref, qkv_ref, out_ref = refs[-3:]
        for at in strips(up_w.shape[0]):
            total = lax.dot_general(dup_ref[...], up_ref[at, :], COLS_OF, preferred_element_type=WIDE)
            for i, ref in enumerate(turned_refs):
                part = qkv_ref[at, i * wide : (i + 1) * wide]
                total = total + lax.dot_general(ref[...], part, COLS_OF, preferred_element_type=WIDE)
            if added is not None:
                total = total + refs[4][:, at].astype(WIDE)
            out_ref[:, at] = total.astype(LOW)

    tiled = [dup, *turned] + ([] if added is None else [added])
    flops = 2 * dup.shape[0] * (up_w.size + qkv_w.size)
    return row_call(body, tiled, [up_w, qkv_w], [up_w.shape[0]], flops)[0]


def grad_call(left, rights, left_part=(0, 1), right_part=(0, 1), sums=False, dealt=False, tile=512):
    steps = left[0].shape[0] // tile
    left_cols = left[0].shape[1] // left_part[1]
    right_cols = [pair[0].shape[1] // right_part[1] for pair in rights]
    count = len(rights)
    piece = left_cols // 16
    made = 1 if dealt else count

    def body(*refs):
        ins, outs = refs[: 2 + 2 * count], refs[2 + 2 * count :]
        grads, totals, accs = outs[:made], outs[made : len(outs) - count], outs[len(outs) - count :]
        step = pl.program_id(0)

        @pl.when(step == 0)
        def _():
            for ref in (*accs, *totals):
                ref[...] = jnp.zeros_like(ref)

        def add(left_ref, right_refs):
            for i, ref in enumerate(right_refs):
                for at in strips(right_cols[i]):
                    accs[i][:, at] += lax.dot_general(
                        left_ref[...], ref[:, at], ROWS_OF, preferred_element_type=WIDE
                    )
                if sums:
                    totals[i][...] += jnp.sum(ref[...].astype(WIDE), axis=0, keepdims=True)

        @pl.when(step < steps)
        def _():
            add(ins[0], ins[2 : 2 + count])

        @pl.when(step >= steps)
        def _():
            add(ins[1], ins[2 + count :])

        @pl.when(step == 2 * steps - 1)
        def _():
            if not dealt:
                for grad, acc in zip(grads, accs):
                    grad[...] = acc[...].astype(LOW)
                return
            start = 0
            for acc, cols in zip(accs, right_cols):
                for column in range(4):
                    for line in range(4):
                        at = (4 * column + line) * piece
                        grads[0][line, column, :, start : start + cols] = acc[at : at + piece, :].astype(LOW)
                start += cols

    def side_spec(cols, part, side):
        def at(step):
            row = jnp.minimum(step, steps - 1) if side == 0 else jnp.maximum(step - steps, 0)
            return (row, part)

        return pl.BlockSpec((tile, cols), at)

    def fixed(shape):
        return pl.BlockSpec(shape, lambda step: (0,) * len(shape))

    specs = [side_spec(left_cols, left_part[0], side) for side in (0, 1)]
    specs += [side_spec(cols, right_part[0], side) for side in (0, 1) for cols in right_cols]
    shapes = [jax.ShapeDtypeStruct((left_cols, cols), LOW) for cols in right_cols]
    if dealt:
        shapes = [jax.ShapeDtypeStruct((4, 4, piece, sum(right_cols)), LOW)]
    if sums:
        shapes += [jax.ShapeDtypeStruct((1, cols), WIDE) for cols in right_cols]
    rows = 2 * left[0].shape[0]
    return pl.pallas_call(
        body,
        grid=(2 * steps,),
        in_specs=specs,
        out_specs=[fixed(shape.shape) for shape in shapes],
        out_shape=shapes,
        scratch_shapes=[pltpu.VMEM((left_cols, cols), WIDE) for cols in right_cols],
        compiler_params=pltpu.CompilerParams(dimension_semantics=("arbitrary",), vmem_limit_bytes=ROOM),
        cost_estimate=hint(
            flops=2 * rows * left_cols * sum(right_cols), transcendentals=0,
            bytes_accessed=2 * rows * (left_cols + sum(right_cols)),
        ),
    )(*left, *[pair[0] for pair in rights], *[pair[1] for pair in rights])


def rope_tables(seq_len):
    lane = jnp.arange(2 * HEAD_DIM, dtype=jnp.int32) % HEAD_DIM
    half = ROT // 2
    turned = lane < ROT
    index = jnp.where(turned, lane % half, 0).astype(jnp.float32)
    freqs = BASE ** (-(index * 2.0) / ROT)
    angles = jnp.arange(seq_len, dtype=jnp.float32)[:, None] * freqs[None, :]
    sine = jnp.sin(angles)
    cosine = jnp.where(turned[None], jnp.cos(angles), 1.0)
    up = jnp.where((lane < half)[None], -sine, 0.0)
    down = jnp.where(((lane >= half) & turned)[None], sine, 0.0)
    return cosine, up, down


def attention_call(deal_own, deal_oth, lengths, joined_own, joined_oth, datt_own, datt_oth, tables, blk, base, seqs, earlier=()):
    _, half_rows, wide = joined_own.shape
    heads_wide = wide // 3
    pairs = heads_wide // 128
    seq_len = 2 * half_rows
    per_side = half_rows // blk
    step = 256
    scale = HEAD_DIM ** (-0.5)
    half = ROT // 2
    contract_last = (((1,), (1,)), ((), ()))
    contract_first = (((0,), (0,)), ((), ()))

    def kernel(own_at, oth_at, len_at, cos_ref, up_ref, down_ref, q0, k0, v0, d0, q1, k1, v1, d1, *rest):
        att0, dq0, dk0, dv0, att1, dq1, dk1, dv1, qs, ks, vs, ds, att_s, dq_s, dk_s, dv_s = rest[len(earlier) :]
        seq = base + pl.program_id(0)
        length = len_at[seq]

        def turn(x, at):
            return (x * cos_ref[at, :] + pltpu.roll(x, 128 - half, 1) * up_ref[at, :]
                    + pltpu.roll(x, half, 1) * down_ref[at, :])

        def unturn(x, at):
            return (x * cos_ref[at, :] - pltpu.roll(x, 128 - half, 1) * up_ref[at, :]
                    - pltpu.roll(x, half, 1) * down_ref[at, :])

        sides = ((own_at, q0, k0, v0, d0, att0, dq0, dk0, dv0), (oth_at, q1, k1, v1, d1, att1, dq1, dk1, dv1))
        for where_at, q_ref, k_ref, v_ref, d_ref, *_ in sides:
            for j in range(per_side):
                at = pl.ds(pl.multiple_of(where_at[seq, j] * blk, blk), blk)
                here = slice(j * blk, (j + 1) * blk)
                qs[at, :] = (turn(q_ref[0, here, :].astype(jnp.float32), at)).astype(jnp.bfloat16) * jnp.bfloat16(scale)
                ks[at, :] = turn(k_ref[0, here, :].astype(jnp.float32), at).astype(jnp.bfloat16)
                vs[at, :] = v_ref[0, here, :]
                ds[at, :] = d_ref[0, here, :]
        att_s[...] = jnp.zeros_like(att_s)
        dq_s[...] = jnp.zeros_like(dq_s)
        dk_s[...] = jnp.zeros_like(dk_s)
        dv_s[...] = jnp.zeros_like(dv_s)
        lane = lax.broadcasted_iota(jnp.int32, (1, 128), 1)

        def one_head(h, carry):
            chosen = (lane // HEAD_DIM) == h
            keep_f = jnp.where(chosen, 1.0, 0.0)
            keep = keep_f.astype(jnp.bfloat16)
            for i in range(seq_len // step):
                rows = slice(i * step, (i + 1) * step)
                n = (i + 1) * step
                q = qs[rows, :] * keep
                d = ds[rows, :] * keep
                k = ks[:n, :]
                v = vs[:n, :]
                s = lax.dot_general(q, k, contract_last, preferred_element_type=jnp.float32)
                q_pos = i * step + lax.broadcasted_iota(jnp.int32, (step, 1), 0)
                limit = jnp.minimum(q_pos, length - 1)
                k_pos = lax.broadcasted_iota(jnp.int32, (step, n), 1)
                s = jnp.where(k_pos <= limit, s, -1e30)
                e = jnp.exp(s - jnp.max(s, axis=-1, keepdims=True))
                p = e * (1.0 / jnp.sum(e, axis=-1, keepdims=True))
                p_low = p.astype(jnp.bfloat16)
                dp = lax.dot_general(d, v, contract_last, preferred_element_type=jnp.float32)
                delta = jnp.sum(p * dp, axis=-1, keepdims=True)
                dsc = (p * (dp - delta)).astype(jnp.bfloat16)
                att_s[rows, :] += keep_f * jnp.dot(p_low, v, preferred_element_type=jnp.float32)
                dq_s[rows, :] += keep_f * jnp.dot(dsc, k, preferred_element_type=jnp.float32)
                dk_s[:n, :] += lax.dot_general(dsc, q, contract_first, preferred_element_type=jnp.float32)
                dv_s[:n, :] += lax.dot_general(p_low, d, contract_first, preferred_element_type=jnp.float32)
            return carry

        lax.fori_loop(0, 128 // HEAD_DIM, one_head, 0)
        for where_at, _, _, _, _, att_ref, dq_ref, dk_ref, dv_ref in sides:
            for j in range(per_side):
                at = pl.ds(pl.multiple_of(where_at[seq, j] * blk, blk), blk)
                here = slice(j * blk, (j + 1) * blk)
                att_ref[0, here, :] = att_s[at, :].astype(jnp.bfloat16)
                dq_ref[0, here, :] = unturn(dq_s[at, :] * scale, at).astype(jnp.bfloat16)
                dk_ref[0, here, :] = unturn(dk_s[at, :], at).astype(jnp.bfloat16)
                dv_ref[0, here, :] = dv_s[at, :].astype(jnp.bfloat16)

    def lanes(offset):
        return pl.BlockSpec((1, half_rows, 128), lambda s, p, *_: (base + s, 0, offset + p))

    table = pl.BlockSpec((seq_len, 128), lambda s, p, *_: (0, 0))
    side_in = [lanes(0), lanes(pairs), lanes(2 * pairs), lanes(0)]
    side_out = [lanes(0)] * 4
    narrow = jax.ShapeDtypeStruct((4, half_rows, heads_wide), jnp.bfloat16)
    work = seqs * pairs * 2 * seq_len * seq_len * 64
    result = pl.pallas_call(
        kernel,
        grid_spec=pltpu.PrefetchScalarGridSpec(
            num_scalar_prefetch=3,
            grid=(seqs, pairs),
            in_specs=[table] * 3 + side_in + side_in + [pl.BlockSpec(memory_space=pl.ANY)] * len(earlier),
            out_specs=side_out + side_out,
            scratch_shapes=[pltpu.VMEM((seq_len, 128), jnp.bfloat16)] * 4
            + [pltpu.VMEM((seq_len, 128), jnp.float32)] * 4,
        ),
        out_shape=[narrow] * 8,
        input_output_aliases={14 + i: i for i in range(len(earlier))},
        compiler_params=pltpu.CompilerParams(
            dimension_semantics=("arbitrary", "arbitrary"), vmem_limit_bytes=56 * 1024 * 1024
        ),
        cost_estimate=hint(
            flops=36 * work, transcendentals=work // 64, bytes_accessed=2 * 8 * seqs * seq_len * heads_wide
        ),
    )(deal_own, deal_oth, lengths, *tables, joined_own, joined_own, joined_own, datt_own,
      joined_oth, joined_oth, joined_oth, datt_oth, *earlier)
    return result


def plane_body(
    tokens, cotangent, lengths, deal, ln_gain, ln_bias, w_qkv, b_qkv, w_out, b_out, w_up, b_up, w_down, b_down
):
    core = lax.axis_index("dp")
    place = lax.axis_index("ctx")
    shard = lax.axis_index("fsdp")
    spot = 2 * shard + core
    _, micro, rows, width = tokens.shape
    blocks = deal.shape[2]
    blk = rows * 4 // blocks
    units = w_down.shape[0] // 2
    head_cols = w_out.shape[0] // 2

    meta = jnp.concatenate([deal[0].reshape(-1), lengths[0] // 64, lengths[0] % 64]).astype(LOW)
    theirs = swap_dp(meta)
    meta = jnp.where(place // micro == core, meta, theirs)
    turn = place % micro
    meta = jnp.concatenate([
        lax.dynamic_slice_in_dim(meta, turn * blocks, blocks), lax.dynamic_slice_in_dim(meta, micro * blocks + turn, 1),
        lax.dynamic_slice_in_dim(meta, micro * (blocks + 1) + turn, 1),
    ])
    size = 2 * ln_gain.shape[0] + b_qkv.shape[0] + b_out.shape[0] + b_up.shape[0] + b_down.shape[0] + meta.shape[0]
    small = jnp.concatenate([ln_gain, ln_bias, b_qkv, b_out, b_up, b_down, meta, jnp.zeros((-size % 512,), LOW)])

    small = lax.all_gather(small, "fsdp", axis=0, tiled=False)
    bounds = [0]
    for piece in (ln_gain, ln_bias, b_qkv, b_out, b_up, b_down, meta):
        bounds.append(bounds[-1] + piece.shape[0])
    gain, shift, bias_qkv, bias_out, bias_up, bias_down, meta = (small[:, a:b] for a, b in zip(bounds[:-1], bounds[1:]))
    gain, shift = gain.astype(WIDE).reshape(-1), shift.astype(WIDE).reshape(-1)
    own_blocks = lax.dynamic_slice_in_dim(deal[0], 2 * place, 2, axis=1)
    local_pos = (own_blocks[:, :, None] * blk + jnp.arange(blk, dtype=jnp.int32)).reshape(micro, rows)
    valid = (local_pos < lengths[0][:, None])[:, :, None]
    inputs = tokens[0].astype(WIDE)
    centered = inputs - jnp.mean(inputs, axis=-1, keepdims=True)
    inv_std = lax.rsqrt(jnp.mean(centered * centered, axis=-1, keepdims=True) + EPS)
    hidden_home = (centered * inv_std * gain + shift).astype(LOW)
    gout_home = jnp.where(valid, cotangent[0], jnp.zeros((), LOW))

    h_received = for_other(after(hidden_home, small), core, blk)
    up_sent = columns_sent([after(piece, small) for piece in columns_cut(w_up, 1, core, shard)])
    g_received = for_other(after(gout_home, h_received), core, blk)
    h_first, h_rest = slots_of(hidden_home, h_received, core, place, blk)
    h_pieces = spread_first(after(h_first, *[piece for _, _, piece in up_sent]))
    early = [piece for _, _, piece in h_pieces]
    h_rest = jnp.concatenate(h_rest)
    g_first, g_rest = slots_of(gout_home, after(g_received, h_rest), core, place, blk)
    h_pieces = h_pieces + spread_rest(after(h_rest, *early), blk)
    hidden_own = placed(h_pieces, shard, 4 * blk)
    hidden = (hidden_own, swap_dp(hidden_own))
    up_w = placed(up_sent, shard, w_up.shape[0])
    g_pieces = spread_first(after(g_first, *early))
    g_pieces = g_pieces + spread_rest(after(jnp.concatenate(g_rest), hidden_own, g_pieces[0][2]), blk)

    bias_ends = (bias_out.astype(WIDE) + bias_down.astype(WIDE)).reshape(-1)
    meta = meta.astype(jnp.int32)
    plane_len = meta[:, blocks] * 64 + meta[:, blocks + 1]
    plane_deal = meta[:, :blocks].reshape(4, 4, 2)[:, (place - jnp.arange(4, dtype=jnp.int32)) % 4]
    deal_own = pick(plane_deal, core, 2)
    deal_oth = pick(plane_deal, 1 - core, 2)
    up_b = lax.dynamic_slice_in_dim(bias_up.reshape(-1), spot * units, units).astype(WIDE)
    qkv_b = pick(bias_qkv.reshape(3, 8, head_cols), spot, 1).reshape(-1).astype(WIDE)

    acts, slopes, dups, datts = [], [], [], []
    for h in hidden:
        act, slope = up_call(h, up_w, up_b)
        acts.append(act)
        slopes.append(slope)
    gout_own = placed(g_pieces, shard, 4 * blk, acts[1])
    gout = (gout_own, swap_dp(gout_own))
    qkv_sent = columns_sent([after(piece, gout_own) for piece in columns_cut(w_qkv, 3, core, shard)])
    qkv_w = placed(qkv_sent, shard, w_qkv.shape[0])
    tables = rope_tables(8 * blk)
    down_w = lax.dynamic_slice_in_dim(w_down, core * units, units, 0)
    out_w = lax.dynamic_slice_in_dim(w_out, core * head_cols, head_cols, 0)

    def scatter(grad):
        return lax.psum_scatter(grad, "ctx", scatter_dimension=0, tiled=True)

    def gather(piece):
        return lax.all_gather(piece, "ctx", axis=0, tiled=True)

    def exchange(piece):
        return lax.all_to_all(piece[0], "fsdp", 0, 0, tiled=True)

    g_down = grad_call(acts, [gout])[0]
    t_down = gather(scatter(g_down))
    for g, slope in zip((after(gout[0], g_down), gout[1]), slopes):
        dup, datt = down_back_call(g, slope, down_w, out_w)
        dups.append(dup)
        datts.append(datt)
    g_up, s_up = grad_call((after(hidden[0], *dups), hidden[1]), [dups], sums=True, dealt=True)
    x_up = exchange(scatter(g_up))
    t_up = gather(x_up[None])
    joins = [join_call(after(h, g_up), qkv_w, qkv_b) for h in hidden]

    per_seq = (4, 4 * blk, -1)
    shaped = [piece.reshape(per_seq) for piece in (joins[0], joins[1], datts[0], datts[1])]
    sides = attention_call(deal_own, deal_oth, plane_len, *shaped, tables, blk, 0, 4)
    sides = [piece.reshape(16 * blk, -1) for piece in sides]
    atts = [sides[0], sides[4]]
    turned = [sides[1:4], sides[5:8]]

    g_qkv, s_q, s_k, s_v = grad_call(
        hidden, [(turned[0][i], turned[1][i]) for i in range(3)], sums=True, dealt=True
    )
    x_qkv = exchange(scatter(g_qkv))
    t_qkv = gather(x_qkv[None])
    b_oth = backward_call(dups[1], after(turned[1], g_qkv, t_down, x_up), up_w, qkv_w)
    o = grad_call(atts, [(after(gout[0], b_oth), gout[1])])[0]
    in_o = inward(o)
    b_total = backward_call(after(dups[0], o), turned[0], up_w, qkv_w, swap_dp(b_oth))
    d_hidden, d_hop = collect(b_total, shard)
    f_oth = forward_call(after(acts[1], b_total, in_o), atts[1], down_w, out_w)
    o = o + in_o
    ac_o = across(o)
    o_down = rows_out(core, shard, t_down, after(swap_dp(t_down), f_oth))
    f_total = forward_call(after(acts[0], o_down, ac_o, *d_hop), atts[0], down_w, out_w, swap_dp(f_oth))
    o = o + ac_o
    out_o = outward(o)
    t_out = line_end(o, out_o, place)
    mixed, _ = collect(f_total, shard)
    t_up = after(t_up, f_total)
    o_up = cols_out(core, shard, t_up, swap_dp(t_up), 1)
    d_hidden = to_home(d_hidden, core, place, blk).astype(WIDE)
    mixed = to_home(mixed, core, place, blk)
    sums_tp = line_sum(jnp.concatenate([s_up, s_q, s_k, s_v], axis=1), place)
    tails = lax.all_gather(sums_tp, ("fsdp", "dp"), axis=0, tiled=True)
    o_qkv = cols_out(core, shard, t_qkv, swap_dp(t_qkv), 3)
    o_out = rows_out(core, shard, t_out, swap_dp(t_out))

    result = jnp.where(valid, inputs + mixed.astype(WIDE) + bias_ends, 0.0).astype(LOW)
    normed = centered * inv_std
    d_norm = d_hidden * gain
    d_inputs = inv_std * (
        d_norm
        - jnp.mean(d_norm, axis=-1, keepdims=True)
        - normed * jnp.mean(d_norm * normed, axis=-1, keepdims=True)
    )
    back = (gout_home.astype(WIDE) + d_inputs).astype(LOW)

    d_bup = lax.dynamic_slice(tails, (2 * shard, 0), (2, units)).reshape(-1)
    d_bqkv = tails[:, units:].reshape(8, 3, head_cols).transpose(1, 0, 2).reshape(-1)
    d_bqkv = lax.dynamic_slice_in_dim(d_bqkv, shard * b_qkv.shape[0], b_qkv.shape[0])
    sums = jnp.stack([
        jnp.sum(d_hidden * normed, axis=(0, 1)), jnp.sum(d_hidden, axis=(0, 1)), jnp.sum(gout_home.astype(WIDE), axis=(0, 1)),
    ])
    sums = every_sum(sums, place)
    sums = lax.dynamic_slice_in_dim(sums, shard * ln_gain.shape[0], ln_gain.shape[0], 1)

    return result[None], back[None], sums[0], sums[1], o_qkv, d_bqkv, o_out, sums[2], o_up, d_bup, o_down, sums[2]


def plane_fits(mesh, shapes):
    tokens, _, _, deal = shapes[:4]
    sizes = dict(mesh.shape)
    dp, ctx, fsdp = sizes["dp"], sizes["ctx"], sizes["fsdp"]
    micro, seq_len, width = tokens.shape[1:]
    blocks = deal.shape[2]
    heads = width // HEAD_DIM
    return (
        dp == 2
        and dp * micro == ctx == fsdp == 4
        and tokens.shape[0] == dp * fsdp
        and blocks == dp * ctx
        and heads % (2 * dp * fsdp) == 0
        and seq_len % 256 == 0
        and (seq_len // blocks) % 128 == 0
    )


def solution(mesh):
    in_specs = (
        P(("dp", "fsdp"), None, "ctx", None),
        P(("dp", "fsdp"), None, "ctx", None),
        P(("dp", "fsdp"), None),
        P(("dp", "fsdp"), None, None),
        P("fsdp"),
        P("fsdp"),
        P("fsdp", None),
        P("fsdp"),
        P("fsdp", None),
        P("fsdp"),
        P("fsdp", None),
        P("fsdp"),
        P("fsdp", None),
        P("fsdp"),
    )
    out_specs = (
        P(("dp", "fsdp"), None, "ctx", None),
        P(("dp", "fsdp"), None, "ctx", None),
        P("fsdp"),
        P("fsdp"),
        P("fsdp", None),
        P("fsdp"),
        P("fsdp", None),
        P("fsdp"),
        P("fsdp", None),
        P("fsdp"),
        P("fsdp", None),
        P("fsdp"),
    )

    def program(*arrays):
        body = plane_body if plane_fits(mesh, arrays) else gathered_body
        return jax.shard_map(body, mesh=mesh, in_specs=in_specs, out_specs=out_specs, check_vma=False)(*arrays)

    return program
```

```python
import jax
import jax.numpy as jnp
from jax import lax
from jax.experimental import pallas as pl
from jax.experimental.pallas import tpu as pltpu
from jax.sharding import PartitionSpec as P

HEAD_DIM = 64
ROT = 32


EPS = 1e-05
BASE = 10000.0


def contract_rows(left, right):
    return lax.dot_general(
        left, right, (((0,), (0,)), ((), ())), preferred_element_type=jnp.float32
    )


def contract_cols(left, right):
    return lax.dot_general(
        left, right, (((1,), (1,)), ((), ())), preferred_element_type=jnp.float32
    )


def angles_of(positions):
    half = ROT // 2
    freqs = BASE ** (-(jnp.arange(half, dtype=jnp.float32) * 2.0) / ROT)
    angles = positions.astype(jnp.float32)[:, None] * freqs[None, :]
    return (jnp.cos(angles)[:, None, :], jnp.sin(angles)[:, None, :])


def rotate(values, cosine, sine):
    half = ROT // 2
    first = values[..., :half]
    second = values[..., half:ROT]
    return jnp.concatenate(
        [first * cosine - second * sine, second * cosine + first * sine, values[..., ROT:]], axis=-1
    )


def rotate_back(values, cosine, sine):
    half = ROT // 2
    first = values[..., :half]
    second = values[..., half:ROT]
    return jnp.concatenate(
        [first * cosine + second * sine, second * cosine - first * sine, values[..., ROT:]], axis=-1
    )


def layer_step(weights, inputs, upstream, length, deal_row):
    gain, shift, w_qkv, b_qkv, w_out, b_out, w_up, b_up, w_down, b_down = weights
    row_count, width = inputs.shape
    block_rows = row_count // 2
    head_count = width // HEAD_DIM
    scale = HEAD_DIM ** (-0.5)
    place = lax.axis_index("ctx")
    offsets = jnp.arange(block_rows, dtype=jnp.int32)
    own_blocks = lax.dynamic_slice_in_dim(deal_row, 2 * place, 2)
    local_pos = (own_blocks[:, None] * block_rows + offsets[None, :]).reshape(row_count)
    every_pos = (deal_row[:, None] * block_rows + offsets[None, :]).reshape(-1)
    valid = (local_pos < length).astype(jnp.float32)[:, None]
    allowed = (every_pos[None, :] <= local_pos[:, None]) & (every_pos[None, :] < length)
    cosine, sine = angles_of(local_pos)
    inputs_f = inputs.astype(jnp.float32)
    gain_f = gain.astype(jnp.float32)
    centered = inputs_f - jnp.mean(inputs_f, axis=-1, keepdims=True)
    variance = jnp.mean(centered * centered, axis=-1, keepdims=True)
    inv_std = lax.rsqrt(variance + EPS)
    normed = centered * inv_std
    hidden = (normed * gain_f + shift.astype(jnp.float32)).astype(jnp.bfloat16)
    joined = jnp.dot(hidden, w_qkv, preferred_element_type=jnp.float32) + b_qkv.astype(jnp.float32)
    query = (
        rotate(joined[:, :width].reshape(row_count, head_count, HEAD_DIM), cosine, sine)
        .reshape(row_count, width)
        .astype(jnp.bfloat16)
    )
    keyed = (
        rotate(joined[:, width : 2 * width].reshape(row_count, head_count, HEAD_DIM), cosine, sine)
        .reshape(row_count, width)
        .astype(jnp.bfloat16)
    )
    valued = joined[:, 2 * width :].astype(jnp.bfloat16)
    keys_all, values_all = (
        lax.all_gather(keyed, "ctx", axis=0, tiled=True),
        lax.all_gather(valued, "ctx", axis=0, tiled=True),
    )
    total_keys = keys_all.shape[0]
    group = min(8, head_count)
    span = group * HEAD_DIM

    def heads_of(array, start, count):
        return array[:, start : start + span].reshape(count, group, HEAD_DIM)

    def block_scores(start):
        raw = (
            jnp.einsum(
                "qhd,khd->hqk",
                heads_of(query, start, row_count),
                heads_of(keys_all, start, total_keys),
                preferred_element_type=jnp.float32,
            )
            * scale
        )
        return jnp.where(allowed[None], raw, -1e30)

    attended_parts = []
    lse_parts = []
    for start in range(0, width, span):
        masked = block_scores(start)
        highest = jnp.max(masked, axis=-1, keepdims=True)
        expo = jnp.exp(masked - highest)
        total = jnp.sum(expo, axis=-1, keepdims=True)
        weights_low = (expo / total).astype(jnp.bfloat16)
        mixed = jnp.einsum(
            "hqk,khd->qhd",
            weights_low,
            heads_of(values_all, start, total_keys),
            preferred_element_type=jnp.float32,
        )
        attended_parts.append(mixed.reshape(row_count, span))
        lse_parts.append(highest + jnp.log(total))
    attended = jnp.concatenate(attended_parts, axis=1).astype(jnp.bfloat16)
    branch = jnp.dot(attended, w_out, preferred_element_type=jnp.float32) + b_out.astype(
        jnp.float32
    )
    upward = jnp.dot(hidden, w_up, preferred_element_type=jnp.float32) + b_up.astype(jnp.float32)
    activated = jax.nn.gelu(upward, approximate=True).astype(jnp.bfloat16)
    feed = jnp.dot(activated, w_down, preferred_element_type=jnp.float32) + b_down.astype(
        jnp.float32
    )
    result = (valid * (inputs_f + branch + feed)).astype(jnp.bfloat16)
    grad_out = upstream.astype(jnp.float32) * valid
    grad_low = grad_out.astype(jnp.bfloat16)
    row_total = jnp.sum(grad_out, axis=0)
    d_down = contract_rows(activated, grad_low)
    d_wout = contract_rows(attended, grad_low)
    d_act = contract_cols(grad_low, w_down)
    _, gelu_pull = jax.vjp(lambda value: jax.nn.gelu(value, approximate=True), upward)
    d_upward = gelu_pull(d_act)[0].astype(jnp.bfloat16)
    d_wup = contract_rows(hidden, d_upward)
    d_bup = jnp.sum(d_upward.astype(jnp.float32), axis=0)
    d_attended = contract_cols(grad_low, w_out).astype(jnp.bfloat16)
    dq_parts = []
    dk_parts = []
    dv_parts = []
    delta_parts = []
    for index, start in enumerate(range(0, width, span)):
        masked = block_scores(start)
        probs = jnp.where(allowed[None], jnp.exp(masked - lse_parts[index]), 0.0)
        d_heads = heads_of(d_attended, start, row_count)
        d_probs = jnp.einsum(
            "qhd,khd->hqk",
            d_heads,
            heads_of(values_all, start, total_keys),
            preferred_element_type=jnp.float32,
        )
        delta = jnp.sum(probs * d_probs, axis=-1, keepdims=True)
        d_scores = (probs * (d_probs - delta)).astype(jnp.bfloat16)
        d_query = (
            jnp.einsum(
                "hqk,khd->qhd",
                d_scores,
                heads_of(keys_all, start, total_keys),
                preferred_element_type=jnp.float32,
            )
            * scale
        )
        dq_parts.append(d_query.reshape(row_count, span))
        delta_parts.append(delta[:, :, 0].T)
        d_keyed = (
            jnp.einsum(
                "hqk,qhd->khd",
                d_scores,
                heads_of(query, start, row_count),
                preferred_element_type=jnp.float32,
            )
            * scale
        )
        d_valued = jnp.einsum(
            "hqk,qhd->khd", probs.astype(jnp.bfloat16), d_heads, preferred_element_type=jnp.float32
        )
        dk_parts.append(d_keyed.reshape(total_keys, span))
        dv_parts.append(d_valued.reshape(total_keys, span))
    keys_grad_all = jnp.concatenate(dk_parts, axis=1)
    values_grad_all = jnp.concatenate(dv_parts, axis=1)
    keys_grad, values_grad = (
        lax.psum_scatter(
            keys_grad_all.astype(jnp.bfloat16), "ctx", scatter_dimension=0, tiled=True
        ).astype(jnp.float32),
        lax.psum_scatter(
            values_grad_all.astype(jnp.bfloat16), "ctx", scatter_dimension=0, tiled=True
        ).astype(jnp.float32),
    )
    query_grad = rotate_back(
        jnp.concatenate(dq_parts, axis=1).reshape(row_count, head_count, HEAD_DIM), cosine, sine
    ).reshape(row_count, width)
    keyed_grad = rotate_back(
        keys_grad.reshape(row_count, head_count, HEAD_DIM), cosine, sine
    ).reshape(row_count, width)
    d_joined = jnp.concatenate([query_grad, keyed_grad, values_grad], axis=1).astype(jnp.bfloat16)
    d_wqkv = contract_rows(hidden, d_joined)
    d_bqkv = jnp.sum(d_joined.astype(jnp.float32), axis=0)
    d_hidden = contract_cols(d_joined, w_qkv) + contract_cols(d_upward, w_up)
    d_gain = jnp.sum(d_hidden * normed, axis=0)
    d_shift = jnp.sum(d_hidden, axis=0)
    d_norm = d_hidden * gain_f
    d_inputs = inv_std * (
        d_norm
        - jnp.mean(d_norm, axis=-1, keepdims=True)
        - normed * jnp.mean(d_norm * normed, axis=-1, keepdims=True)
    )
    back = (grad_out + d_inputs).astype(jnp.bfloat16)
    return (
        result,
        back,
        (d_gain, d_shift, d_wqkv, d_bqkv, d_wout, row_total, d_wup, d_bup, d_down, row_total),
    )


def gathered_body(
    tokens,
    cotangent,
    lengths,
    deal,
    ln_gain,
    ln_bias,
    w_qkv,
    b_qkv,
    w_out,
    b_out,
    w_up,
    b_up,
    w_down,
    b_down,
):
    shards = (ln_gain, ln_bias, w_qkv, b_qkv, w_out, b_out, w_up, b_up, w_down, b_down)
    shard_count = lax.axis_size("fsdp")
    summed = tuple(
        (
            jnp.zeros((piece.shape[0] * shard_count,) + piece.shape[1:], jnp.float32)
            for piece in shards
        )
    )
    results = []
    backs = []
    for micro_index in range(tokens.shape[1]):
        gathered = (
            lax.all_gather(ln_gain, "fsdp", axis=0, tiled=True),
            lax.all_gather(ln_bias, "fsdp", axis=0, tiled=True),
            lax.all_gather(w_qkv, "fsdp", axis=0, tiled=True),
            lax.all_gather(b_qkv, "fsdp", axis=0, tiled=True),
            lax.all_gather(w_out, "fsdp", axis=0, tiled=True),
            lax.all_gather(b_out, "fsdp", axis=0, tiled=True),
            lax.all_gather(w_up, "fsdp", axis=0, tiled=True),
            lax.all_gather(b_up, "fsdp", axis=0, tiled=True),
            lax.all_gather(w_down, "fsdp", axis=0, tiled=True),
            lax.all_gather(b_down, "fsdp", axis=0, tiled=True),
        )
        result, back, local = layer_step(
            gathered,
            tokens[0, micro_index],
            cotangent[0, micro_index],
            lengths[0, micro_index],
            deal[0, micro_index],
        )
        results.append(result)
        backs.append(back)
        summed = tuple((older + newer for older, newer in zip(summed, local)))
    summed = (
        lax.psum_scatter(
            summed[0].astype(jnp.bfloat16), "fsdp", scatter_dimension=0, tiled=True
        ).astype(jnp.float32),
        lax.psum_scatter(
            summed[1].astype(jnp.bfloat16), "fsdp", scatter_dimension=0, tiled=True
        ).astype(jnp.float32),
        lax.psum_scatter(
            summed[2].astype(jnp.bfloat16), "fsdp", scatter_dimension=0, tiled=True
        ).astype(jnp.float32),
        lax.psum_scatter(
            summed[3].astype(jnp.bfloat16), "fsdp", scatter_dimension=0, tiled=True
        ).astype(jnp.float32),
        lax.psum_scatter(
            summed[4].astype(jnp.bfloat16), "fsdp", scatter_dimension=0, tiled=True
        ).astype(jnp.float32),
        lax.psum_scatter(
            summed[5].astype(jnp.bfloat16), "fsdp", scatter_dimension=0, tiled=True
        ).astype(jnp.float32),
        lax.psum_scatter(
            summed[6].astype(jnp.bfloat16), "fsdp", scatter_dimension=0, tiled=True
        ).astype(jnp.float32),
        lax.psum_scatter(
            summed[7].astype(jnp.bfloat16), "fsdp", scatter_dimension=0, tiled=True
        ).astype(jnp.float32),
        lax.psum_scatter(
            summed[8].astype(jnp.bfloat16), "fsdp", scatter_dimension=0, tiled=True
        ).astype(jnp.float32),
        lax.psum_scatter(
            summed[9].astype(jnp.bfloat16), "fsdp", scatter_dimension=0, tiled=True
        ).astype(jnp.float32),
    )
    totals = (
        lax.psum(summed[0].astype(jnp.bfloat16), ("dp", "ctx")).astype(jnp.float32),
        lax.psum(summed[1].astype(jnp.bfloat16), ("dp", "ctx")).astype(jnp.float32),
        lax.psum(summed[2].astype(jnp.bfloat16), ("dp", "ctx")).astype(jnp.float32),
        lax.psum(summed[3].astype(jnp.bfloat16), ("dp", "ctx")).astype(jnp.float32),
        lax.psum(summed[4].astype(jnp.bfloat16), ("dp", "ctx")).astype(jnp.float32),
        lax.psum(summed[5].astype(jnp.bfloat16), ("dp", "ctx")).astype(jnp.float32),
        lax.psum(summed[6].astype(jnp.bfloat16), ("dp", "ctx")).astype(jnp.float32),
        lax.psum(summed[7].astype(jnp.bfloat16), ("dp", "ctx")).astype(jnp.float32),
        lax.psum(summed[8].astype(jnp.bfloat16), ("dp", "ctx")).astype(jnp.float32),
        lax.psum(summed[9].astype(jnp.bfloat16), ("dp", "ctx")).astype(jnp.float32),
    )
    stacked_out = jnp.stack(results)[None]
    stacked_back = jnp.stack(backs)[None]
    return (
        stacked_out,
        stacked_back,
        totals[0],
        totals[1],
        totals[2],
        totals[3],
        totals[4],
        totals[5],
        totals[6],
        totals[7],
        totals[8],
        totals[9],
    )


SWAP = [(0, 1), (1, 0)]
LOW = jnp.bfloat16
SLOW = 1.8
WIDE = jnp.float32


def hint(flops, transcendentals, bytes_accessed):
    return pl.CostEstimate(
        flops=int(flops * SLOW), transcendentals=transcendentals, bytes_accessed=bytes_accessed
    )


def after(value, *others):
    return lax.optimization_barrier((value,) + others)[0]


def swap_dp(value):
    return lax.ppermute(value, "dp", SWAP)


def swap_shard(value, bits):
    return lax.ppermute(value, "fsdp", [(i, i ^ bits) for i in range(4)])


def shift_ctx(value, steps):
    return lax.ppermute(value, "ctx", [(i, (i + steps) % 4) for i in range(4)])


def pick(array, index, axis):
    return lax.dynamic_index_in_dim(array, index, axis, keepdims=False)


def by_core(core, mine, other, axis):
    first = jnp.where(core == 0, mine, other)
    second = jnp.where(core == 0, other, mine)
    return jnp.stack([first, second], axis=axis)


def for_other(rows, core, blk):
    micro, _, width = rows.shape
    return swap_dp(pick(rows.reshape(micro, 2, blk, width), 1 - core, 1))


def deal_out(rows, received, core, blk):
    micro, _, width = rows.shape
    lined = by_core(core, pick(rows.reshape(micro, 2, blk, width), core, 1), received, 0).reshape(4, blk, width)
    return lax.all_to_all(lined, "ctx", 0, 0, tiled=True).reshape(4 * blk, width)


def placed(pieces, shard, size, *gates):
    whole = after(jnp.zeros((4 * size, pieces[0][2].shape[1]), LOW), *gates)
    for bits, start, piece in pieces:
        whole = lax.dynamic_update_slice(whole, piece, ((shard ^ bits) * size + start, 0))
    return whole


def plus(first, *others):
    total = first.astype(WIDE)
    for other in others:
        total = total + other.astype(WIDE)
    return total.astype(LOW)


def collect(total, shard, *gates):
    size = total.shape[0] // 4
    half = size // 2

    def part(bits, which):
        return lax.dynamic_slice_in_dim(total, (shard ^ bits) * size + which * half, half, 0)

    via_x, via_y = swap_shard(part(3, 0), 1), swap_shard(part(3, 1), 2)
    x_top, y_end = swap_shard(part(1, 0), 1), swap_shard(part(2, 1), 2)
    y_top = swap_shard(plus(part(2, 0), after(via_x, *gates)), 2)
    x_end = swap_shard(plus(part(1, 1), after(via_y, *gates)), 1)
    return jnp.concatenate([plus(part(0, 0), x_top, y_top), plus(part(0, 1), x_end, y_end)])


def to_home(mine, core, place, blk):
    width = mine.shape[1]
    lined = lax.all_to_all(mine.reshape(4, blk, width), "ctx", 0, 0, tiled=True).reshape(2, 2, blk, width)
    kept = pick(lined, core, 0)
    received = swap_dp(pick(lined, 1 - core, 0))
    return by_core(core, kept, received, 1).reshape(2, 2 * blk, width)


def columns_cut(weight, parts, core, shard):
    width = weight.shape[1] // (parts * 8)
    pieces = []
    for bits in range(4):
        spot = 2 * (shard ^ bits) + core
        pieces.append(jnp.concatenate(
            [lax.dynamic_slice_in_dim(weight, (t * 8 + spot) * width, width, 1) for t in range(parts)], axis=1
        ))
    return pieces


def columns_sent(pieces):
    return [(bits, 0, piece if bits == 0 else swap_shard(piece, bits)) for bits, piece in enumerate(pieces)]


def inward(value):
    return lax.ppermute(value, "ctx", [(0, 1), (3, 2)])


def across(value):
    return lax.ppermute(value, "ctx", [(1, 2), (2, 1)])


def outward(value):
    return lax.ppermute(value, "ctx", [(1, 0), (2, 3)])


def line_sum(value, place):
    half = value + inward(value)
    whole = half + across(half)
    return line_end(whole, outward(whole), place)


def line_end(whole, received, place):
    return jnp.where((place == 1) | (place == 2), whole, received)


def every_sum(value, place):
    value = value + swap_dp(value)
    value = value + swap_shard(value, 1)
    value = value + swap_shard(value, 2)
    return line_sum(value, place)


def lay_out(core, shard, own, oth, out_shape, grid, block, in_at, out_at):
    def kernel(where, own_ref, oth_ref, out_ref):
        side = pl.program_id(len(grid))

        @pl.when(side == 0)
        def _():
            out_ref[...] = own_ref[...].astype(WIDE)

        @pl.when(side == 1)
        def _():
            out_ref[...] = oth_ref[...].astype(WIDE)

    source = pl.BlockSpec(block, lambda *args: in_at(*args[: len(grid)]))
    target = pl.BlockSpec(block, lambda *args: out_at(*args[:-1], args[-1][0], args[-1][1]))
    count = out_shape[0] * out_shape[1]
    return pl.pallas_call(
        kernel,
        grid_spec=pltpu.PrefetchScalarGridSpec(
            num_scalar_prefetch=1, grid=grid + (2,), in_specs=[source, source], out_specs=target
        ),
        out_shape=jax.ShapeDtypeStruct(out_shape, WIDE),
        compiler_params=pltpu.CompilerParams(dimension_semantics=("arbitrary",) * (len(grid) + 1)),
        cost_estimate=hint(flops=0, transcendentals=0, bytes_accessed=6 * count),
    )(jnp.stack([core, shard]).astype(jnp.int32), own, oth)


def rows_out(core, shard, own, oth):
    rows, width = own.shape
    tile = min(256, rows)
    steps = rows // tile
    return lay_out(
        core, shard, own, oth, (2 * rows, width), (steps,), (tile, width),
        lambda i: (i, 0), lambda i, s, c, f: ((c ^ s) * steps + i, 0),
    )


def cols_out(core, shard, own, oth, parts, held):
    lines, columns, rows, width = own.shape
    width = width // held

    def kernel(where, own_ref, oth_ref, out_ref):
        side = pl.program_id(2)

        @pl.when(side == 0)
        def _():
            out_ref[...] = own_ref[...].reshape(lines * rows, width).astype(WIDE)

        @pl.when(side == 1)
        def _():
            out_ref[...] = oth_ref[...].reshape(lines * rows, width).astype(WIDE)

    source = pl.BlockSpec((lines, 1, rows, width), lambda b, t, s, where: (0, b, 0, t))
    target = pl.BlockSpec((lines * rows, width), lambda b, t, s, where: (0, t * 8 + 2 * b + (where[0] ^ s)))
    return pl.pallas_call(
        kernel,
        grid_spec=pltpu.PrefetchScalarGridSpec(
            num_scalar_prefetch=1, grid=(columns, parts, 2), in_specs=[source, source], out_specs=target
        ),
        out_shape=jax.ShapeDtypeStruct((lines * rows, 2 * columns * parts * width), WIDE),
        compiler_params=pltpu.CompilerParams(dimension_semantics=("arbitrary",) * 3),
        cost_estimate=pl.CostEstimate(flops=0, transcendentals=0, bytes_accessed=12 * own.size),
    )(jnp.stack([core, shard]).astype(jnp.int32), own, oth)


GELU_C = 0.7978845608028654
GELU_A = 0.044715


def gelu_pair(value):
    square = value * value
    tanh = jnp.tanh(GELU_C * value * (1.0 + GELU_A * square))
    half = 0.5 * (1.0 + tanh)
    slope = half + 0.5 * value * (1.0 - tanh * tanh) * (GELU_C * (1.0 + 3.0 * GELU_A * square))
    return value * half, slope


ROWS_OF = (((0,), (0,)), ((), ()))
COLS_OF = (((1,), (1,)), ((), ()))
ROOM = 56 * 1024 * 1024


def row_call(body, tiled, whole, widths, flops, tile=512):
    count = tiled[0].shape[0]

    def rows_spec(width):
        return pl.BlockSpec((tile, width), lambda i: (i, 0))

    moved = sum(a.size * a.dtype.itemsize for a in (*tiled, *whole)) + 2 * count * sum(widths)
    return pl.pallas_call(
        body,
        grid=(count // tile,),
        in_specs=[rows_spec(a.shape[1]) for a in tiled]
        + [pl.BlockSpec(a.shape, lambda i: (0, 0), pipeline_mode=pl.Buffered(1)) for a in whole],
        out_specs=[rows_spec(width) for width in widths],
        out_shape=[jax.ShapeDtypeStruct((count, width), LOW) for width in widths],
        compiler_params=pltpu.CompilerParams(dimension_semantics=("arbitrary",), vmem_limit_bytes=ROOM),
        cost_estimate=hint(flops=flops, transcendentals=0, bytes_accessed=moved),
    )(*tiled, *whole)


def strips(width):
    step = min(256, width)
    return [slice(at, at + step) for at in range(0, width, step)]


def up_call(rows, weight, bias):
    def body(rows_ref, weight_ref, bias_ref, act_ref, slope_ref):
        for at in strips(weight.shape[1]):
            total = jnp.dot(rows_ref[...], weight_ref[:, at], preferred_element_type=WIDE) + bias_ref[:, at]
            act, slope = gelu_pair(total)
            act_ref[:, at] = act.astype(LOW)
            slope_ref[:, at] = slope.astype(LOW)

    width = weight.shape[1]
    return row_call(body, [rows], [weight, bias[None]], [width, width], 2 * rows.shape[0] * weight.size)


def join_call(rows, weight, bias):
    def body(rows_ref, weight_ref, bias_ref, out_ref):
        for at in strips(weight.shape[1]):
            total = jnp.dot(rows_ref[...], weight_ref[:, at], preferred_element_type=WIDE)
            out_ref[:, at] = (total + bias_ref[:, at]).astype(LOW)

    return row_call(body, [rows], [weight, bias[None]], [weight.shape[1]], 2 * rows.shape[0] * weight.size)[0]


def down_back_call(rows, slopes, down_w, out_w):
    def body(rows_ref, slope_ref, down_ref, out_w_ref, dup_ref, datt_ref):
        for at in strips(down_w.shape[0]):
            total = lax.dot_general(rows_ref[...], down_ref[at, :], COLS_OF, preferred_element_type=WIDE)
            dup_ref[:, at] = (total * slope_ref[:, at].astype(WIDE)).astype(LOW)
        total = lax.dot_general(rows_ref[...], out_w_ref[...], COLS_OF, preferred_element_type=WIDE)
        datt_ref[...] = total.astype(LOW)

    flops = 2 * rows.shape[0] * (down_w.size + out_w.size)
    return row_call(body, [rows, slopes], [down_w, out_w], [down_w.shape[0], out_w.shape[0]], flops)


def forward_call(act, att, down_w, out_w, added=None):
    def body(*refs):
        act_ref, att_ref = refs[:2]
        down_ref, out_w_ref, out_ref = refs[-3:]
        for at in strips(down_w.shape[1]):
            total = jnp.dot(act_ref[...], down_ref[:, at], preferred_element_type=WIDE)
            total = total + jnp.dot(att_ref[...], out_w_ref[:, at], preferred_element_type=WIDE)
            if added is not None:
                total = total + refs[2][:, at].astype(WIDE)
            out_ref[:, at] = total.astype(LOW)

    tiled = [act, att] + ([] if added is None else [added])
    flops = 2 * act.shape[0] * (down_w.size + out_w.size)
    return row_call(body, tiled, [down_w, out_w], [down_w.shape[1]], flops)[0]


def backward_call(dup, turned, up_w, qkv_w, added=None):
    wide = turned[0].shape[1]

    def body(*refs):
        dup_ref, turned_refs = refs[0], refs[1:4]
        up_ref, qkv_ref, out_ref = refs[-3:]
        for at in strips(up_w.shape[0]):
            total = lax.dot_general(dup_ref[...], up_ref[at, :], COLS_OF, preferred_element_type=WIDE)
            for i, ref in enumerate(turned_refs):
                part = qkv_ref[at, i * wide : (i + 1) * wide]
                total = total + lax.dot_general(ref[...], part, COLS_OF, preferred_element_type=WIDE)
            if added is not None:
                total = total + refs[4][:, at].astype(WIDE)
            out_ref[:, at] = total.astype(LOW)

    tiled = [dup, *turned] + ([] if added is None else [added])
    flops = 2 * dup.shape[0] * (up_w.size + qkv_w.size)
    return row_call(body, tiled, [up_w, qkv_w], [up_w.shape[0]], flops)[0]


def grad_call(left, rights, left_part=(0, 1), right_part=(0, 1), sums=False, dealt=False, flip=False, tile=512):
    steps = left[0].shape[0] // tile
    left_cols = left[0].shape[1] // left_part[1]
    right_cols = [pair[0].shape[1] // right_part[1] for pair in rights]
    count = len(rights)
    piece = (right_cols[0] if flip else left_cols) // 16
    made = 1 if dealt else count

    def body(*refs):
        ins, outs = refs[: 2 + 2 * count], refs[2 + 2 * count :]
        grads, totals, accs = outs[:made], outs[made : len(outs) - count], outs[len(outs) - count :]
        step = pl.program_id(0)

        @pl.when(step == 0)
        def _():
            for ref in (*accs, *totals):
                ref[...] = jnp.zeros_like(ref)

        def add(left_ref, right_refs):
            for i, ref in enumerate(right_refs):
                for at in strips(right_cols[i]):
                    accs[i][:, at] += lax.dot_general(
                        left_ref[...], ref[:, at], ROWS_OF, preferred_element_type=WIDE
                    )
                if sums:
                    totals[i][...] += jnp.sum(ref[...].astype(WIDE), axis=0, keepdims=True)

        @pl.when(step < steps)
        def _():
            add(ins[0], ins[2 : 2 + count])

        @pl.when(step >= steps)
        def _():
            add(ins[1], ins[2 + count :])

        @pl.when(step == 2 * steps - 1)
        def _():
            if not dealt:
                for grad, acc in zip(grads, accs):
                    grad[...] = acc[...].astype(LOW)
                return
            if flip:
                for spot in range(16):
                    part = accs[0][:, spot * piece : (spot + 1) * piece]
                    grads[0][spot % 4, spot // 4] = part.T.astype(LOW)
                return
            start = 0
            for acc, cols in zip(accs, right_cols):
                for column in range(4):
                    for line in range(4):
                        at = (4 * column + line) * piece
                        grads[0][line, column, :, start : start + cols] = acc[at : at + piece, :].astype(LOW)
                start += cols

    def side_spec(cols, part, side):
        def at(step):
            row = jnp.minimum(step, steps - 1) if side == 0 else jnp.maximum(step - steps, 0)
            return (row, part)

        return pl.BlockSpec((tile, cols), at)

    def fixed(shape):
        return pl.BlockSpec(shape, lambda step: (0,) * len(shape))

    specs = [side_spec(left_cols, left_part[0], side) for side in (0, 1)]
    specs += [side_spec(cols, right_part[0], side) for side in (0, 1) for cols in right_cols]
    shapes = [jax.ShapeDtypeStruct((left_cols, cols), LOW) for cols in right_cols]
    if dealt:
        shapes = [jax.ShapeDtypeStruct((4, 4, piece, left_cols if flip else sum(right_cols)), LOW)]
    if sums:
        shapes += [jax.ShapeDtypeStruct((1, cols), WIDE) for cols in right_cols]
    rows = 2 * left[0].shape[0]
    return pl.pallas_call(
        body,
        grid=(2 * steps,),
        in_specs=specs,
        out_specs=[fixed(shape.shape) for shape in shapes],
        out_shape=shapes,
        scratch_shapes=[pltpu.VMEM((left_cols, cols), WIDE) for cols in right_cols],
        compiler_params=pltpu.CompilerParams(dimension_semantics=("arbitrary",), vmem_limit_bytes=ROOM),
        cost_estimate=hint(
            flops=2 * rows * left_cols * sum(right_cols), transcendentals=0,
            bytes_accessed=2 * rows * (left_cols + sum(right_cols)),
        ),
    )(*left, *[pair[0] for pair in rights], *[pair[1] for pair in rights])


def rope_tables(seq_len):
    lane = jnp.arange(2 * HEAD_DIM, dtype=jnp.int32) % HEAD_DIM
    half = ROT // 2
    turned = lane < ROT
    index = jnp.where(turned, lane % half, 0).astype(jnp.float32)
    freqs = BASE ** (-(index * 2.0) / ROT)
    angles = jnp.arange(seq_len, dtype=jnp.float32)[:, None] * freqs[None, :]
    sine = jnp.sin(angles)
    cosine = jnp.where(turned[None], jnp.cos(angles), 1.0)
    up = jnp.where((lane < half)[None], -sine, 0.0)
    down = jnp.where(((lane >= half) & turned)[None], sine, 0.0)
    return cosine, up, down


def attention_call(deal_own, deal_oth, lengths, joined_own, joined_oth, datt_own, datt_oth, tables, blk, base, seqs, earlier=()):
    _, half_rows, wide = joined_own.shape
    heads_wide = wide // 3
    pairs = heads_wide // 128
    seq_len = 2 * half_rows
    per_side = half_rows // blk
    step = 256
    scale = HEAD_DIM ** (-0.5)
    half = ROT // 2
    contract_last = (((1,), (1,)), ((), ()))
    contract_first = (((0,), (0,)), ((), ()))

    def kernel(own_at, oth_at, len_at, cos_ref, up_ref, down_ref, q0, k0, v0, d0, q1, k1, v1, d1, *rest):
        att0, dq0, dk0, dv0, att1, dq1, dk1, dv1, qs, ks, vs, ds, att_s, dq_s, dk_s, dv_s = rest[len(earlier) :]
        seq = base + pl.program_id(0)
        length = len_at[seq]

        def turn(x, at):
            return (x * cos_ref[at, :] + pltpu.roll(x, 128 - half, 1) * up_ref[at, :]
                    + pltpu.roll(x, half, 1) * down_ref[at, :])

        def unturn(x, at):
            return (x * cos_ref[at, :] - pltpu.roll(x, 128 - half, 1) * up_ref[at, :]
                    - pltpu.roll(x, half, 1) * down_ref[at, :])

        sides = ((own_at, q0, k0, v0, d0, att0, dq0, dk0, dv0), (oth_at, q1, k1, v1, d1, att1, dq1, dk1, dv1))
        for where_at, q_ref, k_ref, v_ref, d_ref, *_ in sides:
            for j in range(per_side):
                at = pl.ds(pl.multiple_of(where_at[seq, j] * blk, blk), blk)
                here = slice(j * blk, (j + 1) * blk)
                qs[at, :] = (turn(q_ref[0, here, :].astype(jnp.float32), at)).astype(jnp.bfloat16) * jnp.bfloat16(scale)
                ks[at, :] = turn(k_ref[0, here, :].astype(jnp.float32), at).astype(jnp.bfloat16)
                vs[at, :] = v_ref[0, here, :]
                ds[at, :] = d_ref[0, here, :]
        att_s[...] = jnp.zeros_like(att_s)
        dq_s[...] = jnp.zeros_like(dq_s)
        dk_s[...] = jnp.zeros_like(dk_s)
        dv_s[...] = jnp.zeros_like(dv_s)
        lane = lax.broadcasted_iota(jnp.int32, (1, 128), 1)

        def one_head(h, carry):
            chosen = (lane // HEAD_DIM) == h
            keep_f = jnp.where(chosen, 1.0, 0.0)
            keep = keep_f.astype(jnp.bfloat16)
            for i in range(seq_len // step):
                rows = slice(i * step, (i + 1) * step)
                n = (i + 1) * step
                q = qs[rows, :] * keep
                d = ds[rows, :] * keep
                k = ks[:n, :]
                v = vs[:n, :]
                s = lax.dot_general(q, k, contract_last, preferred_element_type=jnp.float32)
                q_pos = i * step + lax.broadcasted_iota(jnp.int32, (step, 1), 0)
                limit = jnp.minimum(q_pos, length - 1)
                k_pos = lax.broadcasted_iota(jnp.int32, (step, n), 1)
                s = jnp.where(k_pos <= limit, s, -1e30)
                e = jnp.exp(s - jnp.max(s, axis=-1, keepdims=True))
                p = e * (1.0 / jnp.sum(e, axis=-1, keepdims=True))
                p_low = p.astype(jnp.bfloat16)
                dp = lax.dot_general(d, v, contract_last, preferred_element_type=jnp.float32)
                delta = jnp.sum(p * dp, axis=-1, keepdims=True)
                dsc = (p * (dp - delta)).astype(jnp.bfloat16)
                att_s[rows, :] += keep_f * jnp.dot(p_low, v, preferred_element_type=jnp.float32)
                dq_s[rows, :] += keep_f * jnp.dot(dsc, k, preferred_element_type=jnp.float32)
                dk_s[:n, :] += lax.dot_general(dsc, q, contract_first, preferred_element_type=jnp.float32)
                dv_s[:n, :] += lax.dot_general(p_low, d, contract_first, preferred_element_type=jnp.float32)
            return carry

        lax.fori_loop(0, 128 // HEAD_DIM, one_head, 0)
        for where_at, _, _, _, _, att_ref, dq_ref, dk_ref, dv_ref in sides:
            for j in range(per_side):
                at = pl.ds(pl.multiple_of(where_at[seq, j] * blk, blk), blk)
                here = slice(j * blk, (j + 1) * blk)
                att_ref[0, here, :] = att_s[at, :].astype(jnp.bfloat16)
                dq_ref[0, here, :] = unturn(dq_s[at, :] * scale, at).astype(jnp.bfloat16)
                dk_ref[0, here, :] = unturn(dk_s[at, :], at).astype(jnp.bfloat16)
                dv_ref[0, here, :] = dv_s[at, :].astype(jnp.bfloat16)

    def lanes(offset):
        return pl.BlockSpec((1, half_rows, 128), lambda s, p, *_: (base + s, 0, offset + p))

    table = pl.BlockSpec((seq_len, 128), lambda s, p, *_: (0, 0))
    side_in = [lanes(0), lanes(pairs), lanes(2 * pairs), lanes(0)]
    side_out = [lanes(0)] * 4
    narrow = jax.ShapeDtypeStruct((4, half_rows, heads_wide), jnp.bfloat16)
    work = seqs * pairs * 2 * seq_len * seq_len * 64
    result = pl.pallas_call(
        kernel,
        grid_spec=pltpu.PrefetchScalarGridSpec(
            num_scalar_prefetch=3,
            grid=(seqs, pairs),
            in_specs=[table] * 3 + side_in + side_in + [pl.BlockSpec(memory_space=pl.ANY)] * len(earlier),
            out_specs=side_out + side_out,
            scratch_shapes=[pltpu.VMEM((seq_len, 128), jnp.bfloat16)] * 4
            + [pltpu.VMEM((seq_len, 128), jnp.float32)] * 4,
        ),
        out_shape=[narrow] * 8,
        input_output_aliases={14 + i: i for i in range(len(earlier))},
        compiler_params=pltpu.CompilerParams(
            dimension_semantics=("arbitrary", "arbitrary"), vmem_limit_bytes=56 * 1024 * 1024
        ),
        cost_estimate=hint(
            flops=36 * work, transcendentals=work // 64, bytes_accessed=2 * 8 * seqs * seq_len * heads_wide
        ),
    )(deal_own, deal_oth, lengths, *tables, joined_own, joined_own, joined_own, datt_own,
      joined_oth, joined_oth, joined_oth, datt_oth, *earlier)
    return result


def flipped_out(core, shard, own, oth, start):
    lines, columns, rows, width = own.shape
    width = width // 4

    def kernel(where, own_ref, oth_ref, out_ref):
        side = pl.program_id(1)

        def write(ref):
            for line in range(lines):
                out_ref[:, line * rows : (line + 1) * rows] = ref[line, 0].astype(WIDE).T

        @pl.when(side == 0)
        def _():
            write(own_ref)

        @pl.when(side == 1)
        def _():
            write(oth_ref)

    source = pl.BlockSpec((lines, 1, rows, width), lambda b, s, where: (0, b, 0, start))
    target = pl.BlockSpec((width, lines * rows), lambda b, s, where: (where[0] ^ s, b))
    return pl.pallas_call(
        kernel,
        grid_spec=pltpu.PrefetchScalarGridSpec(
            num_scalar_prefetch=1, grid=(columns, 2), in_specs=[source, source], out_specs=target
        ),
        out_shape=jax.ShapeDtypeStruct((2 * width, lines * columns * rows), WIDE),
        compiler_params=pltpu.CompilerParams(dimension_semantics=("arbitrary",) * 2),
        cost_estimate=pl.CostEstimate(flops=0, transcendentals=0, bytes_accessed=3 * own.size),
    )(jnp.stack([core, shard]).astype(jnp.int32), own, oth)


def plane_body(
    tokens, cotangent, lengths, deal, ln_gain, ln_bias, w_qkv, b_qkv, w_out, b_out, w_up, b_up, w_down, b_down
):
    core = lax.axis_index("dp")
    place = lax.axis_index("ctx")
    shard = lax.axis_index("fsdp")
    spot = 2 * shard + core
    _, micro, rows, width = tokens.shape
    blocks = deal.shape[2]
    blk = rows * 4 // blocks
    units = w_down.shape[0] // 2
    head_cols = w_out.shape[0] // 2

    meta = jnp.concatenate([deal[0].reshape(-1), lengths[0] // 64, lengths[0] % 64]).astype(LOW)
    theirs = swap_dp(meta)
    meta = jnp.where(place // micro == core, meta, theirs)
    turn = place % micro
    meta = jnp.concatenate([
        lax.dynamic_slice_in_dim(meta, turn * blocks, blocks), lax.dynamic_slice_in_dim(meta, micro * blocks + turn, 1),
        lax.dynamic_slice_in_dim(meta, micro * (blocks + 1) + turn, 1),
    ])
    size = 2 * ln_gain.shape[0] + b_qkv.shape[0] + b_out.shape[0] + b_up.shape[0] + b_down.shape[0] + meta.shape[0]
    small = jnp.concatenate([ln_gain, ln_bias, b_qkv, b_out, b_up, b_down, meta, jnp.zeros((-size % 512,), LOW)])

    small = lax.all_gather(small, "fsdp", axis=0, tiled=False)
    bounds = [0]
    for piece in (ln_gain, ln_bias, b_qkv, b_out, b_up, b_down, meta):
        bounds.append(bounds[-1] + piece.shape[0])
    gain, shift, bias_qkv, bias_out, bias_up, bias_down, meta = (small[:, a:b] for a, b in zip(bounds[:-1], bounds[1:]))
    gain, shift = gain.astype(WIDE).reshape(-1), shift.astype(WIDE).reshape(-1)
    own_blocks = lax.dynamic_slice_in_dim(deal[0], 2 * place, 2, axis=1)
    local_pos = (own_blocks[:, :, None] * blk + jnp.arange(blk, dtype=jnp.int32)).reshape(micro, rows)
    valid = (local_pos < lengths[0][:, None])[:, :, None]
    inputs = tokens[0].astype(WIDE)
    centered = inputs - jnp.mean(inputs, axis=-1, keepdims=True)
    inv_std = lax.rsqrt(jnp.mean(centered * centered, axis=-1, keepdims=True) + EPS)
    hidden_home = (centered * inv_std * gain + shift).astype(LOW)
    gout_home = jnp.where(valid, cotangent[0], jnp.zeros((), LOW))

    h_received = for_other(after(hidden_home, small), core, blk)
    up_sent = columns_sent([after(piece, small) for piece in columns_cut(w_up, 1, core, shard)])
    g_received = for_other(after(gout_home, h_received), core, blk)
    h_dealt = deal_out(hidden_home, h_received, core, blk)
    hidden_own = lax.all_gather(after(h_dealt, *[piece for _, _, piece in up_sent]), "fsdp", axis=0, tiled=True)
    hidden = (hidden_own, swap_dp(hidden_own))
    up_w = placed(up_sent, shard, w_up.shape[0])
    g_dealt = deal_out(gout_home, after(g_received, h_dealt), core, blk)
    gout_own = lax.all_gather(g_dealt, "fsdp", axis=0, tiled=True)

    bias_ends = (bias_out.astype(WIDE) + bias_down.astype(WIDE)).reshape(-1)
    meta = meta.astype(jnp.int32)
    plane_len = meta[:, blocks] * 64 + meta[:, blocks + 1]
    plane_deal = meta[:, :blocks].reshape(4, 4, 2)
    deal_own = pick(plane_deal, core, 2)
    deal_oth = pick(plane_deal, 1 - core, 2)
    up_b = lax.dynamic_slice_in_dim(bias_up.reshape(-1), spot * units, units).astype(WIDE)
    qkv_b = pick(bias_qkv.reshape(3, 8, head_cols), spot, 1).reshape(-1).astype(WIDE)

    acts, slopes, dups, datts = [], [], [], []
    for h in hidden:
        act, slope = up_call(h, up_w, up_b)
        acts.append(act)
        slopes.append(slope)
    gout_own = after(gout_own, *acts)
    gout = (gout_own, swap_dp(gout_own))
    qkv_sent = columns_sent([after(piece, gout_own) for piece in columns_cut(w_qkv, 3, core, shard)])
    qkv_w = placed(qkv_sent, shard, w_qkv.shape[0])
    tables = rope_tables(8 * blk)
    down_w = lax.dynamic_slice_in_dim(w_down, core * units, units, 0)
    out_w = lax.dynamic_slice_in_dim(w_out, core * head_cols, head_cols, 0)

    def scatter(grad):
        return lax.psum_scatter(grad, "ctx", scatter_dimension=0, tiled=True)

    def gather(piece):
        return lax.all_gather(piece, "ctx", axis=0, tiled=True)

    def exchange(piece):
        return lax.all_to_all(piece[0], "fsdp", 0, 0, tiled=True)

    g_down = grad_call(acts, [gout])[0]
    t_down = gather(scatter(g_down))
    for g, slope in zip((after(gout[0], g_down), gout[1]), slopes):
        dup, datt = down_back_call(g, slope, down_w, out_w)
        dups.append(dup)
        datts.append(datt)
    waited = [piece for bits, _, piece in qkv_sent if bits]
    g_up, s_up = grad_call((after(hidden[0], *dups, *waited), hidden[1]), [dups], sums=True, dealt=True)
    x_up = exchange(scatter(g_up))
    t_up = gather(x_up[None])
    joins = [join_call(after(h, g_up), qkv_w, qkv_b) for h in hidden]

    per_seq = (4, 4 * blk, -1)
    shaped = [piece.reshape(per_seq) for piece in (joins[0], joins[1], datts[0], datts[1])]
    sides = attention_call(deal_own, deal_oth, plane_len, *shaped, tables, blk, 0, 4)
    sides = [piece.reshape(16 * blk, -1) for piece in sides]
    atts = [sides[0], sides[4]]
    turned = [sides[1:4], sides[5:8]]

    g_out = grad_call(atts, [gout], dealt=True, flip=True)[0]
    g_qkv, s_q, s_k, s_v = grad_call(
        (after(hidden[0], g_out), hidden[1]), [(turned[0][i], turned[1][i]) for i in range(3)], sums=True, dealt=True
    )
    mine = scatter(jnp.concatenate([g_qkv, g_out], axis=3))[0]
    qkv_cols = g_qkv.shape[3]
    x_qkv = lax.all_to_all(mine[:, :, :qkv_cols], "fsdp", 0, 0, tiled=True)
    t_mix = gather(jnp.concatenate([x_qkv, mine[:, :, qkv_cols:]], axis=2)[None])
    sums_tp = line_sum(jnp.concatenate([s_up, s_q, s_k, s_v], axis=1), place)
    tails = lax.all_gather(sums_tp, ("fsdp", "dp"), axis=0, tiled=True)
    b_oth = backward_call(dups[1], after(turned[1], g_qkv, x_up), up_w, qkv_w)
    f_oth = forward_call(after(acts[1], b_oth, t_down), atts[1], down_w, out_w)
    b_total = backward_call(after(dups[0], f_oth), turned[0], up_w, qkv_w, swap_dp(b_oth))
    f_total = forward_call(after(acts[0], b_total), atts[0], down_w, out_w, swap_dp(f_oth))
    d_hidden = collect(b_total, shard, f_total)
    mixed = collect(f_total, shard)
    d_hidden = to_home(after(d_hidden, x_qkv), core, place, blk)
    t_up = after(t_up, f_total, x_qkv)
    o_up = cols_out(core, shard, t_up, after(swap_dp(t_up), tails), 1, 1)
    o_down = rows_out(core, shard, t_down, after(swap_dp(t_down), o_up))
    d_hidden = after(d_hidden, o_down).astype(WIDE)
    mixed = to_home(mixed, core, place, blk)
    t_mix = after(t_mix, o_down)
    t_mix = (t_mix, swap_dp(t_mix))
    o_qkv = cols_out(core, shard, *t_mix, 3, 4)
    o_out = flipped_out(core, shard, *t_mix, 3)

    inputs = after(tokens[0], f_total).astype(WIDE)
    centered = inputs - jnp.mean(inputs, axis=-1, keepdims=True)
    inv_std = lax.rsqrt(jnp.mean(centered * centered, axis=-1, keepdims=True) + EPS)
    normed = centered * inv_std
    d_norm = d_hidden * gain
    d_inputs = inv_std * (
        d_norm
        - jnp.mean(d_norm, axis=-1, keepdims=True)
        - normed * jnp.mean(d_norm * normed, axis=-1, keepdims=True)
    )
    back = (gout_home.astype(WIDE) + d_inputs).astype(LOW)

    mixed = after(mixed, o_qkv, o_out)
    result = jnp.where(valid, inputs + mixed.astype(WIDE) + bias_ends, 0.0).astype(LOW)
    d_bup = lax.dynamic_slice(tails, (2 * shard, 0), (2, units)).reshape(-1)
    d_bqkv = tails[:, units:].reshape(8, 3, head_cols).transpose(1, 0, 2).reshape(-1)
    d_bqkv = lax.dynamic_slice_in_dim(d_bqkv, shard * b_qkv.shape[0], b_qkv.shape[0])
    sums = jnp.stack([
        jnp.sum(d_hidden * normed, axis=(0, 1)), jnp.sum(d_hidden, axis=(0, 1)), jnp.sum(gout_home.astype(WIDE), axis=(0, 1)),
    ])
    sums = every_sum(sums, place)
    sums = lax.dynamic_slice_in_dim(sums, shard * ln_gain.shape[0], ln_gain.shape[0], 1)

    return result[None], back[None], sums[0], sums[1], o_qkv, d_bqkv, o_out, sums[2], o_up, d_bup, o_down, sums[2]


def plane_fits(mesh, shapes):
    tokens, _, _, deal = shapes[:4]
    sizes = dict(mesh.shape)
    dp, ctx, fsdp = sizes["dp"], sizes["ctx"], sizes["fsdp"]
    micro, seq_len, width = tokens.shape[1:]
    blocks = deal.shape[2]
    heads = width // HEAD_DIM
    return (
        dp == 2
        and dp * micro == ctx == fsdp == 4
        and tokens.shape[0] == dp * fsdp
        and blocks == dp * ctx
        and heads % (2 * dp * fsdp) == 0
        and seq_len % 256 == 0
        and (seq_len // blocks) % 128 == 0
    )


def solution(mesh):
    in_specs = (
        P(("dp", "fsdp"), None, "ctx", None),
        P(("dp", "fsdp"), None, "ctx", None),
        P(("dp", "fsdp"), None),
        P(("dp", "fsdp"), None, None),
        P("fsdp"),
        P("fsdp"),
        P("fsdp", None),
        P("fsdp"),
        P("fsdp", None),
        P("fsdp"),
        P("fsdp", None),
        P("fsdp"),
        P("fsdp", None),
        P("fsdp"),
    )
    out_specs = (
        P(("dp", "fsdp"), None, "ctx", None),
        P(("dp", "fsdp"), None, "ctx", None),
        P("fsdp"),
        P("fsdp"),
        P("fsdp", None),
        P("fsdp"),
        P("fsdp", None),
        P("fsdp"),
        P("fsdp", None),
        P("fsdp"),
        P("fsdp", None),
        P("fsdp"),
    )

    def program(*arrays):
        body = plane_body if plane_fits(mesh, arrays) else gathered_body
        return jax.shard_map(body, mesh=mesh, in_specs=in_specs, out_specs=out_specs, check_vma=False)(*arrays)

    return program
```

```python
import jax
import jax.numpy as jnp
from jax import lax
from jax.experimental import pallas as pl
from jax.experimental.pallas import tpu as pltpu
from jax.sharding import PartitionSpec as P

HEAD_DIM = 64
ROT = 32


EPS = 1e-05
BASE = 10000.0


def contract_rows(left, right):
    return lax.dot_general(
        left, right, (((0,), (0,)), ((), ())), preferred_element_type=jnp.float32
    )


def contract_cols(left, right):
    return lax.dot_general(
        left, right, (((1,), (1,)), ((), ())), preferred_element_type=jnp.float32
    )


def angles_of(positions):
    half = ROT // 2
    freqs = BASE ** (-(jnp.arange(half, dtype=jnp.float32) * 2.0) / ROT)
    angles = positions.astype(jnp.float32)[:, None] * freqs[None, :]
    return (jnp.cos(angles)[:, None, :], jnp.sin(angles)[:, None, :])


def rotate(values, cosine, sine):
    half = ROT // 2
    first = values[..., :half]
    second = values[..., half:ROT]
    return jnp.concatenate(
        [first * cosine - second * sine, second * cosine + first * sine, values[..., ROT:]], axis=-1
    )


def rotate_back(values, cosine, sine):
    half = ROT // 2
    first = values[..., :half]
    second = values[..., half:ROT]
    return jnp.concatenate(
        [first * cosine + second * sine, second * cosine - first * sine, values[..., ROT:]], axis=-1
    )


def layer_step(weights, inputs, upstream, length, deal_row):
    gain, shift, w_qkv, b_qkv, w_out, b_out, w_up, b_up, w_down, b_down = weights
    row_count, width = inputs.shape
    block_rows = row_count // 2
    head_count = width // HEAD_DIM
    scale = HEAD_DIM ** (-0.5)
    place = lax.axis_index("ctx")
    offsets = jnp.arange(block_rows, dtype=jnp.int32)
    own_blocks = lax.dynamic_slice_in_dim(deal_row, 2 * place, 2)
    local_pos = (own_blocks[:, None] * block_rows + offsets[None, :]).reshape(row_count)
    every_pos = (deal_row[:, None] * block_rows + offsets[None, :]).reshape(-1)
    valid = (local_pos < length).astype(jnp.float32)[:, None]
    allowed = (every_pos[None, :] <= local_pos[:, None]) & (every_pos[None, :] < length)
    cosine, sine = angles_of(local_pos)
    inputs_f = inputs.astype(jnp.float32)
    gain_f = gain.astype(jnp.float32)
    centered = inputs_f - jnp.mean(inputs_f, axis=-1, keepdims=True)
    variance = jnp.mean(centered * centered, axis=-1, keepdims=True)
    inv_std = lax.rsqrt(variance + EPS)
    normed = centered * inv_std
    hidden = (normed * gain_f + shift.astype(jnp.float32)).astype(jnp.bfloat16)
    joined = jnp.dot(hidden, w_qkv, preferred_element_type=jnp.float32) + b_qkv.astype(jnp.float32)
    query = (
        rotate(joined[:, :width].reshape(row_count, head_count, HEAD_DIM), cosine, sine)
        .reshape(row_count, width)
        .astype(jnp.bfloat16)
    )
    keyed = (
        rotate(joined[:, width : 2 * width].reshape(row_count, head_count, HEAD_DIM), cosine, sine)
        .reshape(row_count, width)
        .astype(jnp.bfloat16)
    )
    valued = joined[:, 2 * width :].astype(jnp.bfloat16)
    keys_all, values_all = (
        lax.all_gather(keyed, "ctx", axis=0, tiled=True),
        lax.all_gather(valued, "ctx", axis=0, tiled=True),
    )
    total_keys = keys_all.shape[0]
    group = min(8, head_count)
    span = group * HEAD_DIM

    def heads_of(array, start, count):
        return array[:, start : start + span].reshape(count, group, HEAD_DIM)

    def block_scores(start):
        raw = (
            jnp.einsum(
                "qhd,khd->hqk",
                heads_of(query, start, row_count),
                heads_of(keys_all, start, total_keys),
                preferred_element_type=jnp.float32,
            )
            * scale
        )
        return jnp.where(allowed[None], raw, -1e30)

    attended_parts = []
    lse_parts = []
    for start in range(0, width, span):
        masked = block_scores(start)
        highest = jnp.max(masked, axis=-1, keepdims=True)
        expo = jnp.exp(masked - highest)
        total = jnp.sum(expo, axis=-1, keepdims=True)
        weights_low = (expo / total).astype(jnp.bfloat16)
        mixed = jnp.einsum(
            "hqk,khd->qhd",
            weights_low,
            heads_of(values_all, start, total_keys),
            preferred_element_type=jnp.float32,
        )
        attended_parts.append(mixed.reshape(row_count, span))
        lse_parts.append(highest + jnp.log(total))
    attended = jnp.concatenate(attended_parts, axis=1).astype(jnp.bfloat16)
    branch = jnp.dot(attended, w_out, preferred_element_type=jnp.float32) + b_out.astype(
        jnp.float32
    )
    upward = jnp.dot(hidden, w_up, preferred_element_type=jnp.float32) + b_up.astype(jnp.float32)
    activated = jax.nn.gelu(upward, approximate=True).astype(jnp.bfloat16)
    feed = jnp.dot(activated, w_down, preferred_element_type=jnp.float32) + b_down.astype(
        jnp.float32
    )
    result = (valid * (inputs_f + branch + feed)).astype(jnp.bfloat16)
    grad_out = upstream.astype(jnp.float32) * valid
    grad_low = grad_out.astype(jnp.bfloat16)
    row_total = jnp.sum(grad_out, axis=0)
    d_down = contract_rows(activated, grad_low)
    d_wout = contract_rows(attended, grad_low)
    d_act = contract_cols(grad_low, w_down)
    _, gelu_pull = jax.vjp(lambda value: jax.nn.gelu(value, approximate=True), upward)
    d_upward = gelu_pull(d_act)[0].astype(jnp.bfloat16)
    d_wup = contract_rows(hidden, d_upward)
    d_bup = jnp.sum(d_upward.astype(jnp.float32), axis=0)
    d_attended = contract_cols(grad_low, w_out).astype(jnp.bfloat16)
    dq_parts = []
    dk_parts = []
    dv_parts = []
    delta_parts = []
    for index, start in enumerate(range(0, width, span)):
        masked = block_scores(start)
        probs = jnp.where(allowed[None], jnp.exp(masked - lse_parts[index]), 0.0)
        d_heads = heads_of(d_attended, start, row_count)
        d_probs = jnp.einsum(
            "qhd,khd->hqk",
            d_heads,
            heads_of(values_all, start, total_keys),
            preferred_element_type=jnp.float32,
        )
        delta = jnp.sum(probs * d_probs, axis=-1, keepdims=True)
        d_scores = (probs * (d_probs - delta)).astype(jnp.bfloat16)
        d_query = (
            jnp.einsum(
                "hqk,khd->qhd",
                d_scores,
                heads_of(keys_all, start, total_keys),
                preferred_element_type=jnp.float32,
            )
            * scale
        )
        dq_parts.append(d_query.reshape(row_count, span))
        delta_parts.append(delta[:, :, 0].T)
        d_keyed = (
            jnp.einsum(
                "hqk,qhd->khd",
                d_scores,
                heads_of(query, start, row_count),
                preferred_element_type=jnp.float32,
            )
            * scale
        )
        d_valued = jnp.einsum(
            "hqk,qhd->khd", probs.astype(jnp.bfloat16), d_heads, preferred_element_type=jnp.float32
        )
        dk_parts.append(d_keyed.reshape(total_keys, span))
        dv_parts.append(d_valued.reshape(total_keys, span))
    keys_grad_all = jnp.concatenate(dk_parts, axis=1)
    values_grad_all = jnp.concatenate(dv_parts, axis=1)
    keys_grad, values_grad = (
        lax.psum_scatter(
            keys_grad_all.astype(jnp.bfloat16), "ctx", scatter_dimension=0, tiled=True
        ).astype(jnp.float32),
        lax.psum_scatter(
            values_grad_all.astype(jnp.bfloat16), "ctx", scatter_dimension=0, tiled=True
        ).astype(jnp.float32),
    )
    query_grad = rotate_back(
        jnp.concatenate(dq_parts, axis=1).reshape(row_count, head_count, HEAD_DIM), cosine, sine
    ).reshape(row_count, width)
    keyed_grad = rotate_back(
        keys_grad.reshape(row_count, head_count, HEAD_DIM), cosine, sine
    ).reshape(row_count, width)
    d_joined = jnp.concatenate([query_grad, keyed_grad, values_grad], axis=1).astype(jnp.bfloat16)
    d_wqkv = contract_rows(hidden, d_joined)
    d_bqkv = jnp.sum(d_joined.astype(jnp.float32), axis=0)
    d_hidden = contract_cols(d_joined, w_qkv) + contract_cols(d_upward, w_up)
    d_gain = jnp.sum(d_hidden * normed, axis=0)
    d_shift = jnp.sum(d_hidden, axis=0)
    d_norm = d_hidden * gain_f
    d_inputs = inv_std * (
        d_norm
        - jnp.mean(d_norm, axis=-1, keepdims=True)
        - normed * jnp.mean(d_norm * normed, axis=-1, keepdims=True)
    )
    back = (grad_out + d_inputs).astype(jnp.bfloat16)
    return (
        result,
        back,
        (d_gain, d_shift, d_wqkv, d_bqkv, d_wout, row_total, d_wup, d_bup, d_down, row_total),
    )


def gathered_body(
    tokens,
    cotangent,
    lengths,
    deal,
    ln_gain,
    ln_bias,
    w_qkv,
    b_qkv,
    w_out,
    b_out,
    w_up,
    b_up,
    w_down,
    b_down,
):
    shards = (ln_gain, ln_bias, w_qkv, b_qkv, w_out, b_out, w_up, b_up, w_down, b_down)
    shard_count = lax.axis_size("fsdp")
    summed = tuple(
        (
            jnp.zeros((piece.shape[0] * shard_count,) + piece.shape[1:], jnp.float32)
            for piece in shards
        )
    )
    results = []
    backs = []
    for micro_index in range(tokens.shape[1]):
        gathered = (
            lax.all_gather(ln_gain, "fsdp", axis=0, tiled=True),
            lax.all_gather(ln_bias, "fsdp", axis=0, tiled=True),
            lax.all_gather(w_qkv, "fsdp", axis=0, tiled=True),
            lax.all_gather(b_qkv, "fsdp", axis=0, tiled=True),
            lax.all_gather(w_out, "fsdp", axis=0, tiled=True),
            lax.all_gather(b_out, "fsdp", axis=0, tiled=True),
            lax.all_gather(w_up, "fsdp", axis=0, tiled=True),
            lax.all_gather(b_up, "fsdp", axis=0, tiled=True),
            lax.all_gather(w_down, "fsdp", axis=0, tiled=True),
            lax.all_gather(b_down, "fsdp", axis=0, tiled=True),
        )
        result, back, local = layer_step(
            gathered,
            tokens[0, micro_index],
            cotangent[0, micro_index],
            lengths[0, micro_index],
            deal[0, micro_index],
        )
        results.append(result)
        backs.append(back)
        summed = tuple((older + newer for older, newer in zip(summed, local)))
    summed = (
        lax.psum_scatter(
            summed[0].astype(jnp.bfloat16), "fsdp", scatter_dimension=0, tiled=True
        ).astype(jnp.float32),
        lax.psum_scatter(
            summed[1].astype(jnp.bfloat16), "fsdp", scatter_dimension=0, tiled=True
        ).astype(jnp.float32),
        lax.psum_scatter(
            summed[2].astype(jnp.bfloat16), "fsdp", scatter_dimension=0, tiled=True
        ).astype(jnp.float32),
        lax.psum_scatter(
            summed[3].astype(jnp.bfloat16), "fsdp", scatter_dimension=0, tiled=True
        ).astype(jnp.float32),
        lax.psum_scatter(
            summed[4].astype(jnp.bfloat16), "fsdp", scatter_dimension=0, tiled=True
        ).astype(jnp.float32),
        lax.psum_scatter(
            summed[5].astype(jnp.bfloat16), "fsdp", scatter_dimension=0, tiled=True
        ).astype(jnp.float32),
        lax.psum_scatter(
            summed[6].astype(jnp.bfloat16), "fsdp", scatter_dimension=0, tiled=True
        ).astype(jnp.float32),
        lax.psum_scatter(
            summed[7].astype(jnp.bfloat16), "fsdp", scatter_dimension=0, tiled=True
        ).astype(jnp.float32),
        lax.psum_scatter(
            summed[8].astype(jnp.bfloat16), "fsdp", scatter_dimension=0, tiled=True
        ).astype(jnp.float32),
        lax.psum_scatter(
            summed[9].astype(jnp.bfloat16), "fsdp", scatter_dimension=0, tiled=True
        ).astype(jnp.float32),
    )
    totals = (
        lax.psum(summed[0].astype(jnp.bfloat16), ("dp", "ctx")).astype(jnp.float32),
        lax.psum(summed[1].astype(jnp.bfloat16), ("dp", "ctx")).astype(jnp.float32),
        lax.psum(summed[2].astype(jnp.bfloat16), ("dp", "ctx")).astype(jnp.float32),
        lax.psum(summed[3].astype(jnp.bfloat16), ("dp", "ctx")).astype(jnp.float32),
        lax.psum(summed[4].astype(jnp.bfloat16), ("dp", "ctx")).astype(jnp.float32),
        lax.psum(summed[5].astype(jnp.bfloat16), ("dp", "ctx")).astype(jnp.float32),
        lax.psum(summed[6].astype(jnp.bfloat16), ("dp", "ctx")).astype(jnp.float32),
        lax.psum(summed[7].astype(jnp.bfloat16), ("dp", "ctx")).astype(jnp.float32),
        lax.psum(summed[8].astype(jnp.bfloat16), ("dp", "ctx")).astype(jnp.float32),
        lax.psum(summed[9].astype(jnp.bfloat16), ("dp", "ctx")).astype(jnp.float32),
    )
    stacked_out = jnp.stack(results)[None]
    stacked_back = jnp.stack(backs)[None]
    return (
        stacked_out,
        stacked_back,
        totals[0],
        totals[1],
        totals[2],
        totals[3],
        totals[4],
        totals[5],
        totals[6],
        totals[7],
        totals[8],
        totals[9],
    )


SWAP = [(0, 1), (1, 0)]
LOW = jnp.bfloat16
SLOW = 1.8
WIDE = jnp.float32


def hint(flops, transcendentals, bytes_accessed):
    return pl.CostEstimate(
        flops=int(flops * SLOW), transcendentals=transcendentals, bytes_accessed=bytes_accessed
    )


def after(value, *others):
    return lax.optimization_barrier((value,) + others)[0]


def swap_dp(value):
    return lax.ppermute(value, "dp", SWAP)


def swap_shard(value, bits):
    return lax.ppermute(value, "fsdp", [(i, i ^ bits) for i in range(4)])


def shift_ctx(value, steps):
    return lax.ppermute(value, "ctx", [(i, (i + steps) % 4) for i in range(4)])


def pick(array, index, axis):
    return lax.dynamic_index_in_dim(array, index, axis, keepdims=False)


def by_core(core, mine, other, axis):
    first = jnp.where(core == 0, mine, other)
    second = jnp.where(core == 0, other, mine)
    return jnp.stack([first, second], axis=axis)


def for_other(rows, core, blk):
    micro, _, width = rows.shape
    return swap_dp(pick(rows.reshape(micro, 2, blk, width), 1 - core, 1))


def line_up(rows, received, core, blk):
    micro, _, width = rows.shape
    return by_core(core, pick(rows.reshape(micro, 2, blk, width), core, 1), received, 0).reshape(4, blk, width)


def deal_out(lined):
    return lax.all_to_all(lined, "ctx", 0, 0, tiled=True).reshape(-1, lined.shape[2])


def normed_rows(rows):
    inputs = rows.astype(WIDE)
    centered = inputs - jnp.mean(inputs, axis=-1, keepdims=True)
    inv_std = lax.rsqrt(jnp.mean(centered * centered, axis=-1, keepdims=True) + EPS)
    return inputs, centered * inv_std, inv_std


def placed(pieces, shard, size, *gates):
    whole = after(jnp.zeros((4 * size, pieces[0][2].shape[1]), LOW), *gates)
    for bits, start, piece in pieces:
        whole = lax.dynamic_update_slice(whole, piece, ((shard ^ bits) * size + start, 0))
    return whole


def plus(first, *others):
    total = first.astype(WIDE)
    for other in others:
        total = total + other.astype(WIDE)
    return total.astype(LOW)


def collect(total, shard, *gates):
    size = total.shape[0] // 4
    half = size // 2

    def part(bits, which):
        return lax.dynamic_slice_in_dim(total, (shard ^ bits) * size + which * half, half, 0)

    via_x, via_y = swap_shard(part(3, 0), 1), swap_shard(part(3, 1), 2)
    x_top, y_end = swap_shard(part(1, 0), 1), swap_shard(part(2, 1), 2)
    y_top = swap_shard(plus(part(2, 0), after(via_x, *gates)), 2)
    x_end = swap_shard(plus(part(1, 1), after(via_y, *gates)), 1)
    return jnp.concatenate([plus(part(0, 0), x_top, y_top), plus(part(0, 1), x_end, y_end)])


def to_home(mine, core, place, blk):
    width = mine.shape[1]
    lined = lax.all_to_all(mine.reshape(4, blk, width), "ctx", 0, 0, tiled=True).reshape(2, 2, blk, width)
    kept = pick(lined, core, 0)
    received = swap_dp(pick(lined, 1 - core, 0))
    return by_core(core, kept, received, 1).reshape(2, 2 * blk, width)


def columns_cut(weight, parts, core, shard):
    width = weight.shape[1] // (parts * 8)
    pieces = []
    for bits in range(4):
        spot = 2 * (shard ^ bits) + core
        pieces.append(jnp.concatenate(
            [lax.dynamic_slice_in_dim(weight, (t * 8 + spot) * width, width, 1) for t in range(parts)], axis=1
        ))
    return pieces


def columns_sent(pieces):
    return [(bits, 0, piece if bits == 0 else swap_shard(piece, bits)) for bits, piece in enumerate(pieces)]


def inward(value):
    return lax.ppermute(value, "ctx", [(0, 1), (3, 2)])


def across(value):
    return lax.ppermute(value, "ctx", [(1, 2), (2, 1)])


def outward(value):
    return lax.ppermute(value, "ctx", [(1, 0), (2, 3)])


def line_sum(value, place):
    half = value + inward(value)
    whole = half + across(half)
    return line_end(whole, outward(whole), place)


def line_end(whole, received, place):
    return jnp.where((place == 1) | (place == 2), whole, received)


def every_sum(value, place):
    value = value + swap_dp(value)
    value = value + swap_shard(value, 1)
    value = value + swap_shard(value, 2)
    return line_sum(value, place)


def lay_out(core, shard, own, oth, out_shape, grid, block, in_at, out_at):
    def kernel(where, own_ref, oth_ref, out_ref):
        side = pl.program_id(len(grid))

        @pl.when(side == 0)
        def _():
            out_ref[...] = own_ref[...].astype(WIDE)

        @pl.when(side == 1)
        def _():
            out_ref[...] = oth_ref[...].astype(WIDE)

    source = pl.BlockSpec(block, lambda *args: in_at(*args[: len(grid)]))
    target = pl.BlockSpec(block, lambda *args: out_at(*args[:-1], args[-1][0], args[-1][1]))
    count = out_shape[0] * out_shape[1]
    return pl.pallas_call(
        kernel,
        grid_spec=pltpu.PrefetchScalarGridSpec(
            num_scalar_prefetch=1, grid=grid + (2,), in_specs=[source, source], out_specs=target
        ),
        out_shape=jax.ShapeDtypeStruct(out_shape, WIDE),
        compiler_params=pltpu.CompilerParams(dimension_semantics=("arbitrary",) * (len(grid) + 1)),
        cost_estimate=hint(flops=0, transcendentals=0, bytes_accessed=6 * count),
    )(jnp.stack([core, shard]).astype(jnp.int32), own, oth)


def rows_out(core, shard, own, oth):
    rows, width = own.shape
    tile = min(256, rows)
    steps = rows // tile
    return lay_out(
        core, shard, own, oth, (2 * rows, width), (steps,), (tile, width),
        lambda i: (i, 0), lambda i, s, c, f: ((c ^ s) * steps + i, 0),
    )


def cols_half(core, shard, half, side, parts, held, earlier=()):
    lines, columns, rows, width = half.shape
    width = width // held

    def kernel(where, half_ref, *rest):
        rest[-1][...] = half_ref[...].reshape(lines * rows, width).astype(WIDE)

    return pl.pallas_call(
        kernel,
        grid_spec=pltpu.PrefetchScalarGridSpec(
            num_scalar_prefetch=1,
            grid=(columns, parts),
            in_specs=[pl.BlockSpec((lines, 1, rows, width), lambda b, t, where: (0, b, 0, t))]
            + [pl.BlockSpec(memory_space=pl.ANY)] * len(earlier),
            out_specs=pl.BlockSpec((lines * rows, width), lambda b, t, where: (0, t * 8 + 2 * b + (where[0] ^ side))),
        ),
        out_shape=jax.ShapeDtypeStruct((lines * rows, 2 * columns * parts * width), WIDE),
        input_output_aliases={2: 0} if earlier else {},
        compiler_params=pltpu.CompilerParams(dimension_semantics=("arbitrary",) * 2),
        cost_estimate=pl.CostEstimate(flops=0, transcendentals=0, bytes_accessed=6 * half.size),
    )(jnp.stack([core, shard]).astype(jnp.int32), half, *earlier)


def cols_out(core, shard, own, oth, parts, held):
    first = cols_half(core, shard, own, 0, parts, held)
    return cols_half(core, shard, oth, 1, parts, held, (first,))


GELU_C = 0.7978845608028654
GELU_A = 0.044715


def gelu_pair(value):
    square = value * value
    tanh = jnp.tanh(GELU_C * value * (1.0 + GELU_A * square))
    half = 0.5 * (1.0 + tanh)
    slope = half + 0.5 * value * (1.0 - tanh * tanh) * (GELU_C * (1.0 + 3.0 * GELU_A * square))
    return value * half, slope


ROWS_OF = (((0,), (0,)), ((), ()))
COLS_OF = (((1,), (1,)), ((), ()))
ROOM = 56 * 1024 * 1024


def row_call(body, tiled, whole, widths, flops, tile=512):
    count = tiled[0].shape[0]

    def rows_spec(width):
        return pl.BlockSpec((tile, width), lambda i: (i, 0))

    moved = sum(a.size * a.dtype.itemsize for a in (*tiled, *whole)) + 2 * count * sum(widths)
    return pl.pallas_call(
        body,
        grid=(count // tile,),
        in_specs=[rows_spec(a.shape[1]) for a in tiled]
        + [pl.BlockSpec(a.shape, lambda i: (0, 0), pipeline_mode=pl.Buffered(1)) for a in whole],
        out_specs=[rows_spec(width) for width in widths],
        out_shape=[jax.ShapeDtypeStruct((count, width), LOW) for width in widths],
        compiler_params=pltpu.CompilerParams(dimension_semantics=("arbitrary",), vmem_limit_bytes=ROOM),
        cost_estimate=hint(flops=flops, transcendentals=0, bytes_accessed=moved),
    )(*tiled, *whole)


def strips(width):
    step = min(256, width)
    return [slice(at, at + step) for at in range(0, width, step)]


def up_call(rows, weight, bias):
    def body(rows_ref, weight_ref, bias_ref, act_ref, slope_ref):
        for at in strips(weight.shape[1]):
            total = jnp.dot(rows_ref[...], weight_ref[:, at], preferred_element_type=WIDE) + bias_ref[:, at]
            act, slope = gelu_pair(total)
            act_ref[:, at] = act.astype(LOW)
            slope_ref[:, at] = slope.astype(LOW)

    width = weight.shape[1]
    return row_call(body, [rows], [weight, bias[None]], [width, width], 2 * rows.shape[0] * weight.size)


def join_call(rows, weight, bias):
    def body(rows_ref, weight_ref, bias_ref, out_ref):
        for at in strips(weight.shape[1]):
            total = jnp.dot(rows_ref[...], weight_ref[:, at], preferred_element_type=WIDE)
            out_ref[:, at] = (total + bias_ref[:, at]).astype(LOW)

    return row_call(body, [rows], [weight, bias[None]], [weight.shape[1]], 2 * rows.shape[0] * weight.size)[0]


def down_back_call(rows, slopes, down_w, out_w):
    def body(rows_ref, slope_ref, down_ref, out_w_ref, dup_ref, datt_ref):
        for at in strips(down_w.shape[0]):
            total = lax.dot_general(rows_ref[...], down_ref[at, :], COLS_OF, preferred_element_type=WIDE)
            dup_ref[:, at] = (total * slope_ref[:, at].astype(WIDE)).astype(LOW)
        total = lax.dot_general(rows_ref[...], out_w_ref[...], COLS_OF, preferred_element_type=WIDE)
        datt_ref[...] = total.astype(LOW)

    flops = 2 * rows.shape[0] * (down_w.size + out_w.size)
    return row_call(body, [rows, slopes], [down_w, out_w], [down_w.shape[0], out_w.shape[0]], flops)


def forward_call(act, att, down_w, out_w, added=None):
    def body(*refs):
        act_ref, att_ref = refs[:2]
        down_ref, out_w_ref, out_ref = refs[-3:]
        for at in strips(down_w.shape[1]):
            total = jnp.dot(act_ref[...], down_ref[:, at], preferred_element_type=WIDE)
            total = total + jnp.dot(att_ref[...], out_w_ref[:, at], preferred_element_type=WIDE)
            if added is not None:
                total = total + refs[2][:, at].astype(WIDE)
            out_ref[:, at] = total.astype(LOW)

    tiled = [act, att] + ([] if added is None else [added])
    flops = 2 * act.shape[0] * (down_w.size + out_w.size)
    return row_call(body, tiled, [down_w, out_w], [down_w.shape[1]], flops)[0]


def backward_call(dup, turned, up_w, qkv_w, added=None):
    wide = turned[0].shape[1]

    def body(*refs):
        dup_ref, turned_refs = refs[0], refs[1:4]
        up_ref, qkv_ref, out_ref = refs[-3:]
        for at in strips(up_w.shape[0]):
            total = lax.dot_general(dup_ref[...], up_ref[at, :], COLS_OF, preferred_element_type=WIDE)
            for i, ref in enumerate(turned_refs):
                part = qkv_ref[at, i * wide : (i + 1) * wide]
                total = total + lax.dot_general(ref[...], part, COLS_OF, preferred_element_type=WIDE)
            if added is not None:
                total = total + refs[4][:, at].astype(WIDE)
            out_ref[:, at] = total.astype(LOW)

    tiled = [dup, *turned] + ([] if added is None else [added])
    flops = 2 * dup.shape[0] * (up_w.size + qkv_w.size)
    return row_call(body, tiled, [up_w, qkv_w], [up_w.shape[0]], flops)[0]


def grad_call(left, rights, left_part=(0, 1), right_part=(0, 1), sums=False, dealt=False, flip=False, tile=512):
    steps = left[0].shape[0] // tile
    left_cols = left[0].shape[1] // left_part[1]
    right_cols = [pair[0].shape[1] // right_part[1] for pair in rights]
    count = len(rights)
    piece = (right_cols[0] if flip else left_cols) // 16
    made = 1 if dealt else count

    def body(*refs):
        ins, outs = refs[: 2 + 2 * count], refs[2 + 2 * count :]
        grads, totals, accs = outs[:made], outs[made : len(outs) - count], outs[len(outs) - count :]
        step = pl.program_id(0)

        @pl.when(step == 0)
        def _():
            for ref in (*accs, *totals):
                ref[...] = jnp.zeros_like(ref)

        def add(left_ref, right_refs):
            for i, ref in enumerate(right_refs):
                for at in strips(right_cols[i]):
                    accs[i][:, at] += lax.dot_general(
                        left_ref[...], ref[:, at], ROWS_OF, preferred_element_type=WIDE
                    )
                if sums:
                    totals[i][...] += jnp.sum(ref[...].astype(WIDE), axis=0, keepdims=True)

        @pl.when(step < steps)
        def _():
            add(ins[0], ins[2 : 2 + count])

        @pl.when(step >= steps)
        def _():
            add(ins[1], ins[2 + count :])

        @pl.when(step == 2 * steps - 1)
        def _():
            if not dealt:
                for grad, acc in zip(grads, accs):
                    grad[...] = acc[...].astype(LOW)
                return
            if flip:
                for spot in range(16):
                    part = accs[0][:, spot * piece : (spot + 1) * piece]
                    grads[0][spot % 4, spot // 4] = part.T.astype(LOW)
                return
            start = 0
            for acc, cols in zip(accs, right_cols):
                for column in range(4):
                    for line in range(4):
                        at = (4 * column + line) * piece
                        grads[0][line, column, :, start : start + cols] = acc[at : at + piece, :].astype(LOW)
                start += cols

    def side_spec(cols, part, side):
        def at(step):
            row = jnp.minimum(step, steps - 1) if side == 0 else jnp.maximum(step - steps, 0)
            return (row, part)

        return pl.BlockSpec((tile, cols), at)

    def fixed(shape):
        return pl.BlockSpec(shape, lambda step: (0,) * len(shape))

    specs = [side_spec(left_cols, left_part[0], side) for side in (0, 1)]
    specs += [side_spec(cols, right_part[0], side) for side in (0, 1) for cols in right_cols]
    shapes = [jax.ShapeDtypeStruct((left_cols, cols), LOW) for cols in right_cols]
    if dealt:
        shapes = [jax.ShapeDtypeStruct((4, 4, piece, left_cols if flip else sum(right_cols)), LOW)]
    if sums:
        shapes += [jax.ShapeDtypeStruct((1, cols), WIDE) for cols in right_cols]
    rows = 2 * left[0].shape[0]
    return pl.pallas_call(
        body,
        grid=(2 * steps,),
        in_specs=specs,
        out_specs=[fixed(shape.shape) for shape in shapes],
        out_shape=shapes,
        scratch_shapes=[pltpu.VMEM((left_cols, cols), WIDE) for cols in right_cols],
        compiler_params=pltpu.CompilerParams(dimension_semantics=("arbitrary",), vmem_limit_bytes=ROOM),
        cost_estimate=hint(
            flops=2 * rows * left_cols * sum(right_cols), transcendentals=0,
            bytes_accessed=2 * rows * (left_cols + sum(right_cols)),
        ),
    )(*left, *[pair[0] for pair in rights], *[pair[1] for pair in rights])


def rope_tables(seq_len):
    lane = jnp.arange(2 * HEAD_DIM, dtype=jnp.int32) % HEAD_DIM
    half = ROT // 2
    turned = lane < ROT
    index = jnp.where(turned, lane % half, 0).astype(jnp.float32)
    freqs = BASE ** (-(index * 2.0) / ROT)
    angles = jnp.arange(seq_len, dtype=jnp.float32)[:, None] * freqs[None, :]
    sine = jnp.sin(angles)
    cosine = jnp.where(turned[None], jnp.cos(angles), 1.0)
    up = jnp.where((lane < half)[None], -sine, 0.0)
    down = jnp.where(((lane >= half) & turned)[None], sine, 0.0)
    return cosine, up, down


def attention_call(deal_own, deal_oth, lengths, joined_own, joined_oth, datt_own, datt_oth, tables, blk, base, seqs, earlier=()):
    _, half_rows, wide = joined_own.shape
    heads_wide = wide // 3
    pairs = heads_wide // 128
    seq_len = 2 * half_rows
    per_side = half_rows // blk
    step = 256
    scale = HEAD_DIM ** (-0.5)
    half = ROT // 2
    contract_last = (((1,), (1,)), ((), ()))
    contract_first = (((0,), (0,)), ((), ()))

    def kernel(own_at, oth_at, len_at, cos_ref, up_ref, down_ref, q0, k0, v0, d0, q1, k1, v1, d1, *rest):
        att0, dq0, dk0, dv0, att1, dq1, dk1, dv1, qs, ks, vs, ds, att_s, dq_s, dk_s, dv_s = rest[len(earlier) :]
        seq = base + pl.program_id(0)
        length = len_at[seq]

        def turn(x, at):
            return (x * cos_ref[at, :] + pltpu.roll(x, 128 - half, 1) * up_ref[at, :]
                    + pltpu.roll(x, half, 1) * down_ref[at, :])

        def unturn(x, at):
            return (x * cos_ref[at, :] - pltpu.roll(x, 128 - half, 1) * up_ref[at, :]
                    - pltpu.roll(x, half, 1) * down_ref[at, :])

        sides = ((own_at, q0, k0, v0, d0, att0, dq0, dk0, dv0), (oth_at, q1, k1, v1, d1, att1, dq1, dk1, dv1))
        for where_at, q_ref, k_ref, v_ref, d_ref, *_ in sides:
            for j in range(per_side):
                at = pl.ds(pl.multiple_of(where_at[seq, j] * blk, blk), blk)
                here = slice(j * blk, (j + 1) * blk)
                qs[at, :] = (turn(q_ref[0, here, :].astype(jnp.float32), at)).astype(jnp.bfloat16) * jnp.bfloat16(scale)
                ks[at, :] = turn(k_ref[0, here, :].astype(jnp.float32), at).astype(jnp.bfloat16)
                vs[at, :] = v_ref[0, here, :]
                ds[at, :] = d_ref[0, here, :]
        att_s[...] = jnp.zeros_like(att_s)
        dq_s[...] = jnp.zeros_like(dq_s)
        dk_s[...] = jnp.zeros_like(dk_s)
        dv_s[...] = jnp.zeros_like(dv_s)
        lane = lax.broadcasted_iota(jnp.int32, (1, 128), 1)

        def one_head(h, carry):
            chosen = (lane // HEAD_DIM) == h
            keep_f = jnp.where(chosen, 1.0, 0.0)
            keep = keep_f.astype(jnp.bfloat16)
            for i in range(seq_len // step):
                rows = slice(i * step, (i + 1) * step)
                n = (i + 1) * step
                q = qs[rows, :] * keep
                d = ds[rows, :] * keep
                k = ks[:n, :]
                v = vs[:n, :]
                s = lax.dot_general(q, k, contract_last, preferred_element_type=jnp.float32)
                q_pos = i * step + lax.broadcasted_iota(jnp.int32, (step, 1), 0)
                limit = jnp.minimum(q_pos, length - 1)
                k_pos = lax.broadcasted_iota(jnp.int32, (step, n), 1)
                s = jnp.where(k_pos <= limit, s, -1e30)
                e = jnp.exp(s - jnp.max(s, axis=-1, keepdims=True))
                p = e * (1.0 / jnp.sum(e, axis=-1, keepdims=True))
                p_low = p.astype(jnp.bfloat16)
                dp = lax.dot_general(d, v, contract_last, preferred_element_type=jnp.float32)
                delta = jnp.sum(p * dp, axis=-1, keepdims=True)
                dsc = (p * (dp - delta)).astype(jnp.bfloat16)
                att_s[rows, :] += keep_f * jnp.dot(p_low, v, preferred_element_type=jnp.float32)
                dq_s[rows, :] += keep_f * jnp.dot(dsc, k, preferred_element_type=jnp.float32)
                dk_s[:n, :] += lax.dot_general(dsc, q, contract_first, preferred_element_type=jnp.float32)
                dv_s[:n, :] += lax.dot_general(p_low, d, contract_first, preferred_element_type=jnp.float32)
            return carry

        lax.fori_loop(0, 128 // HEAD_DIM, one_head, 0)
        for where_at, _, _, _, _, att_ref, dq_ref, dk_ref, dv_ref in sides:
            for j in range(per_side):
                at = pl.ds(pl.multiple_of(where_at[seq, j] * blk, blk), blk)
                here = slice(j * blk, (j + 1) * blk)
                att_ref[0, here, :] = att_s[at, :].astype(jnp.bfloat16)
                dq_ref[0, here, :] = unturn(dq_s[at, :] * scale, at).astype(jnp.bfloat16)
                dk_ref[0, here, :] = unturn(dk_s[at, :], at).astype(jnp.bfloat16)
                dv_ref[0, here, :] = dv_s[at, :].astype(jnp.bfloat16)

    def lanes(offset):
        return pl.BlockSpec((1, half_rows, 128), lambda s, p, *_: (base + s, 0, offset + p))

    table = pl.BlockSpec((seq_len, 128), lambda s, p, *_: (0, 0))
    side_in = [lanes(0), lanes(pairs), lanes(2 * pairs), lanes(0)]
    side_out = [lanes(0)] * 4
    narrow = jax.ShapeDtypeStruct((4, half_rows, heads_wide), jnp.bfloat16)
    work = seqs * pairs * 2 * seq_len * seq_len * 64
    result = pl.pallas_call(
        kernel,
        grid_spec=pltpu.PrefetchScalarGridSpec(
            num_scalar_prefetch=3,
            grid=(seqs, pairs),
            in_specs=[table] * 3 + side_in + side_in + [pl.BlockSpec(memory_space=pl.ANY)] * len(earlier),
            out_specs=side_out + side_out,
            scratch_shapes=[pltpu.VMEM((seq_len, 128), jnp.bfloat16)] * 4
            + [pltpu.VMEM((seq_len, 128), jnp.float32)] * 4,
        ),
        out_shape=[narrow] * 8,
        input_output_aliases={14 + i: i for i in range(len(earlier))},
        compiler_params=pltpu.CompilerParams(
            dimension_semantics=("arbitrary", "arbitrary"), vmem_limit_bytes=56 * 1024 * 1024
        ),
        cost_estimate=hint(
            flops=36 * work, transcendentals=work // 64, bytes_accessed=2 * 8 * seqs * seq_len * heads_wide
        ),
    )(deal_own, deal_oth, lengths, *tables, joined_own, joined_own, joined_own, datt_own,
      joined_oth, joined_oth, joined_oth, datt_oth, *earlier)
    return result


def flipped_out(core, shard, own, oth, start):
    lines, columns, rows, width = own.shape

    def kernel(where, own_ref, oth_ref, out_ref):
        side = pl.program_id(1)

        def write(ref):
            for line in range(lines):
                out_ref[:, line * rows : (line + 1) * rows] = ref[line, 0].astype(WIDE).T

        @pl.when(side == 0)
        def _():
            write(own_ref)

        @pl.when(side == 1)
        def _():
            write(oth_ref)

    source = pl.BlockSpec((lines, 1, rows, width), lambda b, s, where: (0, b, 0, start))
    target = pl.BlockSpec((width, lines * rows), lambda b, s, where: (where[0] ^ s, b))
    return pl.pallas_call(
        kernel,
        grid_spec=pltpu.PrefetchScalarGridSpec(
            num_scalar_prefetch=1, grid=(columns, 2), in_specs=[source, source], out_specs=target
        ),
        out_shape=jax.ShapeDtypeStruct((2 * width, lines * columns * rows), WIDE),
        compiler_params=pltpu.CompilerParams(dimension_semantics=("arbitrary",) * 2),
        cost_estimate=pl.CostEstimate(flops=0, transcendentals=0, bytes_accessed=3 * own.size),
    )(jnp.stack([core, shard]).astype(jnp.int32), own, oth)


def plane_body(
    tokens, cotangent, lengths, deal, ln_gain, ln_bias, w_qkv, b_qkv, w_out, b_out, w_up, b_up, w_down, b_down
):
    core = lax.axis_index("dp")
    place = lax.axis_index("ctx")
    shard = lax.axis_index("fsdp")
    spot = 2 * shard + core
    _, micro, rows, width = tokens.shape
    blocks = deal.shape[2]
    blk = rows * 4 // blocks
    units = w_down.shape[0] // 2
    head_cols = w_out.shape[0] // 2

    h_received = for_other(tokens[0], core, blk)
    norm = lax.all_gather(jnp.stack([ln_gain, ln_bias]), "fsdp", axis=1, tiled=True).astype(WIDE)
    gain, shift = norm[0], norm[1]
    _, hidden_home, _ = normed_rows(line_up(tokens[0], h_received, core, blk))
    hidden_home = (hidden_home * gain + shift).astype(LOW)
    meta = jnp.concatenate([deal[0].reshape(-1), lengths[0] // 64, lengths[0] % 64]).astype(LOW)
    theirs = swap_dp(meta)
    meta = jnp.where(place // micro == core, meta, theirs)
    turn = place % micro
    meta = jnp.concatenate([
        lax.dynamic_slice_in_dim(meta, turn * blocks, blocks), lax.dynamic_slice_in_dim(meta, micro * blocks + turn, 1),
        lax.dynamic_slice_in_dim(meta, micro * (blocks + 1) + turn, 1),
    ])
    size = b_qkv.shape[0] + b_out.shape[0] + b_up.shape[0] + b_down.shape[0] + meta.shape[0]
    small = jnp.concatenate([b_qkv, b_out, b_up, b_down, meta, jnp.zeros((-size % 512,), LOW)])

    up_sent = columns_sent([after(piece, hidden_home) for piece in columns_cut(w_up, 1, core, shard)])
    waited = [piece for bits, _, piece in up_sent if bits]
    small = lax.all_gather(after(small, *waited), "fsdp", axis=0, tiled=False)
    bounds = [0]
    for piece in (b_qkv, b_out, b_up, b_down, meta):
        bounds.append(bounds[-1] + piece.shape[0])
    bias_qkv, bias_out, bias_up, bias_down, meta = (small[:, a:b] for a, b in zip(bounds[:-1], bounds[1:]))
    own_blocks = lax.dynamic_slice_in_dim(deal[0], 2 * place, 2, axis=1)
    local_pos = (own_blocks[:, :, None] * blk + jnp.arange(blk, dtype=jnp.int32)).reshape(micro, rows)
    valid = (local_pos < lengths[0][:, None])[:, :, None]
    gout_home = jnp.where(valid, cotangent[0], jnp.zeros((), LOW))

    g_received = for_other(after(gout_home, hidden_home), core, blk)
    h_dealt = deal_out(hidden_home)
    hidden_own = lax.all_gather(after(h_dealt, *[piece for _, _, piece in up_sent]), "fsdp", axis=0, tiled=True)
    hidden = (hidden_own, swap_dp(hidden_own))
    up_w = placed(up_sent, shard, w_up.shape[0])
    g_dealt = deal_out(line_up(gout_home, after(g_received, h_dealt), core, blk))
    gout_own = lax.all_gather(g_dealt, "fsdp", axis=0, tiled=True)

    bias_ends = (bias_out.astype(WIDE) + bias_down.astype(WIDE)).reshape(-1)
    meta = meta.astype(jnp.int32)
    plane_len = meta[:, blocks] * 64 + meta[:, blocks + 1]
    plane_deal = meta[:, :blocks].reshape(4, 4, 2)
    deal_own = pick(plane_deal, core, 2)
    deal_oth = pick(plane_deal, 1 - core, 2)
    up_b = lax.dynamic_slice_in_dim(bias_up.reshape(-1), spot * units, units).astype(WIDE)
    qkv_b = pick(bias_qkv.reshape(3, 8, head_cols), spot, 1).reshape(-1).astype(WIDE)

    acts, slopes, dups, datts = [], [], [], []
    for h in hidden:
        act, slope = up_call(h, up_w, up_b)
        acts.append(act)
        slopes.append(slope)
    gout_own = after(gout_own, *acts)
    gout = (gout_own, swap_dp(gout_own))
    qkv_sent = columns_sent([after(piece, gout_own) for piece in columns_cut(w_qkv, 3, core, shard)])
    qkv_w = placed(qkv_sent, shard, w_qkv.shape[0])
    tables = rope_tables(8 * blk)
    down_w = lax.dynamic_slice_in_dim(w_down, core * units, units, 0)
    out_w = lax.dynamic_slice_in_dim(w_out, core * head_cols, head_cols, 0)

    def scatter(grad):
        return lax.psum_scatter(grad, "ctx", scatter_dimension=0, tiled=True)

    def gather(piece):
        return lax.all_gather(piece, "ctx", axis=0, tiled=True)

    def exchange(piece):
        return lax.all_to_all(piece[0], "fsdp", 0, 0, tiled=True)

    g_down = grad_call(acts, [gout])[0]
    t_down = gather(scatter(g_down))
    for g, slope in zip((after(gout[0], g_down), gout[1]), slopes):
        dup, datt = down_back_call(g, slope, down_w, out_w)
        dups.append(dup)
        datts.append(datt)
    waited = [piece for bits, _, piece in qkv_sent if bits]
    g_up, s_up = grad_call((after(hidden[0], *dups, *waited), hidden[1]), [dups], sums=True, dealt=True)
    x_up = exchange(scatter(g_up))
    t_up = gather(x_up[None])
    joins = [join_call(after(h, g_up), qkv_w, qkv_b) for h in hidden]

    per_seq = (4, 4 * blk, -1)
    shaped = [piece.reshape(per_seq) for piece in (joins[0], joins[1], datts[0], datts[1])]
    sides = attention_call(deal_own, deal_oth, plane_len, *shaped, tables, blk, 0, 4)
    sides = [piece.reshape(16 * blk, -1) for piece in sides]
    atts = [sides[0], sides[4]]
    turned = [sides[1:4], sides[5:8]]

    g_out = grad_call(atts, [gout], dealt=True, flip=True)[0]
    g_qkv, s_q, s_k, s_v = grad_call(
        (after(hidden[0], g_out), hidden[1]), [(turned[0][i], turned[1][i]) for i in range(3)], sums=True, dealt=True
    )
    mine = scatter(jnp.concatenate([g_qkv, g_out], axis=3))[0]
    qkv_cols = g_qkv.shape[3]
    x_qkv = lax.all_to_all(mine[:, :, :qkv_cols], "fsdp", 0, 0, tiled=True)
    t_qkv = gather(x_qkv[None])
    t_out = gather(after(mine[:, :, qkv_cols:], x_qkv)[None])
    sums_tp = line_sum(jnp.concatenate([s_up, s_q, s_k, s_v], axis=1), place)
    tails = lax.all_gather(sums_tp, ("fsdp", "dp"), axis=0, tiled=True)
    b_oth = backward_call(dups[1], after(turned[1], g_qkv, x_up), up_w, qkv_w)
    f_oth = forward_call(after(acts[1], b_oth, t_down), atts[1], down_w, out_w)
    b_total = backward_call(after(dups[0], f_oth), turned[0], up_w, qkv_w, swap_dp(b_oth))
    f_total = forward_call(after(acts[0], b_total), atts[0], down_w, out_w, swap_dp(f_oth))
    d_hidden = collect(b_total, shard, f_total)
    mixed = collect(f_total, shard)
    d_hidden = to_home(after(d_hidden, x_qkv), core, place, blk)
    t_up = after(t_up, f_total, x_qkv)
    o_up = cols_out(core, shard, t_up, after(swap_dp(t_up), tails), 1, 1)
    o_down = rows_out(core, shard, t_down, after(swap_dp(t_down), o_up))
    d_hidden = after(d_hidden, o_down).astype(WIDE)
    mixed = to_home(mixed, core, place, blk)
    t_qkv = after(t_qkv, o_down)
    o_qkv = cols_out(core, shard, t_qkv, swap_dp(t_qkv), 3, 3)
    t_out = after(t_out, o_qkv)
    o_out = flipped_out(core, shard, t_out, swap_dp(t_out), 0)

    inputs, normed, inv_std = normed_rows(after(tokens[0], f_total))
    d_norm = d_hidden * gain
    d_inputs = inv_std * (
        d_norm
        - jnp.mean(d_norm, axis=-1, keepdims=True)
        - normed * jnp.mean(d_norm * normed, axis=-1, keepdims=True)
    )
    back = (gout_home.astype(WIDE) + d_inputs).astype(LOW)

    mixed = after(mixed, o_qkv, o_out)
    result = jnp.where(valid, inputs + mixed.astype(WIDE) + bias_ends, 0.0).astype(LOW)
    d_bup = lax.dynamic_slice(tails, (2 * shard, 0), (2, units)).reshape(-1)
    d_bqkv = tails[:, units:].reshape(8, 3, head_cols).transpose(1, 0, 2).reshape(-1)
    d_bqkv = lax.dynamic_slice_in_dim(d_bqkv, shard * b_qkv.shape[0], b_qkv.shape[0])
    sums = jnp.stack([
        jnp.sum(d_hidden * normed, axis=(0, 1)), jnp.sum(d_hidden, axis=(0, 1)), jnp.sum(gout_home.astype(WIDE), axis=(0, 1)),
    ])
    sums = every_sum(sums, place)
    sums = lax.dynamic_slice_in_dim(sums, shard * ln_gain.shape[0], ln_gain.shape[0], 1)

    return result[None], back[None], sums[0], sums[1], o_qkv, d_bqkv, o_out, sums[2], o_up, d_bup, o_down, sums[2]


def plane_fits(mesh, shapes):
    tokens, _, _, deal = shapes[:4]
    sizes = dict(mesh.shape)
    dp, ctx, fsdp = sizes["dp"], sizes["ctx"], sizes["fsdp"]
    micro, seq_len, width = tokens.shape[1:]
    blocks = deal.shape[2]
    heads = width // HEAD_DIM
    return (
        dp == 2
        and dp * micro == ctx == fsdp == 4
        and tokens.shape[0] == dp * fsdp
        and blocks == dp * ctx
        and heads % (2 * dp * fsdp) == 0
        and seq_len % 256 == 0
        and (seq_len // blocks) % 128 == 0
    )


def solution(mesh):
    in_specs = (
        P(("dp", "fsdp"), None, "ctx", None),
        P(("dp", "fsdp"), None, "ctx", None),
        P(("dp", "fsdp"), None),
        P(("dp", "fsdp"), None, None),
        P("fsdp"),
        P("fsdp"),
        P("fsdp", None),
        P("fsdp"),
        P("fsdp", None),
        P("fsdp"),
        P("fsdp", None),
        P("fsdp"),
        P("fsdp", None),
        P("fsdp"),
    )
    out_specs = (
        P(("dp", "fsdp"), None, "ctx", None),
        P(("dp", "fsdp"), None, "ctx", None),
        P("fsdp"),
        P("fsdp"),
        P("fsdp", None),
        P("fsdp"),
        P("fsdp", None),
        P("fsdp"),
        P("fsdp", None),
        P("fsdp"),
        P("fsdp", None),
        P("fsdp"),
    )

    def program(*arrays):
        body = plane_body if plane_fits(mesh, arrays) else gathered_body
        return jax.shard_map(body, mesh=mesh, in_specs=in_specs, out_specs=out_specs, check_vma=False)(*arrays)

    return program
```

```python
import jax
import jax.numpy as jnp
from jax import lax
from jax.experimental import pallas as pl
from jax.experimental.pallas import tpu as pltpu
from jax.sharding import PartitionSpec as P

HEAD_DIM = 64
ROT = 32


EPS = 1e-05
BASE = 10000.0


def contract_rows(left, right):
    return lax.dot_general(
        left, right, (((0,), (0,)), ((), ())), preferred_element_type=jnp.float32
    )


def contract_cols(left, right):
    return lax.dot_general(
        left, right, (((1,), (1,)), ((), ())), preferred_element_type=jnp.float32
    )


def angles_of(positions):
    half = ROT // 2
    freqs = BASE ** (-(jnp.arange(half, dtype=jnp.float32) * 2.0) / ROT)
    angles = positions.astype(jnp.float32)[:, None] * freqs[None, :]
    return (jnp.cos(angles)[:, None, :], jnp.sin(angles)[:, None, :])


def rotate(values, cosine, sine):
    half = ROT // 2
    first = values[..., :half]
    second = values[..., half:ROT]
    return jnp.concatenate(
        [first * cosine - second * sine, second * cosine + first * sine, values[..., ROT:]], axis=-1
    )


def rotate_back(values, cosine, sine):
    half = ROT // 2
    first = values[..., :half]
    second = values[..., half:ROT]
    return jnp.concatenate(
        [first * cosine + second * sine, second * cosine - first * sine, values[..., ROT:]], axis=-1
    )


def layer_step(weights, inputs, upstream, length, deal_row):
    gain, shift, w_qkv, b_qkv, w_out, b_out, w_up, b_up, w_down, b_down = weights
    row_count, width = inputs.shape
    block_rows = row_count // 2
    head_count = width // HEAD_DIM
    scale = HEAD_DIM ** (-0.5)
    place = lax.axis_index("ctx")
    offsets = jnp.arange(block_rows, dtype=jnp.int32)
    own_blocks = lax.dynamic_slice_in_dim(deal_row, 2 * place, 2)
    local_pos = (own_blocks[:, None] * block_rows + offsets[None, :]).reshape(row_count)
    every_pos = (deal_row[:, None] * block_rows + offsets[None, :]).reshape(-1)
    valid = (local_pos < length).astype(jnp.float32)[:, None]
    allowed = (every_pos[None, :] <= local_pos[:, None]) & (every_pos[None, :] < length)
    cosine, sine = angles_of(local_pos)
    inputs_f = inputs.astype(jnp.float32)
    gain_f = gain.astype(jnp.float32)
    centered = inputs_f - jnp.mean(inputs_f, axis=-1, keepdims=True)
    variance = jnp.mean(centered * centered, axis=-1, keepdims=True)
    inv_std = lax.rsqrt(variance + EPS)
    normed = centered * inv_std
    hidden = (normed * gain_f + shift.astype(jnp.float32)).astype(jnp.bfloat16)
    joined = jnp.dot(hidden, w_qkv, preferred_element_type=jnp.float32) + b_qkv.astype(jnp.float32)
    query = (
        rotate(joined[:, :width].reshape(row_count, head_count, HEAD_DIM), cosine, sine)
        .reshape(row_count, width)
        .astype(jnp.bfloat16)
    )
    keyed = (
        rotate(joined[:, width : 2 * width].reshape(row_count, head_count, HEAD_DIM), cosine, sine)
        .reshape(row_count, width)
        .astype(jnp.bfloat16)
    )
    valued = joined[:, 2 * width :].astype(jnp.bfloat16)
    keys_all, values_all = (
        lax.all_gather(keyed, "ctx", axis=0, tiled=True),
        lax.all_gather(valued, "ctx", axis=0, tiled=True),
    )
    total_keys = keys_all.shape[0]
    group = min(8, head_count)
    span = group * HEAD_DIM

    def heads_of(array, start, count):
        return array[:, start : start + span].reshape(count, group, HEAD_DIM)

    def block_scores(start):
        raw = (
            jnp.einsum(
                "qhd,khd->hqk",
                heads_of(query, start, row_count),
                heads_of(keys_all, start, total_keys),
                preferred_element_type=jnp.float32,
            )
            * scale
        )
        return jnp.where(allowed[None], raw, -1e30)

    attended_parts = []
    lse_parts = []
    for start in range(0, width, span):
        masked = block_scores(start)
        highest = jnp.max(masked, axis=-1, keepdims=True)
        expo = jnp.exp(masked - highest)
        total = jnp.sum(expo, axis=-1, keepdims=True)
        weights_low = (expo / total).astype(jnp.bfloat16)
        mixed = jnp.einsum(
            "hqk,khd->qhd",
            weights_low,
            heads_of(values_all, start, total_keys),
            preferred_element_type=jnp.float32,
        )
        attended_parts.append(mixed.reshape(row_count, span))
        lse_parts.append(highest + jnp.log(total))
    attended = jnp.concatenate(attended_parts, axis=1).astype(jnp.bfloat16)
    branch = jnp.dot(attended, w_out, preferred_element_type=jnp.float32) + b_out.astype(
        jnp.float32
    )
    upward = jnp.dot(hidden, w_up, preferred_element_type=jnp.float32) + b_up.astype(jnp.float32)
    activated = jax.nn.gelu(upward, approximate=True).astype(jnp.bfloat16)
    feed = jnp.dot(activated, w_down, preferred_element_type=jnp.float32) + b_down.astype(
        jnp.float32
    )
    result = (valid * (inputs_f + branch + feed)).astype(jnp.bfloat16)
    grad_out = upstream.astype(jnp.float32) * valid
    grad_low = grad_out.astype(jnp.bfloat16)
    row_total = jnp.sum(grad_out, axis=0)
    d_down = contract_rows(activated, grad_low)
    d_wout = contract_rows(attended, grad_low)
    d_act = contract_cols(grad_low, w_down)
    _, gelu_pull = jax.vjp(lambda value: jax.nn.gelu(value, approximate=True), upward)
    d_upward = gelu_pull(d_act)[0].astype(jnp.bfloat16)
    d_wup = contract_rows(hidden, d_upward)
    d_bup = jnp.sum(d_upward.astype(jnp.float32), axis=0)
    d_attended = contract_cols(grad_low, w_out).astype(jnp.bfloat16)
    dq_parts = []
    dk_parts = []
    dv_parts = []
    delta_parts = []
    for index, start in enumerate(range(0, width, span)):
        masked = block_scores(start)
        probs = jnp.where(allowed[None], jnp.exp(masked - lse_parts[index]), 0.0)
        d_heads = heads_of(d_attended, start, row_count)
        d_probs = jnp.einsum(
            "qhd,khd->hqk",
            d_heads,
            heads_of(values_all, start, total_keys),
            preferred_element_type=jnp.float32,
        )
        delta = jnp.sum(probs * d_probs, axis=-1, keepdims=True)
        d_scores = (probs * (d_probs - delta)).astype(jnp.bfloat16)
        d_query = (
            jnp.einsum(
                "hqk,khd->qhd",
                d_scores,
                heads_of(keys_all, start, total_keys),
                preferred_element_type=jnp.float32,
            )
            * scale
        )
        dq_parts.append(d_query.reshape(row_count, span))
        delta_parts.append(delta[:, :, 0].T)
        d_keyed = (
            jnp.einsum(
                "hqk,qhd->khd",
                d_scores,
                heads_of(query, start, row_count),
                preferred_element_type=jnp.float32,
            )
            * scale
        )
        d_valued = jnp.einsum(
            "hqk,qhd->khd", probs.astype(jnp.bfloat16), d_heads, preferred_element_type=jnp.float32
        )
        dk_parts.append(d_keyed.reshape(total_keys, span))
        dv_parts.append(d_valued.reshape(total_keys, span))
    keys_grad_all = jnp.concatenate(dk_parts, axis=1)
    values_grad_all = jnp.concatenate(dv_parts, axis=1)
    keys_grad, values_grad = (
        lax.psum_scatter(
            keys_grad_all.astype(jnp.bfloat16), "ctx", scatter_dimension=0, tiled=True
        ).astype(jnp.float32),
        lax.psum_scatter(
            values_grad_all.astype(jnp.bfloat16), "ctx", scatter_dimension=0, tiled=True
        ).astype(jnp.float32),
    )
    query_grad = rotate_back(
        jnp.concatenate(dq_parts, axis=1).reshape(row_count, head_count, HEAD_DIM), cosine, sine
    ).reshape(row_count, width)
    keyed_grad = rotate_back(
        keys_grad.reshape(row_count, head_count, HEAD_DIM), cosine, sine
    ).reshape(row_count, width)
    d_joined = jnp.concatenate([query_grad, keyed_grad, values_grad], axis=1).astype(jnp.bfloat16)
    d_wqkv = contract_rows(hidden, d_joined)
    d_bqkv = jnp.sum(d_joined.astype(jnp.float32), axis=0)
    d_hidden = contract_cols(d_joined, w_qkv) + contract_cols(d_upward, w_up)
    d_gain = jnp.sum(d_hidden * normed, axis=0)
    d_shift = jnp.sum(d_hidden, axis=0)
    d_norm = d_hidden * gain_f
    d_inputs = inv_std * (
        d_norm
        - jnp.mean(d_norm, axis=-1, keepdims=True)
        - normed * jnp.mean(d_norm * normed, axis=-1, keepdims=True)
    )
    back = (grad_out + d_inputs).astype(jnp.bfloat16)
    return (
        result,
        back,
        (d_gain, d_shift, d_wqkv, d_bqkv, d_wout, row_total, d_wup, d_bup, d_down, row_total),
    )


def gathered_body(
    tokens,
    cotangent,
    lengths,
    deal,
    ln_gain,
    ln_bias,
    w_qkv,
    b_qkv,
    w_out,
    b_out,
    w_up,
    b_up,
    w_down,
    b_down,
):
    shards = (ln_gain, ln_bias, w_qkv, b_qkv, w_out, b_out, w_up, b_up, w_down, b_down)
    shard_count = lax.axis_size("fsdp")
    summed = tuple(
        (
            jnp.zeros((piece.shape[0] * shard_count,) + piece.shape[1:], jnp.float32)
            for piece in shards
        )
    )
    results = []
    backs = []
    for micro_index in range(tokens.shape[1]):
        gathered = (
            lax.all_gather(ln_gain, "fsdp", axis=0, tiled=True),
            lax.all_gather(ln_bias, "fsdp", axis=0, tiled=True),
            lax.all_gather(w_qkv, "fsdp", axis=0, tiled=True),
            lax.all_gather(b_qkv, "fsdp", axis=0, tiled=True),
            lax.all_gather(w_out, "fsdp", axis=0, tiled=True),
            lax.all_gather(b_out, "fsdp", axis=0, tiled=True),
            lax.all_gather(w_up, "fsdp", axis=0, tiled=True),
            lax.all_gather(b_up, "fsdp", axis=0, tiled=True),
            lax.all_gather(w_down, "fsdp", axis=0, tiled=True),
            lax.all_gather(b_down, "fsdp", axis=0, tiled=True),
        )
        result, back, local = layer_step(
            gathered,
            tokens[0, micro_index],
            cotangent[0, micro_index],
            lengths[0, micro_index],
            deal[0, micro_index],
        )
        results.append(result)
        backs.append(back)
        summed = tuple((older + newer for older, newer in zip(summed, local)))
    summed = (
        lax.psum_scatter(
            summed[0].astype(jnp.bfloat16), "fsdp", scatter_dimension=0, tiled=True
        ).astype(jnp.float32),
        lax.psum_scatter(
            summed[1].astype(jnp.bfloat16), "fsdp", scatter_dimension=0, tiled=True
        ).astype(jnp.float32),
        lax.psum_scatter(
            summed[2].astype(jnp.bfloat16), "fsdp", scatter_dimension=0, tiled=True
        ).astype(jnp.float32),
        lax.psum_scatter(
            summed[3].astype(jnp.bfloat16), "fsdp", scatter_dimension=0, tiled=True
        ).astype(jnp.float32),
        lax.psum_scatter(
            summed[4].astype(jnp.bfloat16), "fsdp", scatter_dimension=0, tiled=True
        ).astype(jnp.float32),
        lax.psum_scatter(
            summed[5].astype(jnp.bfloat16), "fsdp", scatter_dimension=0, tiled=True
        ).astype(jnp.float32),
        lax.psum_scatter(
            summed[6].astype(jnp.bfloat16), "fsdp", scatter_dimension=0, tiled=True
        ).astype(jnp.float32),
        lax.psum_scatter(
            summed[7].astype(jnp.bfloat16), "fsdp", scatter_dimension=0, tiled=True
        ).astype(jnp.float32),
        lax.psum_scatter(
            summed[8].astype(jnp.bfloat16), "fsdp", scatter_dimension=0, tiled=True
        ).astype(jnp.float32),
        lax.psum_scatter(
            summed[9].astype(jnp.bfloat16), "fsdp", scatter_dimension=0, tiled=True
        ).astype(jnp.float32),
    )
    totals = (
        lax.psum(summed[0].astype(jnp.bfloat16), ("dp", "ctx")).astype(jnp.float32),
        lax.psum(summed[1].astype(jnp.bfloat16), ("dp", "ctx")).astype(jnp.float32),
        lax.psum(summed[2].astype(jnp.bfloat16), ("dp", "ctx")).astype(jnp.float32),
        lax.psum(summed[3].astype(jnp.bfloat16), ("dp", "ctx")).astype(jnp.float32),
        lax.psum(summed[4].astype(jnp.bfloat16), ("dp", "ctx")).astype(jnp.float32),
        lax.psum(summed[5].astype(jnp.bfloat16), ("dp", "ctx")).astype(jnp.float32),
        lax.psum(summed[6].astype(jnp.bfloat16), ("dp", "ctx")).astype(jnp.float32),
        lax.psum(summed[7].astype(jnp.bfloat16), ("dp", "ctx")).astype(jnp.float32),
        lax.psum(summed[8].astype(jnp.bfloat16), ("dp", "ctx")).astype(jnp.float32),
        lax.psum(summed[9].astype(jnp.bfloat16), ("dp", "ctx")).astype(jnp.float32),
    )
    stacked_out = jnp.stack(results)[None]
    stacked_back = jnp.stack(backs)[None]
    return (
        stacked_out,
        stacked_back,
        totals[0],
        totals[1],
        totals[2],
        totals[3],
        totals[4],
        totals[5],
        totals[6],
        totals[7],
        totals[8],
        totals[9],
    )


SWAP = [(0, 1), (1, 0)]
LOW = jnp.bfloat16
SLOW = 1.8
WIDE = jnp.float32


def hint(flops, transcendentals, bytes_accessed):
    return pl.CostEstimate(
        flops=int(flops * SLOW), transcendentals=transcendentals, bytes_accessed=bytes_accessed
    )


def after(value, *others):
    return lax.optimization_barrier((value,) + others)[0]


def swap_dp(value):
    return lax.ppermute(value, "dp", SWAP)


def swap_shard(value, bits):
    return lax.ppermute(value, "fsdp", [(i, i ^ bits) for i in range(4)])


def shift_ctx(value, steps):
    return lax.ppermute(value, "ctx", [(i, (i + steps) % 4) for i in range(4)])


def pick(array, index, axis):
    return lax.dynamic_index_in_dim(array, index, axis, keepdims=False)


def by_core(core, mine, other, axis):
    first = jnp.where(core == 0, mine, other)
    second = jnp.where(core == 0, other, mine)
    return jnp.stack([first, second], axis=axis)


def for_other(rows, core, blk):
    micro, _, width = rows.shape
    return swap_dp(pick(rows.reshape(micro, 2, blk, width), 1 - core, 1))


def line_up(rows, received, core, blk):
    micro, _, width = rows.shape
    return by_core(core, pick(rows.reshape(micro, 2, blk, width), core, 1), received, 0).reshape(4, blk, width)


def deal_out(lined):
    return lax.all_to_all(lined, "ctx", 0, 0, tiled=True).reshape(-1, lined.shape[2])


def normed_rows(rows):
    inputs = rows.astype(WIDE)
    centered = inputs - jnp.mean(inputs, axis=-1, keepdims=True)
    inv_std = lax.rsqrt(jnp.mean(centered * centered, axis=-1, keepdims=True) + EPS)
    return inputs, centered * inv_std, inv_std


def placed(pieces, shard, size, *gates):
    whole = after(jnp.zeros((4 * size, pieces[0][2].shape[1]), LOW), *gates)
    for bits, start, piece in pieces:
        whole = lax.dynamic_update_slice(whole, piece, ((shard ^ bits) * size + start, 0))
    return whole


def plus(first, *others):
    total = first.astype(WIDE)
    for other in others:
        total = total + other.astype(WIDE)
    return total.astype(LOW)


def collect(total, shard, *gates):
    size = total.shape[0] // 4
    half = size // 2

    def part(bits, which):
        return lax.dynamic_slice_in_dim(total, (shard ^ bits) * size + which * half, half, 0)

    via_x, via_y = swap_shard(part(3, 0), 1), swap_shard(part(3, 1), 2)
    x_top, y_end = swap_shard(part(1, 0), 1), swap_shard(part(2, 1), 2)
    y_top = swap_shard(plus(part(2, 0), after(via_x, *gates)), 2)
    x_end = swap_shard(plus(part(1, 1), after(via_y, *gates)), 1)
    return jnp.concatenate([plus(part(0, 0), x_top, y_top), plus(part(0, 1), x_end, y_end)])


def to_home(mine, core, place, blk):
    width = mine.shape[1]
    lined = lax.all_to_all(mine.reshape(4, blk, width), "ctx", 0, 0, tiled=True).reshape(2, 2, blk, width)
    kept = pick(lined, core, 0)
    received = swap_dp(pick(lined, 1 - core, 0))
    return by_core(core, kept, received, 1).reshape(2, 2 * blk, width)


def columns_cut(weight, parts, core, shard):
    width = weight.shape[1] // (parts * 8)
    pieces = []
    for bits in range(4):
        spot = 2 * (shard ^ bits) + core
        pieces.append(jnp.concatenate(
            [lax.dynamic_slice_in_dim(weight, (t * 8 + spot) * width, width, 1) for t in range(parts)], axis=1
        ))
    return pieces


def columns_sent(pieces):
    return [(bits, 0, piece if bits == 0 else swap_shard(piece, bits)) for bits, piece in enumerate(pieces)]


def inward(value):
    return lax.ppermute(value, "ctx", [(0, 1), (3, 2)])


def across(value):
    return lax.ppermute(value, "ctx", [(1, 2), (2, 1)])


def outward(value):
    return lax.ppermute(value, "ctx", [(1, 0), (2, 3)])


def line_sum(value, place):
    half = value + inward(value)
    whole = half + across(half)
    return line_end(whole, outward(whole), place)


def line_end(whole, received, place):
    return jnp.where((place == 1) | (place == 2), whole, received)


def every_sum(value, place):
    value = value + swap_dp(value)
    value = value + swap_shard(value, 1)
    value = value + swap_shard(value, 2)
    return line_sum(value, place)


def lay_out(core, shard, own, oth, out_shape, grid, block, in_at, out_at):
    def kernel(where, own_ref, oth_ref, out_ref):
        side = pl.program_id(len(grid))

        @pl.when(side == 0)
        def _():
            out_ref[...] = own_ref[...].astype(WIDE)

        @pl.when(side == 1)
        def _():
            out_ref[...] = oth_ref[...].astype(WIDE)

    source = pl.BlockSpec(block, lambda *args: in_at(*args[: len(grid)]))
    target = pl.BlockSpec(block, lambda *args: out_at(*args[:-1], args[-1][0], args[-1][1]))
    count = out_shape[0] * out_shape[1]
    return pl.pallas_call(
        kernel,
        grid_spec=pltpu.PrefetchScalarGridSpec(
            num_scalar_prefetch=1, grid=grid + (2,), in_specs=[source, source], out_specs=target
        ),
        out_shape=jax.ShapeDtypeStruct(out_shape, WIDE),
        compiler_params=pltpu.CompilerParams(dimension_semantics=("arbitrary",) * (len(grid) + 1)),
        cost_estimate=hint(flops=0, transcendentals=0, bytes_accessed=6 * count),
    )(jnp.stack([core, shard]).astype(jnp.int32), own, oth)


def rows_out(core, shard, own, oth):
    rows, width = own.shape
    tile = min(256, rows)
    steps = rows // tile
    return lay_out(
        core, shard, own, oth, (2 * rows, width), (steps,), (tile, width),
        lambda i: (i, 0), lambda i, s, c, f: ((c ^ s) * steps + i, 0),
    )


def cols_half(core, shard, half, side, parts, held, earlier=()):
    lines, columns, rows, width = half.shape
    width = width // held

    def kernel(where, half_ref, *rest):
        rest[-1][...] = half_ref[...].reshape(lines * rows, width).astype(WIDE)

    return pl.pallas_call(
        kernel,
        grid_spec=pltpu.PrefetchScalarGridSpec(
            num_scalar_prefetch=1,
            grid=(columns, parts),
            in_specs=[pl.BlockSpec((lines, 1, rows, width), lambda b, t, where: (0, b, 0, t))]
            + [pl.BlockSpec(memory_space=pl.ANY)] * len(earlier),
            out_specs=pl.BlockSpec((lines * rows, width), lambda b, t, where: (0, t * 8 + 2 * b + (where[0] ^ side))),
        ),
        out_shape=jax.ShapeDtypeStruct((lines * rows, 2 * columns * parts * width), WIDE),
        input_output_aliases={2: 0} if earlier else {},
        compiler_params=pltpu.CompilerParams(dimension_semantics=("arbitrary",) * 2),
        cost_estimate=pl.CostEstimate(flops=0, transcendentals=0, bytes_accessed=6 * half.size),
    )(jnp.stack([core, shard]).astype(jnp.int32), half, *earlier)


def cols_out(core, shard, own, oth, parts, held):
    first = cols_half(core, shard, own, 0, parts, held)
    return cols_half(core, shard, oth, 1, parts, held, (first,))


GELU_C = 0.7978845608028654
GELU_A = 0.044715


def gelu_pair(value):
    square = value * value
    tanh = jnp.tanh(GELU_C * value * (1.0 + GELU_A * square))
    half = 0.5 * (1.0 + tanh)
    slope = half + 0.5 * value * (1.0 - tanh * tanh) * (GELU_C * (1.0 + 3.0 * GELU_A * square))
    return value * half, slope


ROWS_OF = (((0,), (0,)), ((), ()))
COLS_OF = (((1,), (1,)), ((), ()))
ROOM = 56 * 1024 * 1024


def row_call(body, tiled, whole, widths, flops, tile=512):
    count = tiled[0].shape[0]

    def rows_spec(width):
        return pl.BlockSpec((tile, width), lambda i: (i, 0))

    moved = sum(a.size * a.dtype.itemsize for a in (*tiled, *whole)) + 2 * count * sum(widths)
    return pl.pallas_call(
        body,
        grid=(count // tile,),
        in_specs=[rows_spec(a.shape[1]) for a in tiled]
        + [pl.BlockSpec(a.shape, lambda i: (0, 0), pipeline_mode=pl.Buffered(1)) for a in whole],
        out_specs=[rows_spec(width) for width in widths],
        out_shape=[jax.ShapeDtypeStruct((count, width), LOW) for width in widths],
        compiler_params=pltpu.CompilerParams(dimension_semantics=("arbitrary",), vmem_limit_bytes=ROOM),
        cost_estimate=hint(flops=flops, transcendentals=0, bytes_accessed=moved),
    )(*tiled, *whole)


def strips(width):
    step = min(256, width)
    return [slice(at, at + step) for at in range(0, width, step)]


def up_call(rows, weight, bias):
    def body(rows_ref, weight_ref, bias_ref, act_ref, slope_ref):
        for at in strips(weight.shape[1]):
            total = jnp.dot(rows_ref[...], weight_ref[:, at], preferred_element_type=WIDE) + bias_ref[:, at]
            act, slope = gelu_pair(total)
            act_ref[:, at] = act.astype(LOW)
            slope_ref[:, at] = slope.astype(LOW)

    width = weight.shape[1]
    return row_call(body, [rows], [weight, bias[None]], [width, width], 2 * rows.shape[0] * weight.size)


def join_call(rows, weight, bias):
    def body(rows_ref, weight_ref, bias_ref, out_ref):
        for at in strips(weight.shape[1]):
            total = jnp.dot(rows_ref[...], weight_ref[:, at], preferred_element_type=WIDE)
            out_ref[:, at] = (total + bias_ref[:, at]).astype(LOW)

    return row_call(body, [rows], [weight, bias[None]], [weight.shape[1]], 2 * rows.shape[0] * weight.size)[0]


def down_back_call(rows, slopes, down_w, out_w):
    def body(rows_ref, slope_ref, down_ref, out_w_ref, dup_ref, datt_ref):
        for at in strips(down_w.shape[0]):
            total = lax.dot_general(rows_ref[...], down_ref[at, :], COLS_OF, preferred_element_type=WIDE)
            dup_ref[:, at] = (total * slope_ref[:, at].astype(WIDE)).astype(LOW)
        total = lax.dot_general(rows_ref[...], out_w_ref[...], COLS_OF, preferred_element_type=WIDE)
        datt_ref[...] = total.astype(LOW)

    flops = 2 * rows.shape[0] * (down_w.size + out_w.size)
    return row_call(body, [rows, slopes], [down_w, out_w], [down_w.shape[0], out_w.shape[0]], flops)


def forward_call(act, att, down_w, out_w, added=None):
    def body(*refs):
        act_ref, att_ref = refs[:2]
        down_ref, out_w_ref, out_ref = refs[-3:]
        for at in strips(down_w.shape[1]):
            total = jnp.dot(act_ref[...], down_ref[:, at], preferred_element_type=WIDE)
            total = total + jnp.dot(att_ref[...], out_w_ref[:, at], preferred_element_type=WIDE)
            if added is not None:
                total = total + refs[2][:, at].astype(WIDE)
            out_ref[:, at] = total.astype(LOW)

    tiled = [act, att] + ([] if added is None else [added])
    flops = 2 * act.shape[0] * (down_w.size + out_w.size)
    return row_call(body, tiled, [down_w, out_w], [down_w.shape[1]], flops)[0]


def backward_call(dup, turned, up_w, qkv_w, added=None):
    wide = turned[0].shape[1]

    def body(*refs):
        dup_ref, turned_refs = refs[0], refs[1:4]
        up_ref, qkv_ref, out_ref = refs[-3:]
        for at in strips(up_w.shape[0]):
            total = lax.dot_general(dup_ref[...], up_ref[at, :], COLS_OF, preferred_element_type=WIDE)
            for i, ref in enumerate(turned_refs):
                part = qkv_ref[at, i * wide : (i + 1) * wide]
                total = total + lax.dot_general(ref[...], part, COLS_OF, preferred_element_type=WIDE)
            if added is not None:
                total = total + refs[4][:, at].astype(WIDE)
            out_ref[:, at] = total.astype(LOW)

    tiled = [dup, *turned] + ([] if added is None else [added])
    flops = 2 * dup.shape[0] * (up_w.size + qkv_w.size)
    return row_call(body, tiled, [up_w, qkv_w], [up_w.shape[0]], flops)[0]


def grad_call(left, rights, left_part=(0, 1), right_part=(0, 1), sums=False, dealt=False, flip=False, tile=512):
    steps = left[0].shape[0] // tile
    left_cols = left[0].shape[1] // left_part[1]
    right_cols = [pair[0].shape[1] // right_part[1] for pair in rights]
    count = len(rights)
    piece = (right_cols[0] if flip else left_cols) // 16
    made = 1 if dealt else count

    def body(*refs):
        ins, outs = refs[: 2 + 2 * count], refs[2 + 2 * count :]
        grads, totals, accs = outs[:made], outs[made : len(outs) - count], outs[len(outs) - count :]
        step = pl.program_id(0)

        @pl.when(step == 0)
        def _():
            for ref in (*accs, *totals):
                ref[...] = jnp.zeros_like(ref)

        def add(left_ref, right_refs):
            for i, ref in enumerate(right_refs):
                for at in strips(right_cols[i]):
                    accs[i][:, at] += lax.dot_general(
                        left_ref[...], ref[:, at], ROWS_OF, preferred_element_type=WIDE
                    )
                if sums:
                    totals[i][...] += jnp.sum(ref[...].astype(WIDE), axis=0, keepdims=True)

        @pl.when(step < steps)
        def _():
            add(ins[0], ins[2 : 2 + count])

        @pl.when(step >= steps)
        def _():
            add(ins[1], ins[2 + count :])

        @pl.when(step == 2 * steps - 1)
        def _():
            if not dealt:
                for grad, acc in zip(grads, accs):
                    grad[...] = acc[...].astype(LOW)
                return
            if flip:
                for spot in range(16):
                    part = accs[0][:, spot * piece : (spot + 1) * piece]
                    grads[0][spot % 4, spot // 4] = part.T.astype(LOW)
                return
            start = 0
            for acc, cols in zip(accs, right_cols):
                for column in range(4):
                    for line in range(4):
                        at = (4 * column + line) * piece
                        grads[0][line, column, :, start : start + cols] = acc[at : at + piece, :].astype(LOW)
                start += cols

    def side_spec(cols, part, side):
        def at(step):
            row = jnp.minimum(step, steps - 1) if side == 0 else jnp.maximum(step - steps, 0)
            return (row, part)

        return pl.BlockSpec((tile, cols), at)

    def fixed(shape):
        return pl.BlockSpec(shape, lambda step: (0,) * len(shape))

    specs = [side_spec(left_cols, left_part[0], side) for side in (0, 1)]
    specs += [side_spec(cols, right_part[0], side) for side in (0, 1) for cols in right_cols]
    shapes = [jax.ShapeDtypeStruct((left_cols, cols), LOW) for cols in right_cols]
    if dealt:
        shapes = [jax.ShapeDtypeStruct((4, 4, piece, left_cols if flip else sum(right_cols)), LOW)]
    if sums:
        shapes += [jax.ShapeDtypeStruct((1, cols), WIDE) for cols in right_cols]
    rows = 2 * left[0].shape[0]
    return pl.pallas_call(
        body,
        grid=(2 * steps,),
        in_specs=specs,
        out_specs=[fixed(shape.shape) for shape in shapes],
        out_shape=shapes,
        scratch_shapes=[pltpu.VMEM((left_cols, cols), WIDE) for cols in right_cols],
        compiler_params=pltpu.CompilerParams(dimension_semantics=("arbitrary",), vmem_limit_bytes=ROOM),
        cost_estimate=hint(
            flops=2 * rows * left_cols * sum(right_cols), transcendentals=0,
            bytes_accessed=2 * rows * (left_cols + sum(right_cols)),
        ),
    )(*left, *[pair[0] for pair in rights], *[pair[1] for pair in rights])


def grad_side(left, right, earlier=None, tile=512):
    shape = (left.shape[1], right.shape[1])
    steps = left.shape[0] // tile

    def body(left_ref, right_ref, *rest):
        step = pl.program_id(0)
        acc = rest[-1]

        @pl.when(step == 0)
        def _():
            acc[...] = jnp.zeros_like(acc) if earlier is None else rest[0][...]

        for at in strips(shape[1]):
            acc[:, at] += lax.dot_general(left_ref[...], right_ref[:, at], ROWS_OF, preferred_element_type=WIDE)

        @pl.when(step == steps - 1)
        def _():
            rest[-2][...] = acc[...].astype(WIDE if earlier is None else LOW)

    def tiles(width):
        return pl.BlockSpec((tile, width), lambda i: (i, 0))

    held = pl.BlockSpec(shape, lambda i: (0, 0), pipeline_mode=pl.Buffered(1))
    more = [] if earlier is None else [earlier]
    return pl.pallas_call(
        body,
        grid=(steps,),
        in_specs=[tiles(shape[0]), tiles(shape[1])] + [held] * len(more),
        out_specs=pl.BlockSpec(shape, lambda i: (0, 0)),
        out_shape=jax.ShapeDtypeStruct(shape, WIDE if earlier is None else LOW),
        scratch_shapes=[pltpu.VMEM(shape, WIDE)],
        compiler_params=pltpu.CompilerParams(dimension_semantics=("arbitrary",), vmem_limit_bytes=ROOM),
        cost_estimate=hint(
            flops=2 * left.size * shape[1], transcendentals=0, bytes_accessed=2 * (left.size + right.size)
        ),
    )(left, right, *more)


def rope_tables(seq_len):
    lane = jnp.arange(2 * HEAD_DIM, dtype=jnp.int32) % HEAD_DIM
    half = ROT // 2
    turned = lane < ROT
    index = jnp.where(turned, lane % half, 0).astype(jnp.float32)
    freqs = BASE ** (-(index * 2.0) / ROT)
    angles = jnp.arange(seq_len, dtype=jnp.float32)[:, None] * freqs[None, :]
    sine = jnp.sin(angles)
    cosine = jnp.where(turned[None], jnp.cos(angles), 1.0)
    up = jnp.where((lane < half)[None], -sine, 0.0)
    down = jnp.where(((lane >= half) & turned)[None], sine, 0.0)
    return cosine, up, down


def attention_call(deal_own, deal_oth, lengths, joined_own, joined_oth, datt_own, datt_oth, tables, blk, base, seqs, earlier=()):
    _, half_rows, wide = joined_own.shape
    heads_wide = wide // 3
    pairs = heads_wide // 128
    seq_len = 2 * half_rows
    per_side = half_rows // blk
    step = 256
    scale = HEAD_DIM ** (-0.5)
    half = ROT // 2
    contract_last = (((1,), (1,)), ((), ()))
    contract_first = (((0,), (0,)), ((), ()))

    def kernel(own_at, oth_at, len_at, cos_ref, up_ref, down_ref, q0, k0, v0, d0, q1, k1, v1, d1, *rest):
        att0, dq0, dk0, dv0, att1, dq1, dk1, dv1, qs, ks, vs, ds, att_s, dq_s, dk_s, dv_s = rest[len(earlier) :]
        seq = base + pl.program_id(0)
        length = len_at[seq]

        def turn(x, at):
            return (x * cos_ref[at, :] + pltpu.roll(x, 128 - half, 1) * up_ref[at, :]
                    + pltpu.roll(x, half, 1) * down_ref[at, :])

        def unturn(x, at):
            return (x * cos_ref[at, :] - pltpu.roll(x, 128 - half, 1) * up_ref[at, :]
                    - pltpu.roll(x, half, 1) * down_ref[at, :])

        sides = ((own_at, q0, k0, v0, d0, att0, dq0, dk0, dv0), (oth_at, q1, k1, v1, d1, att1, dq1, dk1, dv1))
        for where_at, q_ref, k_ref, v_ref, d_ref, *_ in sides:
            for j in range(per_side):
                at = pl.ds(pl.multiple_of(where_at[seq, j] * blk, blk), blk)
                here = slice(j * blk, (j + 1) * blk)
                qs[at, :] = (turn(q_ref[0, here, :].astype(jnp.float32), at)).astype(jnp.bfloat16) * jnp.bfloat16(scale)
                ks[at, :] = turn(k_ref[0, here, :].astype(jnp.float32), at).astype(jnp.bfloat16)
                vs[at, :] = v_ref[0, here, :]
                ds[at, :] = d_ref[0, here, :]
        att_s[...] = jnp.zeros_like(att_s)
        dq_s[...] = jnp.zeros_like(dq_s)
        dk_s[...] = jnp.zeros_like(dk_s)
        dv_s[...] = jnp.zeros_like(dv_s)
        lane = lax.broadcasted_iota(jnp.int32, (1, 128), 1)

        def one_head(h, carry):
            chosen = (lane // HEAD_DIM) == h
            keep_f = jnp.where(chosen, 1.0, 0.0)
            keep = keep_f.astype(jnp.bfloat16)
            for i in range(seq_len // step):
                rows = slice(i * step, (i + 1) * step)
                n = (i + 1) * step
                q = qs[rows, :] * keep
                d = ds[rows, :] * keep
                k = ks[:n, :]
                v = vs[:n, :]
                s = lax.dot_general(q, k, contract_last, preferred_element_type=jnp.float32)
                q_pos = i * step + lax.broadcasted_iota(jnp.int32, (step, 1), 0)
                limit = jnp.minimum(q_pos, length - 1)
                k_pos = lax.broadcasted_iota(jnp.int32, (step, n), 1)
                s = jnp.where(k_pos <= limit, s, -1e30)
                e = jnp.exp(s - jnp.max(s, axis=-1, keepdims=True))
                p = e * (1.0 / jnp.sum(e, axis=-1, keepdims=True))
                p_low = p.astype(jnp.bfloat16)
                dp = lax.dot_general(d, v, contract_last, preferred_element_type=jnp.float32)
                delta = jnp.sum(p * dp, axis=-1, keepdims=True)
                dsc = (p * (dp - delta)).astype(jnp.bfloat16)
                att_s[rows, :] += keep_f * jnp.dot(p_low, v, preferred_element_type=jnp.float32)
                dq_s[rows, :] += keep_f * jnp.dot(dsc, k, preferred_element_type=jnp.float32)
                dk_s[:n, :] += lax.dot_general(dsc, q, contract_first, preferred_element_type=jnp.float32)
                dv_s[:n, :] += lax.dot_general(p_low, d, contract_first, preferred_element_type=jnp.float32)
            return carry

        lax.fori_loop(0, 128 // HEAD_DIM, one_head, 0)
        for where_at, _, _, _, _, att_ref, dq_ref, dk_ref, dv_ref in sides:
            for j in range(per_side):
                at = pl.ds(pl.multiple_of(where_at[seq, j] * blk, blk), blk)
                here = slice(j * blk, (j + 1) * blk)
                att_ref[0, here, :] = att_s[at, :].astype(jnp.bfloat16)
                dq_ref[0, here, :] = unturn(dq_s[at, :] * scale, at).astype(jnp.bfloat16)
                dk_ref[0, here, :] = unturn(dk_s[at, :], at).astype(jnp.bfloat16)
                dv_ref[0, here, :] = dv_s[at, :].astype(jnp.bfloat16)

    def lanes(offset):
        return pl.BlockSpec((1, half_rows, 128), lambda s, p, *_: (base + s, 0, offset + p))

    table = pl.BlockSpec((seq_len, 128), lambda s, p, *_: (0, 0))
    side_in = [lanes(0), lanes(pairs), lanes(2 * pairs), lanes(0)]
    side_out = [lanes(0)] * 4
    narrow = jax.ShapeDtypeStruct((4, half_rows, heads_wide), jnp.bfloat16)
    work = seqs * pairs * 2 * seq_len * seq_len * 64
    result = pl.pallas_call(
        kernel,
        grid_spec=pltpu.PrefetchScalarGridSpec(
            num_scalar_prefetch=3,
            grid=(seqs, pairs),
            in_specs=[table] * 3 + side_in + side_in + [pl.BlockSpec(memory_space=pl.ANY)] * len(earlier),
            out_specs=side_out + side_out,
            scratch_shapes=[pltpu.VMEM((seq_len, 128), jnp.bfloat16)] * 4
            + [pltpu.VMEM((seq_len, 128), jnp.float32)] * 4,
        ),
        out_shape=[narrow] * 8,
        input_output_aliases={14 + i: i for i in range(len(earlier))},
        compiler_params=pltpu.CompilerParams(
            dimension_semantics=("arbitrary", "arbitrary"), vmem_limit_bytes=56 * 1024 * 1024
        ),
        cost_estimate=hint(
            flops=36 * work, transcendentals=work // 64, bytes_accessed=2 * 8 * seqs * seq_len * heads_wide
        ),
    )(deal_own, deal_oth, lengths, *tables, joined_own, joined_own, joined_own, datt_own,
      joined_oth, joined_oth, joined_oth, datt_oth, *earlier)
    return result


def flipped_out(core, shard, own, oth, start):
    lines, columns, rows, width = own.shape

    def kernel(where, own_ref, oth_ref, out_ref):
        side = pl.program_id(1)

        def write(ref):
            for line in range(lines):
                out_ref[:, line * rows : (line + 1) * rows] = ref[line, 0].astype(WIDE).T

        @pl.when(side == 0)
        def _():
            write(own_ref)

        @pl.when(side == 1)
        def _():
            write(oth_ref)

    source = pl.BlockSpec((lines, 1, rows, width), lambda b, s, where: (0, b, 0, start))
    target = pl.BlockSpec((width, lines * rows), lambda b, s, where: (where[0] ^ s, b))
    return pl.pallas_call(
        kernel,
        grid_spec=pltpu.PrefetchScalarGridSpec(
            num_scalar_prefetch=1, grid=(columns, 2), in_specs=[source, source], out_specs=target
        ),
        out_shape=jax.ShapeDtypeStruct((2 * width, lines * columns * rows), WIDE),
        compiler_params=pltpu.CompilerParams(dimension_semantics=("arbitrary",) * 2),
        cost_estimate=pl.CostEstimate(flops=0, transcendentals=0, bytes_accessed=3 * own.size),
    )(jnp.stack([core, shard]).astype(jnp.int32), own, oth)


def plane_body(
    tokens, cotangent, lengths, deal, ln_gain, ln_bias, w_qkv, b_qkv, w_out, b_out, w_up, b_up, w_down, b_down
):
    core = lax.axis_index("dp")
    place = lax.axis_index("ctx")
    shard = lax.axis_index("fsdp")
    spot = 2 * shard + core
    _, micro, rows, width = tokens.shape
    blocks = deal.shape[2]
    blk = rows * 4 // blocks
    units = w_down.shape[0] // 2
    head_cols = w_out.shape[0] // 2

    h_received = for_other(tokens[0], core, blk)
    norm = lax.all_gather(jnp.stack([ln_gain, ln_bias]), "fsdp", axis=1, tiled=True).astype(WIDE)
    gain, shift = norm[0], norm[1]
    _, hidden_home, _ = normed_rows(line_up(tokens[0], h_received, core, blk))
    hidden_home = (hidden_home * gain + shift).astype(LOW)
    meta = jnp.concatenate([deal[0].reshape(-1), lengths[0] // 64, lengths[0] % 64]).astype(LOW)
    theirs = swap_dp(meta)
    meta = jnp.where(place // micro == core, meta, theirs)
    turn = place % micro
    meta = jnp.concatenate([
        lax.dynamic_slice_in_dim(meta, turn * blocks, blocks), lax.dynamic_slice_in_dim(meta, micro * blocks + turn, 1),
        lax.dynamic_slice_in_dim(meta, micro * (blocks + 1) + turn, 1),
    ])
    size = b_qkv.shape[0] + b_out.shape[0] + b_up.shape[0] + b_down.shape[0] + meta.shape[0]
    small = jnp.concatenate([b_qkv, b_out, b_up, b_down, meta, jnp.zeros((-size % 512,), LOW)])

    up_sent = columns_sent([after(piece, hidden_home) for piece in columns_cut(w_up, 1, core, shard)])
    waited = [piece for bits, _, piece in up_sent if bits]
    small = lax.all_gather(after(small, *waited), "fsdp", axis=0, tiled=False)
    bounds = [0]
    for piece in (b_qkv, b_out, b_up, b_down, meta):
        bounds.append(bounds[-1] + piece.shape[0])
    bias_qkv, bias_out, bias_up, bias_down, meta = (small[:, a:b] for a, b in zip(bounds[:-1], bounds[1:]))
    own_blocks = lax.dynamic_slice_in_dim(deal[0], 2 * place, 2, axis=1)
    local_pos = (own_blocks[:, :, None] * blk + jnp.arange(blk, dtype=jnp.int32)).reshape(micro, rows)
    valid = (local_pos < lengths[0][:, None])[:, :, None]
    gout_home = jnp.where(valid, cotangent[0], jnp.zeros((), LOW))

    g_received = for_other(after(gout_home, hidden_home), core, blk)
    h_dealt = deal_out(hidden_home)
    hidden_own = lax.all_gather(after(h_dealt, *[piece for _, _, piece in up_sent]), "fsdp", axis=0, tiled=True)
    hidden = (hidden_own, swap_dp(hidden_own))
    up_w = placed(up_sent, shard, w_up.shape[0])
    g_dealt = deal_out(line_up(gout_home, after(g_received, h_dealt), core, blk))
    gout_own = lax.all_gather(g_dealt, "fsdp", axis=0, tiled=True)

    bias_ends = (bias_out.astype(WIDE) + bias_down.astype(WIDE)).reshape(-1)
    meta = meta.astype(jnp.int32)
    plane_len = meta[:, blocks] * 64 + meta[:, blocks + 1]
    plane_deal = meta[:, :blocks].reshape(4, 4, 2)
    deal_own = pick(plane_deal, core, 2)
    deal_oth = pick(plane_deal, 1 - core, 2)
    up_b = lax.dynamic_slice_in_dim(bias_up.reshape(-1), spot * units, units).astype(WIDE)
    qkv_b = pick(bias_qkv.reshape(3, 8, head_cols), spot, 1).reshape(-1).astype(WIDE)

    acts, slopes, dups, datts = [], [], [], []
    for h in hidden:
        act, slope = up_call(h, up_w, up_b)
        acts.append(act)
        slopes.append(slope)
    gout_own = after(gout_own, *acts)
    gout = (gout_own, swap_dp(gout_own))
    qkv_sent = columns_sent([after(piece, gout_own) for piece in columns_cut(w_qkv, 3, core, shard)])
    qkv_w = placed(qkv_sent, shard, w_qkv.shape[0])
    tables = rope_tables(8 * blk)
    down_w = lax.dynamic_slice_in_dim(w_down, core * units, units, 0)
    out_w = lax.dynamic_slice_in_dim(w_out, core * head_cols, head_cols, 0)

    def scatter(grad):
        return lax.psum_scatter(grad, "ctx", scatter_dimension=0, tiled=True)

    def gather(piece):
        return lax.all_gather(piece, "ctx", axis=0, tiled=True)

    def exchange(piece):
        return lax.all_to_all(piece[0], "fsdp", 0, 0, tiled=True)

    g_down = grad_side(acts[1], gout[1], grad_side(acts[0], gout[0]))
    t_down = gather(scatter(g_down))
    for g, slope in zip((after(gout[0], g_down), gout[1]), slopes):
        dup, datt = down_back_call(g, slope, down_w, out_w)
        dups.append(dup)
        datts.append(datt)
    waited = [piece for bits, _, piece in qkv_sent if bits]
    g_up, s_up = grad_call((after(hidden[0], *dups, *waited), hidden[1]), [dups], sums=True, dealt=True)
    x_up = exchange(scatter(g_up))
    t_up = gather(x_up[None])
    joins = [join_call(after(h, g_up), qkv_w, qkv_b) for h in hidden]

    per_seq = (4, 4 * blk, -1)
    shaped = [piece.reshape(per_seq) for piece in (joins[0], joins[1], datts[0], datts[1])]
    sides = attention_call(deal_own, deal_oth, plane_len, *shaped, tables, blk, 0, 4)
    sides = [piece.reshape(16 * blk, -1) for piece in sides]
    atts = [sides[0], sides[4]]
    turned = [sides[1:4], sides[5:8]]

    g_out = grad_call(atts, [gout], dealt=True, flip=True)[0]
    g_qkv, s_q, s_k, s_v = grad_call(
        (after(hidden[0], g_out), hidden[1]), [(turned[0][i], turned[1][i]) for i in range(3)], sums=True, dealt=True
    )
    mine = scatter(jnp.concatenate([g_qkv, g_out], axis=3))[0]
    qkv_cols = g_qkv.shape[3]
    x_qkv = lax.all_to_all(mine[:, :, :qkv_cols], "fsdp", 0, 0, tiled=True)
    t_qkv = gather(x_qkv[None])
    t_out = gather(after(mine[:, :, qkv_cols:], x_qkv)[None])
    sums_tp = line_sum(jnp.concatenate([s_up, s_q, s_k, s_v], axis=1), place)
    tails = lax.all_gather(sums_tp, ("fsdp", "dp"), axis=0, tiled=True)
    b_oth = backward_call(dups[1], after(turned[1], g_qkv, x_up), up_w, qkv_w)
    f_oth = forward_call(after(acts[1], b_oth, t_down), atts[1], down_w, out_w)
    b_total = backward_call(after(dups[0], f_oth), turned[0], up_w, qkv_w, swap_dp(b_oth))
    f_total = forward_call(after(acts[0], b_total), atts[0], down_w, out_w, swap_dp(f_oth))
    d_hidden = collect(b_total, shard, f_total)
    mixed = collect(f_total, shard)
    d_hidden = to_home(after(d_hidden, x_qkv), core, place, blk)
    t_up = after(t_up, f_total, x_qkv)
    o_up = cols_out(core, shard, t_up, after(swap_dp(t_up), tails), 1, 1)
    o_down = rows_out(core, shard, t_down, after(swap_dp(t_down), o_up))
    d_hidden = d_hidden.astype(WIDE)
    mixed = to_home(mixed, core, place, blk)
    t_qkv = after(t_qkv, o_down)
    o_qkv = cols_out(core, shard, t_qkv, swap_dp(t_qkv), 3, 3)
    t_out = after(t_out, o_qkv)
    o_out = flipped_out(core, shard, t_out, swap_dp(t_out), 0)

    inputs, normed, inv_std = normed_rows(after(tokens[0], f_total))
    d_norm = d_hidden * gain
    d_inputs = inv_std * (
        d_norm
        - jnp.mean(d_norm, axis=-1, keepdims=True)
        - normed * jnp.mean(d_norm * normed, axis=-1, keepdims=True)
    )
    back = (gout_home.astype(WIDE) + d_inputs).astype(LOW)

    mixed = after(mixed, o_qkv)
    result = jnp.where(valid, inputs + mixed.astype(WIDE) + bias_ends, 0.0).astype(LOW)
    d_bup = lax.dynamic_slice(tails, (2 * shard, 0), (2, units)).reshape(-1)
    d_bqkv = tails[:, units:].reshape(8, 3, head_cols).transpose(1, 0, 2).reshape(-1)
    d_bqkv = lax.dynamic_slice_in_dim(d_bqkv, shard * b_qkv.shape[0], b_qkv.shape[0])
    sums = jnp.stack([
        jnp.sum(d_hidden * normed, axis=(0, 1)), jnp.sum(d_hidden, axis=(0, 1)), jnp.sum(gout_home.astype(WIDE), axis=(0, 1)),
    ])
    sums = every_sum(sums, place)
    sums = lax.dynamic_slice_in_dim(sums, shard * ln_gain.shape[0], ln_gain.shape[0], 1)

    return result[None], back[None], sums[0], sums[1], o_qkv, d_bqkv, o_out, sums[2], o_up, d_bup, o_down, sums[2]


def plane_fits(mesh, shapes):
    tokens, _, _, deal = shapes[:4]
    sizes = dict(mesh.shape)
    dp, ctx, fsdp = sizes["dp"], sizes["ctx"], sizes["fsdp"]
    micro, seq_len, width = tokens.shape[1:]
    blocks = deal.shape[2]
    heads = width // HEAD_DIM
    return (
        dp == 2
        and dp * micro == ctx == fsdp == 4
        and tokens.shape[0] == dp * fsdp
        and blocks == dp * ctx
        and heads % (2 * dp * fsdp) == 0
        and seq_len % 256 == 0
        and (seq_len // blocks) % 128 == 0
    )


def solution(mesh):
    in_specs = (
        P(("dp", "fsdp"), None, "ctx", None),
        P(("dp", "fsdp"), None, "ctx", None),
        P(("dp", "fsdp"), None),
        P(("dp", "fsdp"), None, None),
        P("fsdp"),
        P("fsdp"),
        P("fsdp", None),
        P("fsdp"),
        P("fsdp", None),
        P("fsdp"),
        P("fsdp", None),
        P("fsdp"),
        P("fsdp", None),
        P("fsdp"),
    )
    out_specs = (
        P(("dp", "fsdp"), None, "ctx", None),
        P(("dp", "fsdp"), None, "ctx", None),
        P("fsdp"),
        P("fsdp"),
        P("fsdp", None),
        P("fsdp"),
        P("fsdp", None),
        P("fsdp"),
        P("fsdp", None),
        P("fsdp"),
        P("fsdp", None),
        P("fsdp"),
    )

    def program(*arrays):
        body = plane_body if plane_fits(mesh, arrays) else gathered_body
        return jax.shard_map(body, mesh=mesh, in_specs=in_specs, out_specs=out_specs, check_vma=False)(*arrays)

    return program
```

```python
import jax
import jax.numpy as jnp
from jax import lax
from jax.experimental import pallas as pl
from jax.experimental.pallas import tpu as pltpu
from jax.sharding import PartitionSpec as P

HEAD_DIM = 64
ROT = 32


EPS = 1e-05
BASE = 10000.0


def contract_rows(left, right):
    return lax.dot_general(
        left, right, (((0,), (0,)), ((), ())), preferred_element_type=jnp.float32
    )


def contract_cols(left, right):
    return lax.dot_general(
        left, right, (((1,), (1,)), ((), ())), preferred_element_type=jnp.float32
    )


def angles_of(positions):
    half = ROT // 2
    freqs = BASE ** (-(jnp.arange(half, dtype=jnp.float32) * 2.0) / ROT)
    angles = positions.astype(jnp.float32)[:, None] * freqs[None, :]
    return (jnp.cos(angles)[:, None, :], jnp.sin(angles)[:, None, :])


def rotate(values, cosine, sine):
    half = ROT // 2
    first = values[..., :half]
    second = values[..., half:ROT]
    return jnp.concatenate(
        [first * cosine - second * sine, second * cosine + first * sine, values[..., ROT:]], axis=-1
    )


def rotate_back(values, cosine, sine):
    half = ROT // 2
    first = values[..., :half]
    second = values[..., half:ROT]
    return jnp.concatenate(
        [first * cosine + second * sine, second * cosine - first * sine, values[..., ROT:]], axis=-1
    )


def layer_step(weights, inputs, upstream, length, deal_row):
    gain, shift, w_qkv, b_qkv, w_out, b_out, w_up, b_up, w_down, b_down = weights
    row_count, width = inputs.shape
    block_rows = row_count // 2
    head_count = width // HEAD_DIM
    scale = HEAD_DIM ** (-0.5)
    place = lax.axis_index("ctx")
    offsets = jnp.arange(block_rows, dtype=jnp.int32)
    own_blocks = lax.dynamic_slice_in_dim(deal_row, 2 * place, 2)
    local_pos = (own_blocks[:, None] * block_rows + offsets[None, :]).reshape(row_count)
    every_pos = (deal_row[:, None] * block_rows + offsets[None, :]).reshape(-1)
    valid = (local_pos < length).astype(jnp.float32)[:, None]
    allowed = (every_pos[None, :] <= local_pos[:, None]) & (every_pos[None, :] < length)
    cosine, sine = angles_of(local_pos)
    inputs_f = inputs.astype(jnp.float32)
    gain_f = gain.astype(jnp.float32)
    centered = inputs_f - jnp.mean(inputs_f, axis=-1, keepdims=True)
    variance = jnp.mean(centered * centered, axis=-1, keepdims=True)
    inv_std = lax.rsqrt(variance + EPS)
    normed = centered * inv_std
    hidden = (normed * gain_f + shift.astype(jnp.float32)).astype(jnp.bfloat16)
    joined = jnp.dot(hidden, w_qkv, preferred_element_type=jnp.float32) + b_qkv.astype(jnp.float32)
    query = (
        rotate(joined[:, :width].reshape(row_count, head_count, HEAD_DIM), cosine, sine)
        .reshape(row_count, width)
        .astype(jnp.bfloat16)
    )
    keyed = (
        rotate(joined[:, width : 2 * width].reshape(row_count, head_count, HEAD_DIM), cosine, sine)
        .reshape(row_count, width)
        .astype(jnp.bfloat16)
    )
    valued = joined[:, 2 * width :].astype(jnp.bfloat16)
    keys_all, values_all = (
        lax.all_gather(keyed, "ctx", axis=0, tiled=True),
        lax.all_gather(valued, "ctx", axis=0, tiled=True),
    )
    total_keys = keys_all.shape[0]
    group = min(8, head_count)
    span = group * HEAD_DIM

    def heads_of(array, start, count):
        return array[:, start : start + span].reshape(count, group, HEAD_DIM)

    def block_scores(start):
        raw = (
            jnp.einsum(
                "qhd,khd->hqk",
                heads_of(query, start, row_count),
                heads_of(keys_all, start, total_keys),
                preferred_element_type=jnp.float32,
            )
            * scale
        )
        return jnp.where(allowed[None], raw, -1e30)

    attended_parts = []
    lse_parts = []
    for start in range(0, width, span):
        masked = block_scores(start)
        highest = jnp.max(masked, axis=-1, keepdims=True)
        expo = jnp.exp(masked - highest)
        total = jnp.sum(expo, axis=-1, keepdims=True)
        weights_low = (expo / total).astype(jnp.bfloat16)
        mixed = jnp.einsum(
            "hqk,khd->qhd",
            weights_low,
            heads_of(values_all, start, total_keys),
            preferred_element_type=jnp.float32,
        )
        attended_parts.append(mixed.reshape(row_count, span))
        lse_parts.append(highest + jnp.log(total))
    attended = jnp.concatenate(attended_parts, axis=1).astype(jnp.bfloat16)
    branch = jnp.dot(attended, w_out, preferred_element_type=jnp.float32) + b_out.astype(
        jnp.float32
    )
    upward = jnp.dot(hidden, w_up, preferred_element_type=jnp.float32) + b_up.astype(jnp.float32)
    activated = jax.nn.gelu(upward, approximate=True).astype(jnp.bfloat16)
    feed = jnp.dot(activated, w_down, preferred_element_type=jnp.float32) + b_down.astype(
        jnp.float32
    )
    result = (valid * (inputs_f + branch + feed)).astype(jnp.bfloat16)
    grad_out = upstream.astype(jnp.float32) * valid
    grad_low = grad_out.astype(jnp.bfloat16)
    row_total = jnp.sum(grad_out, axis=0)
    d_down = contract_rows(activated, grad_low)
    d_wout = contract_rows(attended, grad_low)
    d_act = contract_cols(grad_low, w_down)
    _, gelu_pull = jax.vjp(lambda value: jax.nn.gelu(value, approximate=True), upward)
    d_upward = gelu_pull(d_act)[0].astype(jnp.bfloat16)
    d_wup = contract_rows(hidden, d_upward)
    d_bup = jnp.sum(d_upward.astype(jnp.float32), axis=0)
    d_attended = contract_cols(grad_low, w_out).astype(jnp.bfloat16)
    dq_parts = []
    dk_parts = []
    dv_parts = []
    delta_parts = []
    for index, start in enumerate(range(0, width, span)):
        masked = block_scores(start)
        probs = jnp.where(allowed[None], jnp.exp(masked - lse_parts[index]), 0.0)
        d_heads = heads_of(d_attended, start, row_count)
        d_probs = jnp.einsum(
            "qhd,khd->hqk",
            d_heads,
            heads_of(values_all, start, total_keys),
            preferred_element_type=jnp.float32,
        )
        delta = jnp.sum(probs * d_probs, axis=-1, keepdims=True)
        d_scores = (probs * (d_probs - delta)).astype(jnp.bfloat16)
        d_query = (
            jnp.einsum(
                "hqk,khd->qhd",
                d_scores,
                heads_of(keys_all, start, total_keys),
                preferred_element_type=jnp.float32,
            )
            * scale
        )
        dq_parts.append(d_query.reshape(row_count, span))
        delta_parts.append(delta[:, :, 0].T)
        d_keyed = (
            jnp.einsum(
                "hqk,qhd->khd",
                d_scores,
                heads_of(query, start, row_count),
                preferred_element_type=jnp.float32,
            )
            * scale
        )
        d_valued = jnp.einsum(
            "hqk,qhd->khd", probs.astype(jnp.bfloat16), d_heads, preferred_element_type=jnp.float32
        )
        dk_parts.append(d_keyed.reshape(total_keys, span))
        dv_parts.append(d_valued.reshape(total_keys, span))
    keys_grad_all = jnp.concatenate(dk_parts, axis=1)
    values_grad_all = jnp.concatenate(dv_parts, axis=1)
    keys_grad, values_grad = (
        lax.psum_scatter(
            keys_grad_all.astype(jnp.bfloat16), "ctx", scatter_dimension=0, tiled=True
        ).astype(jnp.float32),
        lax.psum_scatter(
            values_grad_all.astype(jnp.bfloat16), "ctx", scatter_dimension=0, tiled=True
        ).astype(jnp.float32),
    )
    query_grad = rotate_back(
        jnp.concatenate(dq_parts, axis=1).reshape(row_count, head_count, HEAD_DIM), cosine, sine
    ).reshape(row_count, width)
    keyed_grad = rotate_back(
        keys_grad.reshape(row_count, head_count, HEAD_DIM), cosine, sine
    ).reshape(row_count, width)
    d_joined = jnp.concatenate([query_grad, keyed_grad, values_grad], axis=1).astype(jnp.bfloat16)
    d_wqkv = contract_rows(hidden, d_joined)
    d_bqkv = jnp.sum(d_joined.astype(jnp.float32), axis=0)
    d_hidden = contract_cols(d_joined, w_qkv) + contract_cols(d_upward, w_up)
    d_gain = jnp.sum(d_hidden * normed, axis=0)
    d_shift = jnp.sum(d_hidden, axis=0)
    d_norm = d_hidden * gain_f
    d_inputs = inv_std * (
        d_norm
        - jnp.mean(d_norm, axis=-1, keepdims=True)
        - normed * jnp.mean(d_norm * normed, axis=-1, keepdims=True)
    )
    back = (grad_out + d_inputs).astype(jnp.bfloat16)
    return (
        result,
        back,
        (d_gain, d_shift, d_wqkv, d_bqkv, d_wout, row_total, d_wup, d_bup, d_down, row_total),
    )


def gathered_body(
    tokens,
    cotangent,
    lengths,
    deal,
    ln_gain,
    ln_bias,
    w_qkv,
    b_qkv,
    w_out,
    b_out,
    w_up,
    b_up,
    w_down,
    b_down,
):
    shards = (ln_gain, ln_bias, w_qkv, b_qkv, w_out, b_out, w_up, b_up, w_down, b_down)
    shard_count = lax.axis_size("fsdp")
    summed = tuple(
        (
            jnp.zeros((piece.shape[0] * shard_count,) + piece.shape[1:], jnp.float32)
            for piece in shards
        )
    )
    results = []
    backs = []
    for micro_index in range(tokens.shape[1]):
        gathered = (
            lax.all_gather(ln_gain, "fsdp", axis=0, tiled=True),
            lax.all_gather(ln_bias, "fsdp", axis=0, tiled=True),
            lax.all_gather(w_qkv, "fsdp", axis=0, tiled=True),
            lax.all_gather(b_qkv, "fsdp", axis=0, tiled=True),
            lax.all_gather(w_out, "fsdp", axis=0, tiled=True),
            lax.all_gather(b_out, "fsdp", axis=0, tiled=True),
            lax.all_gather(w_up, "fsdp", axis=0, tiled=True),
            lax.all_gather(b_up, "fsdp", axis=0, tiled=True),
            lax.all_gather(w_down, "fsdp", axis=0, tiled=True),
            lax.all_gather(b_down, "fsdp", axis=0, tiled=True),
        )
        result, back, local = layer_step(
            gathered,
            tokens[0, micro_index],
            cotangent[0, micro_index],
            lengths[0, micro_index],
            deal[0, micro_index],
        )
        results.append(result)
        backs.append(back)
        summed = tuple((older + newer for older, newer in zip(summed, local)))
    summed = (
        lax.psum_scatter(
            summed[0].astype(jnp.bfloat16), "fsdp", scatter_dimension=0, tiled=True
        ).astype(jnp.float32),
        lax.psum_scatter(
            summed[1].astype(jnp.bfloat16), "fsdp", scatter_dimension=0, tiled=True
        ).astype(jnp.float32),
        lax.psum_scatter(
            summed[2].astype(jnp.bfloat16), "fsdp", scatter_dimension=0, tiled=True
        ).astype(jnp.float32),
        lax.psum_scatter(
            summed[3].astype(jnp.bfloat16), "fsdp", scatter_dimension=0, tiled=True
        ).astype(jnp.float32),
        lax.psum_scatter(
            summed[4].astype(jnp.bfloat16), "fsdp", scatter_dimension=0, tiled=True
        ).astype(jnp.float32),
        lax.psum_scatter(
            summed[5].astype(jnp.bfloat16), "fsdp", scatter_dimension=0, tiled=True
        ).astype(jnp.float32),
        lax.psum_scatter(
            summed[6].astype(jnp.bfloat16), "fsdp", scatter_dimension=0, tiled=True
        ).astype(jnp.float32),
        lax.psum_scatter(
            summed[7].astype(jnp.bfloat16), "fsdp", scatter_dimension=0, tiled=True
        ).astype(jnp.float32),
        lax.psum_scatter(
            summed[8].astype(jnp.bfloat16), "fsdp", scatter_dimension=0, tiled=True
        ).astype(jnp.float32),
        lax.psum_scatter(
            summed[9].astype(jnp.bfloat16), "fsdp", scatter_dimension=0, tiled=True
        ).astype(jnp.float32),
    )
    totals = (
        lax.psum(summed[0].astype(jnp.bfloat16), ("dp", "ctx")).astype(jnp.float32),
        lax.psum(summed[1].astype(jnp.bfloat16), ("dp", "ctx")).astype(jnp.float32),
        lax.psum(summed[2].astype(jnp.bfloat16), ("dp", "ctx")).astype(jnp.float32),
        lax.psum(summed[3].astype(jnp.bfloat16), ("dp", "ctx")).astype(jnp.float32),
        lax.psum(summed[4].astype(jnp.bfloat16), ("dp", "ctx")).astype(jnp.float32),
        lax.psum(summed[5].astype(jnp.bfloat16), ("dp", "ctx")).astype(jnp.float32),
        lax.psum(summed[6].astype(jnp.bfloat16), ("dp", "ctx")).astype(jnp.float32),
        lax.psum(summed[7].astype(jnp.bfloat16), ("dp", "ctx")).astype(jnp.float32),
        lax.psum(summed[8].astype(jnp.bfloat16), ("dp", "ctx")).astype(jnp.float32),
        lax.psum(summed[9].astype(jnp.bfloat16), ("dp", "ctx")).astype(jnp.float32),
    )
    stacked_out = jnp.stack(results)[None]
    stacked_back = jnp.stack(backs)[None]
    return (
        stacked_out,
        stacked_back,
        totals[0],
        totals[1],
        totals[2],
        totals[3],
        totals[4],
        totals[5],
        totals[6],
        totals[7],
        totals[8],
        totals[9],
    )


SWAP = [(0, 1), (1, 0)]
LOW = jnp.bfloat16
SLOW = 1.8
WIDE = jnp.float32


def hint(flops, transcendentals, bytes_accessed):
    return pl.CostEstimate(
        flops=int(flops * SLOW), transcendentals=transcendentals, bytes_accessed=bytes_accessed
    )


def after(value, *others):
    return lax.optimization_barrier((value,) + others)[0]


def swap_dp(value):
    return lax.ppermute(value, "dp", SWAP)


def swap_shard(value, bits):
    return lax.ppermute(value, "fsdp", [(i, i ^ bits) for i in range(4)])


def shift_ctx(value, steps):
    return lax.ppermute(value, "ctx", [(i, (i + steps) % 4) for i in range(4)])


def pick(array, index, axis):
    return lax.dynamic_index_in_dim(array, index, axis, keepdims=False)


def by_core(core, mine, other, axis):
    first = jnp.where(core == 0, mine, other)
    second = jnp.where(core == 0, other, mine)
    return jnp.stack([first, second], axis=axis)


def for_other(rows, core, blk):
    micro, _, width = rows.shape
    return swap_dp(pick(rows.reshape(micro, 2, blk, width), 1 - core, 1))


def line_up(rows, received, core, blk):
    micro, _, width = rows.shape
    return by_core(core, pick(rows.reshape(micro, 2, blk, width), core, 1), received, 0).reshape(4, blk, width)


def deal_out(lined):
    return lax.all_to_all(lined, "ctx", 0, 0, tiled=True).reshape(-1, lined.shape[2])


def normed_rows(rows):
    inputs = rows.astype(WIDE)
    centered = inputs - jnp.mean(inputs, axis=-1, keepdims=True)
    inv_std = lax.rsqrt(jnp.mean(centered * centered, axis=-1, keepdims=True) + EPS)
    return inputs, centered * inv_std, inv_std


def placed(pieces, shard, size, *gates):
    whole = after(jnp.zeros((4 * size, pieces[0][2].shape[1]), LOW), *gates)
    for bits, start, piece in pieces:
        whole = lax.dynamic_update_slice(whole, piece, ((shard ^ bits) * size + start, 0))
    return whole


def plus(first, *others):
    total = first.astype(WIDE)
    for other in others:
        total = total + other.astype(WIDE)
    return total.astype(LOW)


def collect(total, shard, *gates):
    size = total.shape[0] // 4
    half = size // 2

    def part(bits, which):
        return lax.dynamic_slice_in_dim(total, (shard ^ bits) * size + which * half, half, 0)

    via_x, via_y = swap_shard(part(3, 0), 1), swap_shard(part(3, 1), 2)
    x_top, y_end = swap_shard(part(1, 0), 1), swap_shard(part(2, 1), 2)
    y_top = swap_shard(plus(part(2, 0), after(via_x, *gates)), 2)
    x_end = swap_shard(plus(part(1, 1), after(via_y, *gates)), 1)
    return jnp.concatenate([plus(part(0, 0), x_top, y_top), plus(part(0, 1), x_end, y_end)])


def to_home(mine, core, place, blk):
    width = mine.shape[1]
    lined = lax.all_to_all(mine.reshape(4, blk, width), "ctx", 0, 0, tiled=True).reshape(2, 2, blk, width)
    kept = pick(lined, core, 0)
    received = swap_dp(pick(lined, 1 - core, 0))
    return by_core(core, kept, received, 1).reshape(2, 2 * blk, width)


def columns_cut(weight, parts, core, shard):
    width = weight.shape[1] // (parts * 8)
    pieces = []
    for bits in range(4):
        spot = 2 * (shard ^ bits) + core
        pieces.append(jnp.concatenate(
            [lax.dynamic_slice_in_dim(weight, (t * 8 + spot) * width, width, 1) for t in range(parts)], axis=1
        ))
    return pieces


def columns_sent(pieces):
    return [(bits, 0, piece if bits == 0 else swap_shard(piece, bits)) for bits, piece in enumerate(pieces)]


def inward(value):
    return lax.ppermute(value, "ctx", [(0, 1), (3, 2)])


def across(value):
    return lax.ppermute(value, "ctx", [(1, 2), (2, 1)])


def outward(value):
    return lax.ppermute(value, "ctx", [(1, 0), (2, 3)])


def line_sum(value, place):
    half = value + inward(value)
    whole = half + across(half)
    return line_end(whole, outward(whole), place)


def line_end(whole, received, place):
    return jnp.where((place == 1) | (place == 2), whole, received)


def every_sum(value, place):
    value = value + swap_dp(value)
    value = value + swap_shard(value, 1)
    value = value + swap_shard(value, 2)
    return line_sum(value, place)


def lay_out(core, shard, own, oth, out_shape, grid, block, in_at, out_at):
    def kernel(where, own_ref, oth_ref, out_ref):
        side = pl.program_id(len(grid))

        @pl.when(side == 0)
        def _():
            out_ref[...] = own_ref[...].astype(WIDE)

        @pl.when(side == 1)
        def _():
            out_ref[...] = oth_ref[...].astype(WIDE)

    source = pl.BlockSpec(block, lambda *args: in_at(*args[: len(grid)]))
    target = pl.BlockSpec(block, lambda *args: out_at(*args[:-1], args[-1][0], args[-1][1]))
    count = out_shape[0] * out_shape[1]
    return pl.pallas_call(
        kernel,
        grid_spec=pltpu.PrefetchScalarGridSpec(
            num_scalar_prefetch=1, grid=grid + (2,), in_specs=[source, source], out_specs=target
        ),
        out_shape=jax.ShapeDtypeStruct(out_shape, WIDE),
        compiler_params=pltpu.CompilerParams(dimension_semantics=("arbitrary",) * (len(grid) + 1)),
        cost_estimate=hint(flops=0, transcendentals=0, bytes_accessed=6 * count),
    )(jnp.stack([core, shard]).astype(jnp.int32), own, oth)


def rows_out(core, shard, own, oth):
    rows, width = own.shape
    tile = min(256, rows)
    steps = rows // tile
    return lay_out(
        core, shard, own, oth, (2 * rows, width), (steps,), (tile, width),
        lambda i: (i, 0), lambda i, s, c, f: ((c ^ s) * steps + i, 0),
    )


def cols_half(core, shard, half, side, parts, held, earlier=()):
    lines, columns, rows, width = half.shape
    width = width // held

    def kernel(where, half_ref, *rest):
        rest[-1][...] = half_ref[...].reshape(lines * rows, width).astype(WIDE)

    return pl.pallas_call(
        kernel,
        grid_spec=pltpu.PrefetchScalarGridSpec(
            num_scalar_prefetch=1,
            grid=(columns, parts),
            in_specs=[pl.BlockSpec((lines, 1, rows, width), lambda b, t, where: (0, b, 0, t))]
            + [pl.BlockSpec(memory_space=pl.ANY)] * len(earlier),
            out_specs=pl.BlockSpec((lines * rows, width), lambda b, t, where: (0, t * 8 + 2 * b + (where[0] ^ side))),
        ),
        out_shape=jax.ShapeDtypeStruct((lines * rows, 2 * columns * parts * width), WIDE),
        input_output_aliases={2: 0} if earlier else {},
        compiler_params=pltpu.CompilerParams(dimension_semantics=("arbitrary",) * 2),
        cost_estimate=pl.CostEstimate(flops=0, transcendentals=0, bytes_accessed=6 * half.size),
    )(jnp.stack([core, shard]).astype(jnp.int32), half, *earlier)


def cols_out(core, shard, own, oth, parts, held):
    first = cols_half(core, shard, own, 0, parts, held)
    return cols_half(core, shard, oth, 1, parts, held, (first,))


GELU_C = 0.7978845608028654
GELU_A = 0.044715


def gelu_pair(value):
    square = value * value
    tanh = jnp.tanh(GELU_C * value * (1.0 + GELU_A * square))
    half = 0.5 * (1.0 + tanh)
    slope = half + 0.5 * value * (1.0 - tanh * tanh) * (GELU_C * (1.0 + 3.0 * GELU_A * square))
    return value * half, slope


ROWS_OF = (((0,), (0,)), ((), ()))
COLS_OF = (((1,), (1,)), ((), ()))
ROOM = 56 * 1024 * 1024


def row_call(body, tiled, whole, widths, flops, tile=512):
    count = tiled[0].shape[0]

    def rows_spec(width):
        return pl.BlockSpec((tile, width), lambda i: (i, 0))

    moved = sum(a.size * a.dtype.itemsize for a in (*tiled, *whole)) + 2 * count * sum(widths)
    return pl.pallas_call(
        body,
        grid=(count // tile,),
        in_specs=[rows_spec(a.shape[1]) for a in tiled]
        + [pl.BlockSpec(a.shape, lambda i: (0, 0), pipeline_mode=pl.Buffered(1)) for a in whole],
        out_specs=[rows_spec(width) for width in widths],
        out_shape=[jax.ShapeDtypeStruct((count, width), LOW) for width in widths],
        compiler_params=pltpu.CompilerParams(dimension_semantics=("arbitrary",), vmem_limit_bytes=ROOM),
        cost_estimate=hint(flops=flops, transcendentals=0, bytes_accessed=moved),
    )(*tiled, *whole)


def strips(width):
    step = min(256, width)
    return [slice(at, at + step) for at in range(0, width, step)]


def up_call(rows, weight, bias):
    def body(rows_ref, weight_ref, bias_ref, act_ref, slope_ref):
        for at in strips(weight.shape[1]):
            total = jnp.dot(rows_ref[...], weight_ref[:, at], preferred_element_type=WIDE) + bias_ref[:, at]
            act, slope = gelu_pair(total)
            act_ref[:, at] = act.astype(LOW)
            slope_ref[:, at] = slope.astype(LOW)

    width = weight.shape[1]
    return row_call(body, [rows], [weight, bias[None]], [width, width], 2 * rows.shape[0] * weight.size)


def join_call(rows, weight, bias):
    def body(rows_ref, weight_ref, bias_ref, out_ref):
        for at in strips(weight.shape[1]):
            total = jnp.dot(rows_ref[...], weight_ref[:, at], preferred_element_type=WIDE)
            out_ref[:, at] = (total + bias_ref[:, at]).astype(LOW)

    return row_call(body, [rows], [weight, bias[None]], [weight.shape[1]], 2 * rows.shape[0] * weight.size)[0]


def down_back_call(rows, slopes, down_w, out_w):
    def body(rows_ref, slope_ref, down_ref, out_w_ref, dup_ref, datt_ref):
        for at in strips(down_w.shape[0]):
            total = lax.dot_general(rows_ref[...], down_ref[at, :], COLS_OF, preferred_element_type=WIDE)
            dup_ref[:, at] = (total * slope_ref[:, at].astype(WIDE)).astype(LOW)
        total = lax.dot_general(rows_ref[...], out_w_ref[...], COLS_OF, preferred_element_type=WIDE)
        datt_ref[...] = total.astype(LOW)

    flops = 2 * rows.shape[0] * (down_w.size + out_w.size)
    return row_call(body, [rows, slopes], [down_w, out_w], [down_w.shape[0], out_w.shape[0]], flops)


def forward_call(act, att, down_w, out_w, added=None):
    def body(*refs):
        act_ref, att_ref = refs[:2]
        down_ref, out_w_ref, out_ref = refs[-3:]
        for at in strips(down_w.shape[1]):
            total = jnp.dot(act_ref[...], down_ref[:, at], preferred_element_type=WIDE)
            total = total + jnp.dot(att_ref[...], out_w_ref[:, at], preferred_element_type=WIDE)
            if added is not None:
                total = total + refs[2][:, at].astype(WIDE)
            out_ref[:, at] = total.astype(LOW)

    tiled = [act, att] + ([] if added is None else [added])
    flops = 2 * act.shape[0] * (down_w.size + out_w.size)
    return row_call(body, tiled, [down_w, out_w], [down_w.shape[1]], flops)[0]


def backward_call(dup, turned, up_w, qkv_w, added=None):
    wide = turned[0].shape[1]

    def body(*refs):
        dup_ref, turned_refs = refs[0], refs[1:4]
        up_ref, qkv_ref, out_ref = refs[-3:]
        for at in strips(up_w.shape[0]):
            total = lax.dot_general(dup_ref[...], up_ref[at, :], COLS_OF, preferred_element_type=WIDE)
            for i, ref in enumerate(turned_refs):
                part = qkv_ref[at, i * wide : (i + 1) * wide]
                total = total + lax.dot_general(ref[...], part, COLS_OF, preferred_element_type=WIDE)
            if added is not None:
                total = total + refs[4][:, at].astype(WIDE)
            out_ref[:, at] = total.astype(LOW)

    tiled = [dup, *turned] + ([] if added is None else [added])
    flops = 2 * dup.shape[0] * (up_w.size + qkv_w.size)
    return row_call(body, tiled, [up_w, qkv_w], [up_w.shape[0]], flops)[0]


def grad_call(left, rights, left_part=(0, 1), right_part=(0, 1), sums=False, dealt=False, flip=False, tile=512):
    steps = left[0].shape[0] // tile
    left_cols = left[0].shape[1] // left_part[1]
    right_cols = [pair[0].shape[1] // right_part[1] for pair in rights]
    count = len(rights)
    piece = (right_cols[0] if flip else left_cols) // 16
    made = 1 if dealt else count

    def body(*refs):
        ins, outs = refs[: 2 + 2 * count], refs[2 + 2 * count :]
        grads, totals, accs = outs[:made], outs[made : len(outs) - count], outs[len(outs) - count :]
        step = pl.program_id(0)

        @pl.when(step == 0)
        def _():
            for ref in (*accs, *totals):
                ref[...] = jnp.zeros_like(ref)

        def add(left_ref, right_refs):
            for i, ref in enumerate(right_refs):
                for at in strips(right_cols[i]):
                    accs[i][:, at] += lax.dot_general(
                        left_ref[...], ref[:, at], ROWS_OF, preferred_element_type=WIDE
                    )
                if sums:
                    totals[i][...] += jnp.sum(ref[...].astype(WIDE), axis=0, keepdims=True)

        @pl.when(step < steps)
        def _():
            add(ins[0], ins[2 : 2 + count])

        @pl.when(step >= steps)
        def _():
            add(ins[1], ins[2 + count :])

        @pl.when(step == 2 * steps - 1)
        def _():
            if not dealt:
                for grad, acc in zip(grads, accs):
                    grad[...] = acc[...].astype(LOW)
                return
            if flip:
                for spot in range(16):
                    part = accs[0][:, spot * piece : (spot + 1) * piece]
                    grads[0][spot % 4, spot // 4] = part.T.astype(LOW)
                return
            start = 0
            for acc, cols in zip(accs, right_cols):
                for column in range(4):
                    for line in range(4):
                        at = (4 * column + line) * piece
                        grads[0][line, column, :, start : start + cols] = acc[at : at + piece, :].astype(LOW)
                start += cols

    def side_spec(cols, part, side):
        def at(step):
            row = jnp.minimum(step, steps - 1) if side == 0 else jnp.maximum(step - steps, 0)
            return (row, part)

        return pl.BlockSpec((tile, cols), at)

    def fixed(shape):
        return pl.BlockSpec(shape, lambda step: (0,) * len(shape))

    specs = [side_spec(left_cols, left_part[0], side) for side in (0, 1)]
    specs += [side_spec(cols, right_part[0], side) for side in (0, 1) for cols in right_cols]
    shapes = [jax.ShapeDtypeStruct((left_cols, cols), LOW) for cols in right_cols]
    if dealt:
        shapes = [jax.ShapeDtypeStruct((4, 4, piece, left_cols if flip else sum(right_cols)), LOW)]
    if sums:
        shapes += [jax.ShapeDtypeStruct((1, cols), WIDE) for cols in right_cols]
    rows = 2 * left[0].shape[0]
    return pl.pallas_call(
        body,
        grid=(2 * steps,),
        in_specs=specs,
        out_specs=[fixed(shape.shape) for shape in shapes],
        out_shape=shapes,
        scratch_shapes=[pltpu.VMEM((left_cols, cols), WIDE) for cols in right_cols],
        compiler_params=pltpu.CompilerParams(dimension_semantics=("arbitrary",), vmem_limit_bytes=ROOM),
        cost_estimate=hint(
            flops=2 * rows * left_cols * sum(right_cols), transcendentals=0,
            bytes_accessed=2 * rows * (left_cols + sum(right_cols)),
        ),
    )(*left, *[pair[0] for pair in rights], *[pair[1] for pair in rights])


def grad_side(left, right, earlier=None, tile=512):
    shape = (left.shape[1], right.shape[1])
    steps = left.shape[0] // tile

    def body(left_ref, right_ref, *rest):
        step = pl.program_id(0)
        acc = rest[-1]

        @pl.when(step == 0)
        def _():
            acc[...] = jnp.zeros_like(acc) if earlier is None else rest[0][...]

        for at in strips(shape[1]):
            acc[:, at] += lax.dot_general(left_ref[...], right_ref[:, at], ROWS_OF, preferred_element_type=WIDE)

        @pl.when(step == steps - 1)
        def _():
            rest[-2][...] = acc[...].astype(WIDE if earlier is None else LOW)

    def tiles(width):
        return pl.BlockSpec((tile, width), lambda i: (i, 0))

    held = pl.BlockSpec(shape, lambda i: (0, 0), pipeline_mode=pl.Buffered(1))
    more = [] if earlier is None else [earlier]
    return pl.pallas_call(
        body,
        grid=(steps,),
        in_specs=[tiles(shape[0]), tiles(shape[1])] + [held] * len(more),
        out_specs=pl.BlockSpec(shape, lambda i: (0, 0)),
        out_shape=jax.ShapeDtypeStruct(shape, WIDE if earlier is None else LOW),
        scratch_shapes=[pltpu.VMEM(shape, WIDE)],
        compiler_params=pltpu.CompilerParams(dimension_semantics=("arbitrary",), vmem_limit_bytes=ROOM),
        cost_estimate=hint(
            flops=2 * left.size * shape[1], transcendentals=0, bytes_accessed=2 * (left.size + right.size)
        ),
    )(left, right, *more)


def rope_tables(seq_len):
    lane = jnp.arange(2 * HEAD_DIM, dtype=jnp.int32) % HEAD_DIM
    half = ROT // 2
    turned = lane < ROT
    index = jnp.where(turned, lane % half, 0).astype(jnp.float32)
    freqs = BASE ** (-(index * 2.0) / ROT)
    angles = jnp.arange(seq_len, dtype=jnp.float32)[:, None] * freqs[None, :]
    sine = jnp.sin(angles)
    cosine = jnp.where(turned[None], jnp.cos(angles), 1.0)
    up = jnp.where((lane < half)[None], -sine, 0.0)
    down = jnp.where(((lane >= half) & turned)[None], sine, 0.0)
    return cosine, up, down


def attention_call(deal_own, deal_oth, lengths, joined_own, joined_oth, datt_own, datt_oth, tables, blk, base, seqs, earlier=()):
    _, half_rows, wide = joined_own.shape
    heads_wide = wide // 3
    pairs = heads_wide // 128
    seq_len = 2 * half_rows
    per_side = half_rows // blk
    step = 256
    scale = HEAD_DIM ** (-0.5)
    half = ROT // 2
    contract_last = (((1,), (1,)), ((), ()))
    contract_first = (((0,), (0,)), ((), ()))

    def kernel(own_at, oth_at, len_at, cos_ref, up_ref, down_ref, q0, k0, v0, d0, q1, k1, v1, d1, *rest):
        att0, dq0, dk0, dv0, att1, dq1, dk1, dv1, qs, ks, vs, ds, att_s, dq_s, dk_s, dv_s = rest[len(earlier) :]
        seq = base + pl.program_id(0)
        length = len_at[seq]

        def turn(x, at):
            return (x * cos_ref[at, :] + pltpu.roll(x, 128 - half, 1) * up_ref[at, :]
                    + pltpu.roll(x, half, 1) * down_ref[at, :])

        def unturn(x, at):
            return (x * cos_ref[at, :] - pltpu.roll(x, 128 - half, 1) * up_ref[at, :]
                    - pltpu.roll(x, half, 1) * down_ref[at, :])

        sides = ((own_at, q0, k0, v0, d0, att0, dq0, dk0, dv0), (oth_at, q1, k1, v1, d1, att1, dq1, dk1, dv1))
        for where_at, q_ref, k_ref, v_ref, d_ref, *_ in sides:
            for j in range(per_side):
                at = pl.ds(pl.multiple_of(where_at[seq, j] * blk, blk), blk)
                here = slice(j * blk, (j + 1) * blk)
                qs[at, :] = (turn(q_ref[0, here, :].astype(jnp.float32), at)).astype(jnp.bfloat16) * jnp.bfloat16(scale)
                ks[at, :] = turn(k_ref[0, here, :].astype(jnp.float32), at).astype(jnp.bfloat16)
                vs[at, :] = v_ref[0, here, :]
                ds[at, :] = d_ref[0, here, :]
        att_s[...] = jnp.zeros_like(att_s)
        dq_s[...] = jnp.zeros_like(dq_s)
        dk_s[...] = jnp.zeros_like(dk_s)
        dv_s[...] = jnp.zeros_like(dv_s)
        lane = lax.broadcasted_iota(jnp.int32, (1, 128), 1)

        def one_head(h, carry):
            chosen = (lane // HEAD_DIM) == h
            keep_f = jnp.where(chosen, 1.0, 0.0)
            keep = keep_f.astype(jnp.bfloat16)
            for i in range(seq_len // step):
                rows = slice(i * step, (i + 1) * step)
                n = (i + 1) * step
                q = qs[rows, :] * keep
                d = ds[rows, :] * keep
                k = ks[:n, :]
                v = vs[:n, :]
                s = lax.dot_general(q, k, contract_last, preferred_element_type=jnp.float32)
                q_pos = i * step + lax.broadcasted_iota(jnp.int32, (step, 1), 0)
                limit = jnp.minimum(q_pos, length - 1)
                k_pos = lax.broadcasted_iota(jnp.int32, (step, n), 1)
                s = jnp.where(k_pos <= limit, s, -1e30)
                e = jnp.exp(s - jnp.max(s, axis=-1, keepdims=True))
                p = e * (1.0 / jnp.sum(e, axis=-1, keepdims=True))
                p_low = p.astype(jnp.bfloat16)
                dp = lax.dot_general(d, v, contract_last, preferred_element_type=jnp.float32)
                delta = jnp.sum(p * dp, axis=-1, keepdims=True)
                dsc = (p * (dp - delta)).astype(jnp.bfloat16)
                att_s[rows, :] += keep_f * jnp.dot(p_low, v, preferred_element_type=jnp.float32)
                dq_s[rows, :] += keep_f * jnp.dot(dsc, k, preferred_element_type=jnp.float32)
                dk_s[:n, :] += lax.dot_general(dsc, q, contract_first, preferred_element_type=jnp.float32)
                dv_s[:n, :] += lax.dot_general(p_low, d, contract_first, preferred_element_type=jnp.float32)
            return carry

        lax.fori_loop(0, 128 // HEAD_DIM, one_head, 0)
        for where_at, _, _, _, _, att_ref, dq_ref, dk_ref, dv_ref in sides:
            for j in range(per_side):
                at = pl.ds(pl.multiple_of(where_at[seq, j] * blk, blk), blk)
                here = slice(j * blk, (j + 1) * blk)
                att_ref[0, here, :] = att_s[at, :].astype(jnp.bfloat16)
                dq_ref[0, here, :] = unturn(dq_s[at, :] * scale, at).astype(jnp.bfloat16)
                dk_ref[0, here, :] = unturn(dk_s[at, :], at).astype(jnp.bfloat16)
                dv_ref[0, here, :] = dv_s[at, :].astype(jnp.bfloat16)

    def lanes(offset):
        return pl.BlockSpec((1, half_rows, 128), lambda s, p, *_: (base + s, 0, offset + p))

    table = pl.BlockSpec((seq_len, 128), lambda s, p, *_: (0, 0))
    side_in = [lanes(0), lanes(pairs), lanes(2 * pairs), lanes(0)]
    side_out = [lanes(0)] * 4
    narrow = jax.ShapeDtypeStruct((4, half_rows, heads_wide), jnp.bfloat16)
    work = seqs * pairs * 2 * seq_len * seq_len * 64
    result = pl.pallas_call(
        kernel,
        grid_spec=pltpu.PrefetchScalarGridSpec(
            num_scalar_prefetch=3,
            grid=(seqs, pairs),
            in_specs=[table] * 3 + side_in + side_in + [pl.BlockSpec(memory_space=pl.ANY)] * len(earlier),
            out_specs=side_out + side_out,
            scratch_shapes=[pltpu.VMEM((seq_len, 128), jnp.bfloat16)] * 4
            + [pltpu.VMEM((seq_len, 128), jnp.float32)] * 4,
        ),
        out_shape=[narrow] * 8,
        input_output_aliases={14 + i: i for i in range(len(earlier))},
        compiler_params=pltpu.CompilerParams(
            dimension_semantics=("arbitrary", "arbitrary"), vmem_limit_bytes=56 * 1024 * 1024
        ),
        cost_estimate=hint(
            flops=36 * work, transcendentals=work // 64, bytes_accessed=2 * 8 * seqs * seq_len * heads_wide
        ),
    )(deal_own, deal_oth, lengths, *tables, joined_own, joined_own, joined_own, datt_own,
      joined_oth, joined_oth, joined_oth, datt_oth, *earlier)
    return result


def flipped_out(core, shard, own, oth, start):
    lines, columns, rows, width = own.shape

    def kernel(where, own_ref, oth_ref, out_ref):
        side = pl.program_id(1)

        def write(ref):
            for line in range(lines):
                out_ref[:, line * rows : (line + 1) * rows] = ref[line, 0].astype(WIDE).T

        @pl.when(side == 0)
        def _():
            write(own_ref)

        @pl.when(side == 1)
        def _():
            write(oth_ref)

    source = pl.BlockSpec((lines, 1, rows, width), lambda b, s, where: (0, b, 0, start))
    target = pl.BlockSpec((width, lines * rows), lambda b, s, where: (where[0] ^ s, b))
    return pl.pallas_call(
        kernel,
        grid_spec=pltpu.PrefetchScalarGridSpec(
            num_scalar_prefetch=1, grid=(columns, 2), in_specs=[source, source], out_specs=target
        ),
        out_shape=jax.ShapeDtypeStruct((2 * width, lines * columns * rows), WIDE),
        compiler_params=pltpu.CompilerParams(dimension_semantics=("arbitrary",) * 2),
        cost_estimate=pl.CostEstimate(flops=0, transcendentals=0, bytes_accessed=3 * own.size),
    )(jnp.stack([core, shard]).astype(jnp.int32), own, oth)


def plane_body(
    tokens, cotangent, lengths, deal, ln_gain, ln_bias, w_qkv, b_qkv, w_out, b_out, w_up, b_up, w_down, b_down
):
    core = lax.axis_index("dp")
    place = lax.axis_index("ctx")
    shard = lax.axis_index("fsdp")
    spot = 2 * shard + core
    _, micro, rows, width = tokens.shape
    blocks = deal.shape[2]
    blk = rows * 4 // blocks
    units = w_down.shape[0] // 2
    head_cols = w_out.shape[0] // 2

    h_received = for_other(tokens[0], core, blk)
    norm = lax.all_gather(jnp.stack([ln_gain, ln_bias]), "fsdp", axis=1, tiled=True).astype(WIDE)
    gain, shift = norm[0], norm[1]
    _, hidden_home, _ = normed_rows(line_up(tokens[0], h_received, core, blk))
    hidden_home = (hidden_home * gain + shift).astype(LOW)
    meta = jnp.concatenate([deal[0].reshape(-1), lengths[0] // 64, lengths[0] % 64]).astype(LOW)
    theirs = swap_dp(meta)
    meta = jnp.where(place // micro == core, meta, theirs)
    turn = place % micro
    meta = jnp.concatenate([
        lax.dynamic_slice_in_dim(meta, turn * blocks, blocks), lax.dynamic_slice_in_dim(meta, micro * blocks + turn, 1),
        lax.dynamic_slice_in_dim(meta, micro * (blocks + 1) + turn, 1),
    ])
    size = b_qkv.shape[0] + b_out.shape[0] + b_up.shape[0] + b_down.shape[0] + meta.shape[0]
    small = jnp.concatenate([b_qkv, b_out, b_up, b_down, meta, jnp.zeros((-size % 512,), LOW)])

    up_sent = columns_sent([after(piece, hidden_home) for piece in columns_cut(w_up, 1, core, shard)])
    waited = [piece for bits, _, piece in up_sent if bits]
    small = lax.all_gather(after(small, *waited), "fsdp", axis=0, tiled=False)
    bounds = [0]
    for piece in (b_qkv, b_out, b_up, b_down, meta):
        bounds.append(bounds[-1] + piece.shape[0])
    bias_qkv, bias_out, bias_up, bias_down, meta = (small[:, a:b] for a, b in zip(bounds[:-1], bounds[1:]))
    own_blocks = lax.dynamic_slice_in_dim(deal[0], 2 * place, 2, axis=1)
    local_pos = (own_blocks[:, :, None] * blk + jnp.arange(blk, dtype=jnp.int32)).reshape(micro, rows)
    valid = (local_pos < lengths[0][:, None])[:, :, None]
    gout_home = jnp.where(valid, cotangent[0], jnp.zeros((), LOW))

    g_received = for_other(after(gout_home, hidden_home), core, blk)
    h_dealt = deal_out(hidden_home)
    hidden_own = lax.all_gather(after(h_dealt, *[piece for _, _, piece in up_sent]), "fsdp", axis=0, tiled=True)
    hidden = (hidden_own, swap_dp(hidden_own))
    up_w = placed(up_sent, shard, w_up.shape[0])
    g_dealt = deal_out(line_up(gout_home, after(g_received, h_dealt), core, blk))
    gout_own = lax.all_gather(g_dealt, "fsdp", axis=0, tiled=True)

    bias_ends = (bias_out.astype(WIDE) + bias_down.astype(WIDE)).reshape(-1)
    meta = meta.astype(jnp.int32)
    plane_len = meta[:, blocks] * 64 + meta[:, blocks + 1]
    plane_deal = meta[:, :blocks].reshape(4, 4, 2)
    deal_own = pick(plane_deal, core, 2)
    deal_oth = pick(plane_deal, 1 - core, 2)
    up_b = lax.dynamic_slice_in_dim(bias_up.reshape(-1), spot * units, units).astype(WIDE)
    qkv_b = pick(bias_qkv.reshape(3, 8, head_cols), spot, 1).reshape(-1).astype(WIDE)

    down_w = lax.dynamic_slice_in_dim(w_down, core * units, units, 0)
    out_w = lax.dynamic_slice_in_dim(w_out, core * head_cols, head_cols, 0)
    acts, slopes, dups, datts = [], [], [], []
    for h in hidden:
        act, slope = up_call(after(h, down_w, out_w), up_w, up_b)
        acts.append(act)
        slopes.append(slope)
    gout_own = after(gout_own, *acts)
    gout = (gout_own, swap_dp(gout_own))
    qkv_sent = columns_sent([after(piece, gout_own) for piece in columns_cut(w_qkv, 3, core, shard)])
    qkv_w = placed(qkv_sent, shard, w_qkv.shape[0])
    tables = rope_tables(8 * blk)

    def scatter(grad):
        return lax.psum_scatter(grad, "ctx", scatter_dimension=0, tiled=True)

    def gather(piece):
        return lax.all_gather(piece, "ctx", axis=0, tiled=True)

    def exchange(piece):
        return lax.all_to_all(piece[0], "fsdp", 0, 0, tiled=True)

    g_down = grad_side(acts[1], gout[1], grad_side(acts[0], gout[0]))
    t_down = gather(scatter(g_down))
    for g, slope in zip((after(gout[0], g_down), gout[1]), slopes):
        dup, datt = down_back_call(g, slope, down_w, out_w)
        dups.append(dup)
        datts.append(datt)
    waited = [piece for bits, _, piece in qkv_sent if bits]
    g_up, s_up = grad_call((after(hidden[0], *dups, *waited), hidden[1]), [dups], sums=True, dealt=True)
    x_up = exchange(scatter(g_up))
    t_up = gather(x_up[None])
    joins = [join_call(after(h, g_up), qkv_w, qkv_b) for h in hidden]

    per_seq = (4, 4 * blk, -1)
    shaped = [piece.reshape(per_seq) for piece in (joins[0], joins[1], datts[0], datts[1])]
    sides = attention_call(deal_own, deal_oth, plane_len, *shaped, tables, blk, 0, 4)
    sides = [piece.reshape(16 * blk, -1) for piece in sides]
    atts = [sides[0], sides[4]]
    turned = [sides[1:4], sides[5:8]]

    g_out = grad_call(atts, [gout], dealt=True, flip=True)[0]
    g_qkv, s_q, s_k, s_v = grad_call(
        (after(hidden[0], g_out), hidden[1]), [(turned[0][i], turned[1][i]) for i in range(3)], sums=True, dealt=True
    )
    mine = scatter(jnp.concatenate([g_qkv, g_out], axis=3))[0]
    qkv_cols = g_qkv.shape[3]
    x_qkv = lax.all_to_all(mine[:, :, :qkv_cols], "fsdp", 0, 0, tiled=True)
    t_qkv = gather(x_qkv[None])
    t_out = gather(after(mine[:, :, qkv_cols:], x_qkv)[None])
    sums_tp = line_sum(jnp.concatenate([s_up, s_q, s_k, s_v], axis=1), place)
    tails = lax.all_gather(sums_tp, ("fsdp", "dp"), axis=0, tiled=True)
    b_oth = backward_call(dups[1], after(turned[1], g_qkv, x_up), up_w, qkv_w)
    f_oth = forward_call(after(acts[1], b_oth, t_down), atts[1], down_w, out_w)
    b_total = backward_call(after(dups[0], f_oth), turned[0], up_w, qkv_w, swap_dp(b_oth))
    f_total = forward_call(after(acts[0], b_total), atts[0], down_w, out_w, swap_dp(f_oth))
    d_hidden = collect(b_total, shard, f_total)
    mixed = collect(f_total, shard)
    d_hidden = to_home(after(d_hidden, x_qkv), core, place, blk)
    t_up = after(t_up, f_total, x_qkv)
    o_up = cols_out(core, shard, t_up, after(swap_dp(t_up), tails), 1, 1)
    o_down = rows_out(core, shard, t_down, after(swap_dp(t_down), o_up))
    d_hidden = d_hidden.astype(WIDE)
    mixed = to_home(mixed, core, place, blk)
    t_qkv = after(t_qkv, o_down)
    o_qkv = cols_out(core, shard, t_qkv, swap_dp(t_qkv), 3, 3)
    t_out = after(t_out, o_qkv)
    o_out = flipped_out(core, shard, t_out, swap_dp(t_out), 0)

    inputs, normed, inv_std = normed_rows(after(tokens[0], f_total))
    d_norm = d_hidden * gain
    d_inputs = inv_std * (
        d_norm
        - jnp.mean(d_norm, axis=-1, keepdims=True)
        - normed * jnp.mean(d_norm * normed, axis=-1, keepdims=True)
    )
    back = (gout_home.astype(WIDE) + d_inputs).astype(LOW)

    mixed = after(mixed, o_qkv)
    result = jnp.where(valid, inputs + mixed.astype(WIDE) + bias_ends, 0.0).astype(LOW)
    d_bup = lax.dynamic_slice(tails, (2 * shard, 0), (2, units)).reshape(-1)
    d_bqkv = tails[:, units:].reshape(8, 3, head_cols).transpose(1, 0, 2).reshape(-1)
    d_bqkv = lax.dynamic_slice_in_dim(d_bqkv, shard * b_qkv.shape[0], b_qkv.shape[0])
    sums = jnp.stack([
        jnp.sum(d_hidden * normed, axis=(0, 1)), jnp.sum(d_hidden, axis=(0, 1)), jnp.sum(gout_home.astype(WIDE), axis=(0, 1)),
    ])
    sums = every_sum(sums, place)
    sums = lax.dynamic_slice_in_dim(sums, shard * ln_gain.shape[0], ln_gain.shape[0], 1)

    return result[None], back[None], sums[0], sums[1], o_qkv, d_bqkv, o_out, sums[2], o_up, d_bup, o_down, sums[2]


def plane_fits(mesh, shapes):
    tokens, _, _, deal = shapes[:4]
    sizes = dict(mesh.shape)
    dp, ctx, fsdp = sizes["dp"], sizes["ctx"], sizes["fsdp"]
    micro, seq_len, width = tokens.shape[1:]
    blocks = deal.shape[2]
    heads = width // HEAD_DIM
    return (
        dp == 2
        and dp * micro == ctx == fsdp == 4
        and tokens.shape[0] == dp * fsdp
        and blocks == dp * ctx
        and heads % (2 * dp * fsdp) == 0
        and seq_len % 256 == 0
        and (seq_len // blocks) % 128 == 0
    )


def solution(mesh):
    in_specs = (
        P(("dp", "fsdp"), None, "ctx", None),
        P(("dp", "fsdp"), None, "ctx", None),
        P(("dp", "fsdp"), None),
        P(("dp", "fsdp"), None, None),
        P("fsdp"),
        P("fsdp"),
        P("fsdp", None),
        P("fsdp"),
        P("fsdp", None),
        P("fsdp"),
        P("fsdp", None),
        P("fsdp"),
        P("fsdp", None),
        P("fsdp"),
    )
    out_specs = (
        P(("dp", "fsdp"), None, "ctx", None),
        P(("dp", "fsdp"), None, "ctx", None),
        P("fsdp"),
        P("fsdp"),
        P("fsdp", None),
        P("fsdp"),
        P("fsdp", None),
        P("fsdp"),
        P("fsdp", None),
        P("fsdp"),
        P("fsdp", None),
        P("fsdp"),
    )

    def program(*arrays):
        body = plane_body if plane_fits(mesh, arrays) else gathered_body
        return jax.shard_map(body, mesh=mesh, in_specs=in_specs, out_specs=out_specs, check_vma=False)(*arrays)

    return program
```
